32 devices in a mesh: dp: 16 (over z, y, x), tensor: 2 (over core).
Axes of the slice: x: 2, y: 2, z: 4, core: 2. Of those that a mesh axis runs over, the one named last changes fastest.
Arguments:
- layer_in: bfloat16 [32768, 768], P(('dp', 'tensor')), may hold values from -6 to 6
- upstream: bfloat16 [32768, 768], P(('dp', 'tensor')), may hold values from -6 to 6
- lengths: int32 [32], P('dp'), may hold values from 256 to 1024, as said below
- rescale: float32 [768], replicated, may hold values from 0.5 to 1.5
- gating: bfloat16 [768, 1536], P('dp', 'tensor'), may hold values from -0.21875 to 0.21875
- content: bfloat16 [768, 1536], P('dp', 'tensor'), may hold values from -0.21875 to 0.21875
- selector: bfloat16 [768, 128], P('dp'), may hold values from -0.21875 to 0.21875
- timestep: bfloat16 [768, 24], P('dp', 'tensor'), may hold values from -0.21875 to 0.21875
- filters: float32 [4, 1536], P(None, 'tensor'), may hold values from -3 to 3
- kernels: float32 [4, 128], replicated, may hold values from -3 to 3
- biases: float32 [24], P('tensor'), may hold values from -6 to -2
- decays: float32 [24], P('tensor'), may hold values from -1 to 2
- shortcut: float32 [24], P('tensor'), may hold values from 0.5 to 1.5
- amplitude: float32 [1536], P('tensor'), may hold values from 0.5 to 1.5
- outgoing: bfloat16 [1536, 768], P('tensor', 'dp'), may hold values from -0.15625 to 0.15625
Outputs:
- layer_out: bfloat16 [32768, 768], P(('dp', 'tensor'))
- input_grad: bfloat16 [32768, 768], P(('dp', 'tensor'))
- rescale_grad: float32 [768], replicated
- gating_grad: float32 [768, 1536], P('dp', 'tensor')
- content_grad: float32 [768, 1536], P('dp', 'tensor')
- selector_grad: float32 [768, 128], P('dp')
- timestep_grad: float32 [768, 24], P('dp', 'tensor')
- filters_grad: float32 [4, 1536], P(None, 'tensor')
- kernels_grad: float32 [4, 128], replicated
- biases_grad: float32 [24], P('tensor')
- decays_grad: float32 [24], P('tensor')
- shortcut_grad: float32 [24], P('tensor')
- amplitude_grad: float32 [1536], P('tensor')
- outgoing_grad: float32 [1536, 768], P('tensor', 'dp')
The draws below stay inside these ranges and needn't reach their ends.
Inputs may be any that keep to these rules, and one draw needn't show every extreme that they name: lengths[s] is the number of valid tokens of sequence s; in every draw some sequence fills all 1024 of its slots.
All inputs are finite; a program needn't handle non-finite values.
Results may differ from the reference program's by a relative error of at most 0.011.
Values may be sent and summed in bfloat16 or wider, within the bound.
No kernel may reach another device: no remote copies, remote signals or barrier semaphores. Data moves between devices by JAX's collectives and lax.ppermute only.
A program may use at most 256 MiB of HBM per device.

```python
import math
import jax
import jax.numpy as jnp
from jax import lax

MODEL_WIDTH = 768
INNER_WIDTH = 1536
HEAD_COUNT = 24
HEAD_SIZE = 64
STATE_SIZE = 64
FILTER_TAPS = 4
SLOT_ROWS = 1024
LEAST_LENGTH = 256
MICRO_BATCHES = 2
TOKENS = 32768
SEQUENCES = 32
HALF_ROWS = 512
N_DP = 16
N_TENSOR = 2


def draw_lengths(key, part):
    first_key, second_key = jax.random.split(key)
    lengths_drawn = jax.random.randint(first_key, (SEQUENCES,), LEAST_LENGTH, SLOT_ROWS + 1)
    chosen = jax.random.randint(second_key, (), 0, SEQUENCES)
    return jnp.where(jnp.arange(SEQUENCES) == chosen, SLOT_ROWS, lengths_drawn).astype(jnp.int32)


def block_levels(rng, dims, shards, least, largest):
    def one(dim, shards_of):
        draws = jax.random.uniform(jax.random.fold_in(jax.random.fold_in(rng, 6), dim), (shards_of,), jnp.float32, least / len(shards), largest / len(shards))
        return jnp.repeat(jnp.exp(draws), dims[dim] // shards_of).reshape((-1,) + (1,) * (len(dims) - dim - 1))

    gain = one(*shards[0])
    for cut in shards[1:]:
        gain = gain * one(*cut)
    return gain


def centred(own_key, shape, deviation, reach, cuts=(), dtype=jnp.bfloat16):
    values = jax.random.normal(own_key, shape, jnp.float32) * deviation
    if len(cuts) > 0:
        values = block_levels(own_key, shape, cuts, -0.22, 0.18) * values
    return jnp.clip(values, min=-reach, max=reach).astype(dtype)


def setup_inputs(seed: int = 0) -> dict:
    key_of = jax.random.split(jax.random.key(seed), 16)
    return {
        "layer_in": centred(key_of[0], (TOKENS, MODEL_WIDTH), 1.0, 6.0, ((0, 32),)),
        "upstream": centred(key_of[1], (TOKENS, MODEL_WIDTH), 1.0, 6.0, ((0, 32),)),
        "lengths": draw_lengths(jax.random.fold_in(key_of[15], 71), 0),
        "rescale": jnp.clip(1.0 + 0.1 * jax.random.normal(key_of[3], (MODEL_WIDTH,), jnp.float32), 0.5, 1.5),
        "gating": centred(key_of[4], (MODEL_WIDTH, INNER_WIDTH), MODEL_WIDTH ** -0.5, 0.21875, ((0, 16), (1, 2))),
        "content": centred(key_of[5], (MODEL_WIDTH, INNER_WIDTH), MODEL_WIDTH ** -0.5, 0.21875, ((0, 16), (1, 2))),
        "selector": centred(key_of[6], (MODEL_WIDTH, 2 * STATE_SIZE), MODEL_WIDTH ** -0.5, 0.21875, ((0, 16),)),
        "timestep": centred(key_of[7], (MODEL_WIDTH, HEAD_COUNT), MODEL_WIDTH ** -0.5, 0.21875, ((0, 16), (1, 2))),
        "filters": centred(key_of[8], (FILTER_TAPS, INNER_WIDTH), FILTER_TAPS ** -0.5, 3.0, ((1, 2),), jnp.float32),
        "kernels": centred(key_of[9], (FILTER_TAPS, 2 * STATE_SIZE), FILTER_TAPS ** -0.5, 3.0, (), jnp.float32),
        "biases": jnp.clip(-6.0 + 4.0 * jax.random.uniform(key_of[10], (HEAD_COUNT,), jnp.float32) ** block_levels(key_of[10], (HEAD_COUNT,), ((0, 2),), -0.2, 0.2), -6.0, -2.0),
        "decays": jnp.clip(-1.0 + 3.0 * jax.random.uniform(key_of[11], (HEAD_COUNT,), jnp.float32) ** block_levels(key_of[11], (HEAD_COUNT,), ((0, 2),), -0.2, 0.2), -1.0, 2.0),
        "shortcut": jnp.clip(0.5 + 1.0 * jax.random.uniform(key_of[12], (HEAD_COUNT,), jnp.float32) ** block_levels(key_of[12], (HEAD_COUNT,), ((0, 2),), -0.2, 0.2), 0.5, 1.5),
        "amplitude": jnp.clip(1.0 + 0.1 * jax.random.normal(key_of[13], (INNER_WIDTH,), jnp.float32), 0.5, 1.5),
        "outgoing": centred(key_of[14], (INNER_WIDTH, MODEL_WIDTH), INNER_WIDTH ** -0.5, 0.15625, ((0, 2), (1, 16))),
    }


epsilon = 1e-05
precise = lax.Precision.HIGHEST

@jax.custom_vjp
def low(v):
    return lax.optimization_barrier(v.astype(jnp.bfloat16)).astype(jnp.float32)

@jax.custom_vjp
def low_back(v):
    return v

def low_keep(v):
    return (low(v), None)

def low_pass(kept, grad):
    return (grad,)

def back_keep(v):
    return (v, None)

def back_low(kept, grad):
    return (low(grad),)
low.defvjp(low_keep, low_pass)
low_back.defvjp(back_keep, back_low)

def causal_conv(values, kernel):
    taps = kernel.shape[0]
    length = values.shape[0]
    padded = jnp.pad(values, ((taps - 1, 0), (0, 0)))
    summed = jnp.zeros_like(values)
    for offset in range(taps):
        summed = summed + padded[offset:offset + length] * kernel[offset]
    return summed

def mix_heads(values_low, select_low, step_sizes, decays, shortcut):
    b_rows = select_low[:, :STATE_SIZE]
    c_rows = select_low[:, STATE_SIZE:]
    gram_rows = jnp.dot(c_rows, b_rows.T, precision=precise)
    places = jnp.arange(SLOT_ROWS)
    below_mask = places[:, None] > places[None, :]
    above_mask = places[:, None] < places[None, :]
    head_values = values_low.reshape(SLOT_ROWS, HEAD_COUNT, HEAD_SIZE).transpose(1, 0, 2)
    rates = jnp.exp(decays)

    def one_head(pieces):
        values_head, steps_head, rate_head, skip_head = pieces
        log_decay = -rate_head * steps_head
        ahead_terms = jnp.where(below_mask, log_decay[:, None], 0.0)
        ahead_sums = jnp.cumsum(ahead_terms, axis=0)
        behind_terms = jnp.where(above_mask, log_decay[:, None], 0.0)
        behind_sums = jnp.cumsum(behind_terms[::-1], axis=0)[::-1]
        ahead_log = jnp.where(below_mask, ahead_sums, -1e+30)
        behind_log = jnp.where(above_mask, behind_sums, -1e+30)
        coupling = gram_rows * (jnp.exp(ahead_log) + jnp.exp(behind_log))
        return jnp.dot(coupling, steps_head[:, None] * values_head, precision=precise) + skip_head * values_head
    mixed_heads = lax.map(jax.checkpoint(one_head), (head_values, step_sizes.T, rates, shortcut))
    return mixed_heads.transpose(1, 0, 2).reshape(SLOT_ROWS, INNER_WIDTH)

def one_sequence(params, tok_rows, mask_row):
    rescale, gating, content, selector, timestep, filters, kernels, biases, decays, shortcut, amplitude, outgoing = params
    inverse = lax.rsqrt(lax.optimization_barrier(jnp.mean(tok_rows * tok_rows, axis=-1, keepdims=True)) + epsilon)
    normed = low(tok_rows * inverse * rescale)
    gate_in = low_back(jnp.dot(normed, gating, precision=precise))
    values_in = low_back(jnp.dot(normed, content, precision=precise))
    select_in = low_back(jnp.dot(normed, selector, precision=precise))
    step_in = low_back(jnp.dot(normed, timestep, precision=precise))
    values_low = low(jax.nn.silu(causal_conv(values_in, filters)) * mask_row[:, None])
    select_low = low(jax.nn.silu(causal_conv(select_in, kernels)))
    step_sizes = jax.nn.softplus(step_in + biases)
    mixed = mix_heads(values_low, select_low, step_sizes, decays, shortcut)
    gated_pre = mixed * jax.nn.silu(gate_in)
    out_scale = lax.rsqrt(lax.optimization_barrier(jnp.mean(gated_pre * gated_pre, axis=-1, keepdims=True)) + epsilon)
    gated = low(gated_pre * out_scale * amplitude)
    branch = low_back(jnp.dot(gated, outgoing, precision=precise))
    return mask_row[:, None] * (tok_rows + branch)

def run_block(params, seq_block, mask_block):
    return jax.vmap(one_sequence, in_axes=(None, 0, 0))(params, seq_block, mask_block)

def forward(params, sequences, masks):
    group_size = math.gcd(SEQUENCES, 4)
    seq_blocks = sequences.reshape(SEQUENCES // group_size, group_size, SLOT_ROWS, MODEL_WIDTH)
    mask_blocks = masks.reshape(SEQUENCES // group_size, group_size, SLOT_ROWS)

    def block_step(carried, pieces):
        outputs = jax.checkpoint(run_block)(params, pieces[0], pieces[1])
        return (carried, outputs)
    _, out_blocks = lax.scan(block_step, jnp.zeros((), jnp.float32), (seq_blocks, mask_blocks))
    return out_blocks.reshape(SEQUENCES, SLOT_ROWS, MODEL_WIDTH)

def to_sequences(array):
    shaped = array.reshape(N_DP, N_TENSOR, MICRO_BATCHES, HALF_ROWS, MODEL_WIDTH)
    return shaped.transpose(0, 2, 1, 3, 4).reshape(SEQUENCES, SLOT_ROWS, MODEL_WIDTH)

def to_rows(array):
    shaped = array.reshape(N_DP, MICRO_BATCHES, N_TENSOR, HALF_ROWS, MODEL_WIDTH)
    return shaped.transpose(0, 2, 1, 3, 4).reshape(TOKENS, MODEL_WIDTH)

def reference(layer_in, upstream, lengths, rescale, gating, content, selector, timestep, filters, kernels, biases, decays, shortcut, amplitude, outgoing):
    params = tuple((weight.astype(jnp.float32) for weight in (rescale, gating, content, selector, timestep, filters, kernels, biases, decays, shortcut, amplitude, outgoing)))
    masks = (jnp.arange(SLOT_ROWS)[None, :] < lengths[:, None]).astype(jnp.float32)
    sequences = to_sequences(layer_in.astype(jnp.float32))

    def apply_layer(tokens_in, weights_in):
        return forward(weights_in, tokens_in, masks)
    result, pullback = jax.vjp(apply_layer, sequences, params)
    grad_seq, grads = pullback(to_sequences(upstream.astype(jnp.float32)))
    return (to_rows(result).astype(jnp.bfloat16), to_rows(grad_seq).astype(jnp.bfloat16), grads[0], grads[1], grads[2], grads[3], grads[4], grads[5], grads[6], grads[7], grads[8], grads[9], grads[10], grads[11])
```

```python
import functools

import jax
import jax.numpy as jnp
from jax import lax
from jax.experimental import pallas as pl
from jax.experimental.pallas import tpu as pltpu
from jax.sharding import PartitionSpec as P

BLOCK = 128
HEAD = 64
STATE = 64
GROUP = 256
LOG2E = 1.4426950408889634
epsilon = 1e-05
f32 = jnp.float32
bf16 = jnp.bfloat16
ANY = pl.ANY


def dot(a, b):
    return lax.dot_general(a, b, (((1,), (0,)), ((), ())), preferred_element_type=f32)


def dot_nt(a, b):
    return lax.dot_general(a, b, (((1,), (1,)), ((), ())), preferred_element_type=f32)


def dot_full(a, b):
    return lax.dot_general(
        a, b, (((1,), (0,)), ((), ())), preferred_element_type=f32, precision=lax.Precision.HIGHEST
    )


def iota(shape, axis):
    return lax.broadcasted_iota(jnp.int32, shape, axis)


def chunk(c):
    return pl.ds(pl.multiple_of(c * BLOCK, BLOCK), BLOCK)


def halo(c):
    return pl.ds(pl.multiple_of(c * BLOCK, BLOCK), BLOCK + 8)


def sigmoid(v):
    return 1.0 / (1.0 + jnp.exp(-v))


def conv_taps(padded, taps_ref):
    total = padded[8 : 8 + BLOCK] * taps_ref[3:4]
    for back in range(1, 4):
        total = total + padded[8 - back : 8 - back + BLOCK] * taps_ref[3 - back : 4 - back]
    return total


def lane_low():
    return iota((BLOCK, 2 * HEAD), 1) < HEAD


def spread(block, column):
    return jnp.broadcast_to(block[:, column : column + 1], (BLOCK, BLOCK))


def pair_rows(piece, low):
    return jnp.concatenate(
        (jnp.where(low, piece, 0.0), jnp.where(low, 0.0, piece)), axis=0
    ).astype(bf16)


def prep_kernel(
    normed, selector, timestep, kernels, biases, rates,
    select_in, b_rows, c_rows, select_t, gram, gram_t,
    ends, starts, steps, ends_t, starts_t, steps_t, slope_t, padded,
):
    chunks = normed.shape[0] // BLOCK
    groups = ends_t.shape[0]
    per = GROUP // HEAD
    down = iota((BLOCK, BLOCK), 0)
    across = iota((BLOCK, BLOCK), 1)
    tri = (down >= across).astype(f32)
    off = (down != across).astype(f32)
    padded[0:8] = jnp.zeros((8, BLOCK), f32)

    def project(c, carry):
        rows = chunk(c)
        selected = dot(normed[rows], selector[...])
        select_in[rows] = selected
        padded[pl.ds(pl.multiple_of(c * BLOCK + 8, 8), BLOCK)] = selected
        return carry

    lax.fori_loop(0, chunks, project, 0)

    def body(c, carry):
        rows = chunk(c)
        tokens = normed[rows]
        pre = conv_taps(padded[halo(c)], kernels)
        act = pre * sigmoid(pre)
        act_t = act.T.astype(bf16)
        act = act.astype(bf16)
        b_rows[rows] = act[:, :STATE]
        c_rows[rows] = act[:, STATE:]
        select_t[c] = act_t
        gram[c] = dot(act[:, STATE:], act_t[:STATE]) * off
        gram_t[c] = dot(act[:, :STATE], act_t[STATE:]) * off
        logits = dot(tokens, timestep[...]) + biases[...]
        small = jnp.exp(-jnp.abs(logits))
        whole = 1.0 + small
        log_part = jnp.where(
            whole == 1.0, small, jnp.log(whole) * (small / jnp.where(whole == 1.0, 1.0, whole - 1.0))
        )
        step = jnp.maximum(logits, 0.0) + log_part
        decay = -rates[...] * step
        inclusive = dot_full(tri, decay)
        end = inclusive * LOG2E
        start = (inclusive - decay) * LOG2E
        ends[rows] = end
        starts[rows] = start
        steps[rows] = step
        turned = ((ends_t, end), (starts_t, start), (steps_t, step), (slope_t, sigmoid(logits)))
        for target, value in turned:
            value_t = value.T
            for g in range(groups):
                target[g, 0:per, rows] = value_t[g * per : (g + 1) * per]
        return carry

    lax.fori_loop(0, chunks, body, 0)


def roll_heads(source, target, base):
    shift = lax.rem(BLOCK - base, BLOCK)
    target[...] = pltpu.roll(source[...], shift, 1)


def mix_kernel(
    half, length, normed, content, filters, shortcut, c_rows, select_t, gram,
    ends, starts, steps, ends_t, starts_t,
    mixed, x_low, values, early, late,
    padded, ends_g, starts_g, steps_g, scaled, gain_e, gain_l, totals,
):
    heads_half = pl.num_programs(0) * (GROUP // HEAD)
    base = half * heads_half + pl.program_id(0) * (GROUP // HEAD)
    chunks = normed.shape[0] // BLOCK
    pairs = GROUP // (2 * HEAD)
    roll_heads(ends, ends_g, base)
    roll_heads(starts, starts_g, base)
    roll_heads(steps, steps_g, base)
    padded[0:8] = jnp.zeros((8, GROUP), f32)

    def project(c, carry):
        rows = chunk(c)
        block = dot(normed[rows], content[...])
        padded[pl.ds(pl.multiple_of(c * BLOCK + 8, 8), BLOCK)] = block
        values[rows] = block.astype(bf16)
        return carry

    lax.fori_loop(0, chunks, project, 0)

    def gains(c, carry):
        rows = chunk(c)
        pre = conv_taps(padded[halo(c)], filters)
        inside = (c * BLOCK + iota((BLOCK, GROUP), 0)) < length[0]
        act = jnp.where(inside, pre * sigmoid(pre), 0.0).astype(bf16)
        x_low[rows] = act
        low = lane_low()
        end_block = ends_g[rows]
        start_block = starts_g[rows]
        step_block = steps_g[rows]
        for p in range(pairs):
            lanes = slice(2 * HEAD * p, 2 * HEAD * (p + 1))
            end = jnp.where(low, spread(end_block, 2 * p), spread(end_block, 2 * p + 1))
            start = jnp.where(low, spread(start_block, 2 * p), spread(start_block, 2 * p + 1))
            step = jnp.where(low, spread(step_block, 2 * p), spread(step_block, 2 * p + 1))
            total = end[BLOCK - 1 : BLOCK]
            xs = act[:, lanes].astype(f32) * step
            scaled[rows, lanes] = xs
            totals[c, :, lanes] = jnp.broadcast_to(total, (8, 2 * HEAD))
            both = jnp.concatenate((jnp.exp2(total - end) * xs, jnp.exp2(start) * xs), axis=1)
            gain = dot(select_t[c, :STATE], both.astype(bf16))
            gain_e[c, :, lanes] = gain[:, : 2 * HEAD]
            gain_l[c, :, lanes] = gain[:, 2 * HEAD :]
        return carry

    lax.fori_loop(0, chunks, gains, 0)

    state = jnp.zeros((STATE, GROUP), f32)
    for c in range(chunks):
        early[c] = state.astype(bf16)
        state = jnp.exp2(totals[c, :1]) * state + gain_e[c]
    state = jnp.zeros((STATE, GROUP), f32)
    for c in reversed(range(chunks)):
        late[c] = state.astype(bf16)
        state = jnp.exp2(totals[c, :1]) * state + gain_l[c]

    def mix(c, carry):
        rows = chunk(c)
        low = lane_low()
        end_block = ends_g[rows]
        start_block = starts_g[rows]
        coupled = gram[c]
        for p in range(pairs):
            lanes = slice(2 * HEAD * p, 2 * HEAD * (p + 1))
            ends_p = [spread(end_block, 2 * p + k) for k in range(2)]
            starts_p = [spread(start_block, 2 * p + k) for k in range(2)]
            coupling = []
            for k in range(2):
                end_row = ends_t[0, 2 * p + k : 2 * p + k + 1, rows]
                start_row = starts_t[0, 2 * p + k : 2 * p + k + 1, rows]
                power = jnp.exp2(jnp.minimum(ends_p[k] - end_row, start_row - starts_p[k]))
                coupling.append((coupled * power).astype(bf16))
            xs = scaled[rows, lanes]
            inner = dot(jnp.concatenate(coupling, axis=1), pair_rows(xs, low))
            states = jnp.concatenate((early[c, :, lanes], late[c, :, lanes]), axis=1)
            outer = dot(c_rows[rows], states)
            end = jnp.where(low, ends_p[0], ends_p[1])
            start = jnp.where(low, starts_p[0], starts_p[1])
            total = end[BLOCK - 1 : BLOCK]
            mixed[rows, lanes] = (
                inner
                + jnp.exp2(end) * outer[:, : 2 * HEAD]
                + jnp.exp2(total - start) * outer[:, 2 * HEAD :]
                + shortcut[:, lanes] * x_low[rows, lanes].astype(f32)
            )
        return carry

    lax.fori_loop(0, chunks, mix, 0)


def gate_kernel(
    first, last, inner_width, *refs
):
    refs = list(refs)
    length, normed, gating, out_t, amplitude, mixed = refs[:6]
    refs = refs[6:]
    if not first:
        squares_in, total_in = refs[:2]
        refs = refs[2:]
    if last:
        tokens, cotangent = refs[:2]
        refs = refs[2:]
        gate_out, scale_out, cross_out, layer_out, squares, total = refs
    else:
        gate_out, squares, total = refs
    chunks = normed.shape[0] // BLOCK
    step = pl.program_id(0)

    @pl.when(step == 0)
    def _():
        if first:
            squares[...] = jnp.zeros(squares.shape, f32)
            total[...] = jnp.zeros(total.shape, f32)
        else:
            squares[...] = squares_in[...]
            total[...] = total_in[...]

    def body(c, carry):
        rows = chunk(c)
        gate = dot(normed[rows], gating[...])
        gate_out[rows] = gate
        gated = mixed[rows] * (gate * sigmoid(gate))
        square = gated * gated
        squares[rows] += square[:, : GROUP // 2] + square[:, GROUP // 2 :]
        total[rows] += dot_nt((gated * amplitude[...]).astype(bf16), out_t[...])
        return carry

    lax.fori_loop(0, chunks, body, 0)

    if last:

        @pl.when(step == pl.num_programs(0) - 1)
        def _():
            def finish(c, carry):
                rows = chunk(c)
                mean = jnp.sum(squares[rows], axis=1, keepdims=True) / inner_width
                scale = lax.rsqrt(mean + epsilon)
                inside = (c * BLOCK + iota((BLOCK, 1), 0)) < length[0]
                projected = total[rows]
                sum_out = tokens[rows].astype(f32) + scale * projected
                layer_out[rows] = jnp.where(inside, sum_out, 0.0).astype(bf16)
                inner = jnp.sum(cotangent[rows].astype(f32) * projected, axis=1, keepdims=True)
                cross = scale * scale * scale * inner / inner_width
                scale_out[rows] = jnp.broadcast_to(scale, (BLOCK, BLOCK))
                cross_out[rows] = jnp.broadcast_to(cross, (BLOCK, BLOCK))
                return carry

            lax.fori_loop(0, chunks, finish, 0)


def gate_back_kernel(
    cotangent, cotangent_t, normed_t, out_t, amplitude, mixed, gate_in, x_low, scale_in, cross_in,
    mixed_grad, gate_grad, gating_grad, out_grad, amplitude_grad, shortcut_grad, gated_s,
):
    chunks = cotangent.shape[0] // BLOCK

    def body(c, carry):
        amplitude_sum, shortcut_sum = carry
        rows = chunk(c)
        dgated = dot(cotangent[rows], out_t[...])
        gate = gate_in[rows]
        sig = sigmoid(gate)
        act = gate * sig
        slope = sig * (1.0 + gate * (1.0 - sig))
        y = mixed[rows]
        gz = y * act
        scale = jnp.concatenate((scale_in[rows], scale_in[rows]), axis=1)
        cross = jnp.concatenate((cross_in[rows], cross_in[rows]), axis=1)
        unit = gz * scale
        gated_s[rows] = (unit * amplitude[...]).astype(bf16)
        dgz = scale * (amplitude[...] * dgated) - gz * cross
        gate_grad[rows] = (dgz * y * slope).astype(bf16)
        dmix = dgz * act
        mixed_grad[rows] = dmix.astype(bf16)
        amplitude_sum = amplitude_sum + jnp.sum(dgated * unit, axis=0, keepdims=True)
        shortcut_sum = shortcut_sum + jnp.sum(
            dmix * x_low[rows].astype(f32), axis=0, keepdims=True
        )
        return amplitude_sum, shortcut_sum

    zero = jnp.zeros((1, GROUP), f32)
    amplitude_sum, shortcut_sum = lax.fori_loop(0, chunks, body, (zero, zero))
    amplitude_grad[...] = amplitude_sum
    shortcut_grad[...] = shortcut_sum
    gating_grad[...] = dot(normed_t[...], gate_grad[...]).astype(bf16)
    out_grad[...] = dot(cotangent_t[...], gated_s[...]).astype(bf16)


def mix_back_kernel(half, first, last, *refs):
    refs = list(refs)
    (
        length, normed_t, filters, shortcut, b_rows, c_rows, select_t, gram_t,
        ends, starts, steps, ends_t, starts_t, mixed_grad, x_low, values, early, late,
    ) = refs[:18]
    refs = refs[18:]
    if not first:
        gram_in, b_in, c_in = refs[:3]
        refs = refs[3:]
    (
        values_grad, content_grad, filters_grad, decay_grad, direct_grad, gram_grad, b_grad, c_grad,
        padded, ends_g, starts_g, steps_g, pre_grad, gain_e, gain_l, totals,
        early_grad, late_grad, sums, inside_sums, through,
    ) = refs
    step_id = pl.program_id(0)
    heads_half = pl.num_programs(0) * (GROUP // HEAD)
    base = half * heads_half + step_id * (GROUP // HEAD)
    rows_all = x_low.shape[0]
    chunks = rows_all // BLOCK
    pairs = GROUP // (2 * HEAD)

    @pl.when(step_id == 0)
    def _():
        if first:
            gram_grad[...] = jnp.zeros(gram_grad.shape, f32)
            b_grad[...] = jnp.zeros(b_grad.shape, f32)
            c_grad[...] = jnp.zeros(c_grad.shape, f32)
        else:
            gram_grad[...] = gram_in[...]
            b_grad[...] = b_in[...]
            c_grad[...] = c_in[...]

    roll_heads(ends, ends_g, base)
    roll_heads(starts, starts_g, base)
    roll_heads(steps, steps_g, base)
    padded[0:8] = jnp.zeros((8, GROUP), f32)
    pre_grad[rows_all : rows_all + 8] = jnp.zeros((8, GROUP), f32)

    def gains(c, carry):
        rows = chunk(c)
        low = lane_low()
        padded[pl.ds(pl.multiple_of(c * BLOCK + 8, 8), BLOCK)] = values[rows].astype(f32)
        end_block = ends_g[rows]
        start_block = starts_g[rows]
        for p in range(pairs):
            lanes = slice(2 * HEAD * p, 2 * HEAD * (p + 1))
            end = jnp.where(low, spread(end_block, 2 * p), spread(end_block, 2 * p + 1))
            start = jnp.where(low, spread(start_block, 2 * p), spread(start_block, 2 * p + 1))
            total = end[BLOCK - 1 : BLOCK]
            totals[c, :, lanes] = jnp.broadcast_to(total, (8, 2 * HEAD))
            dy = mixed_grad[rows, lanes].astype(f32)
            both = jnp.concatenate((jnp.exp2(end) * dy, jnp.exp2(total - start) * dy), axis=1)
            gain = dot(select_t[c, STATE:], both.astype(bf16))
            gain_e[c, :, lanes] = gain[:, : 2 * HEAD]
            gain_l[c, :, lanes] = gain[:, 2 * HEAD :]
        return carry

    lax.fori_loop(0, chunks, gains, 0)

    state = jnp.zeros((STATE, GROUP), f32)
    for c in reversed(range(chunks)):
        early_grad[c] = state.astype(bf16)
        kept = jnp.exp2(totals[c, :1]) * state
        through[c : c + 1] = jnp.sum(kept * early[c].astype(f32), axis=0, keepdims=True)
        state = kept + gain_e[c]
    state = jnp.zeros((STATE, GROUP), f32)
    for c in range(chunks):
        late_grad[c] = state.astype(bf16)
        kept = jnp.exp2(totals[c, :1]) * state
        through[c : c + 1] += jnp.sum(kept * late[c].astype(f32), axis=0, keepdims=True)
        state = kept + gain_l[c]

    down = iota((BLOCK, BLOCK), 0)
    across = iota((BLOCK, BLOCK), 1)

    def mix(c, carry):
        rows = chunk(c)
        low = lane_low()
        both_tri = jnp.concatenate((down >= across, down <= across), axis=1).astype(f32).astype(bf16)
        end_block = ends_g[rows]
        start_block = starts_g[rows]
        step_block = steps_g[rows]
        coupled = gram_t[c]
        gram_sum = gram_grad[c]
        b_sum = b_grad[rows]
        c_sum = c_grad[rows]
        lane_sums = [jnp.zeros((8, BLOCK), f32) for _ in range(5)]
        head_rows = []
        for p in range(pairs):
            lanes = slice(2 * HEAD * p, 2 * HEAD * (p + 1))
            ends_p = [spread(end_block, 2 * p + k) for k in range(2)]
            starts_p = [spread(start_block, 2 * p + k) for k in range(2)]
            end = jnp.where(low, ends_p[0], ends_p[1])
            start = jnp.where(low, starts_p[0], starts_p[1])
            total = end[BLOCK - 1 : BLOCK]
            step = jnp.where(low, spread(step_block, 2 * p), spread(step_block, 2 * p + 1))
            x = x_low[rows, lanes].astype(f32)
            dy = mixed_grad[rows, lanes].astype(f32)
            xs = x * step
            dy_rows = pair_rows(dy, low)
            powers = []
            coupling = []
            for k in range(2):
                end_row = ends_t[0, 2 * p + k : 2 * p + k + 1, rows]
                start_row = starts_t[0, 2 * p + k : 2 * p + k + 1, rows]
                power = jnp.exp2(jnp.minimum(end_row - ends_p[k], starts_p[k] - start_row))
                powers.append(power)
                coupling.append((coupled * power).astype(bf16))
            coupling_both = jnp.concatenate(coupling, axis=1)
            inner = dot(coupling_both, dy_rows)
            pair_products = dot_nt(xs.astype(bf16), dy_rows)
            for k in range(2):
                product = pair_products[:, BLOCK * k : BLOCK * (k + 1)]
                gram_sum = gram_sum + product * powers[k]
                spread_log = (product * coupling[k].astype(f32)).astype(bf16)
                crossing = dot(spread_log, both_tri)
                picked = jnp.where(
                    down < across,
                    crossing[:, :BLOCK],
                    jnp.where(down > across, crossing[:, BLOCK:], 0.0),
                )
                head_rows.append(jnp.sum(picked, axis=0, keepdims=True))
            states = jnp.concatenate((early[c, :, lanes], late[c, :, lanes]), axis=1)
            states_grad = jnp.concatenate((early_grad[c, :, lanes], late_grad[c, :, lanes]), axis=1)
            raw_y = dot(c_rows[rows], states)
            raw_x = dot(b_rows[rows], states_grad)
            dy_both = jnp.concatenate((jnp.exp2(end) * dy, jnp.exp2(total - start) * dy), axis=1)
            weight_both = jnp.concatenate((jnp.exp2(total - end), jnp.exp2(start)), axis=1)
            xs_both = jnp.concatenate((xs, xs), axis=1) * weight_both
            outer_both = weight_both * raw_x
            c_sum = c_sum + dot_nt(dy_both.astype(bf16), states)
            b_sum = b_sum + dot_nt(xs_both.astype(bf16), states_grad)
            grad_xs = inner + outer_both[:, : 2 * HEAD] + outer_both[:, 2 * HEAD :]
            from_y = dy_both * raw_y
            from_x = xs_both * raw_x
            products = (
                from_y[:, : 2 * HEAD],
                from_y[:, 2 * HEAD :],
                from_x[:, : 2 * HEAD],
                from_x[:, 2 * HEAD :],
                x * grad_xs,
            )
            row_id = iota((8, BLOCK), 0)
            lane_id = iota((8, BLOCK), 1)
            pick = (row_id == 2 * p + lane_id // HEAD).astype(f32).astype(bf16)
            for q in range(5):
                lane_sums[q] = lane_sums[q] + dot_nt(pick, products[q].astype(bf16))
            pre_grad[rows, lanes] = step * grad_xs + shortcut[:, lanes] * dy
        gram_grad[c] = gram_sum
        b_grad[rows] = b_sum
        c_grad[rows] = c_sum
        tile = pl.ds(pl.multiple_of(c * 8, 8), 8)
        for q in range(5):
            sums[q, tile] = lane_sums[q]
        inside_sums[tile] = jnp.concatenate(head_rows + [jnp.zeros((4, BLOCK), f32)], axis=0)
        return carry

    lax.fori_loop(0, chunks, mix, 0)

    head_cols = (iota((GROUP, BLOCK), 0) // HEAD == iota((GROUP, BLOCK), 1)).astype(f32)
    through_heads = dot_full(through[...], head_cols)
    tall = 8 * chunks
    chunk_rows = (iota((tall, chunks), 0) // 8 == iota((tall, chunks), 1)).astype(f32)
    through_tall = dot_full(chunk_rows, through_heads)
    own = iota((tall, BLOCK), 1) == iota((tall, BLOCK), 0) % 8
    through_rows = jnp.sum(jnp.where(own, through_tall, 0.0), axis=1, keepdims=True)
    decay_grad[0] = (
        inside_sums[...]
        + dot_full(sums[0], (down >= across).astype(f32))
        + dot_full(sums[1], (down <= across).astype(f32))
        + dot_full(sums[2], (down < across).astype(f32))
        + dot_full(sums[3], (down > across).astype(f32))
        + through_rows
    )
    direct_grad[0] = sums[4]

    def conv_back(c, carry):
        rows = chunk(c)
        window = padded[halo(c)]
        pre = conv_taps(window, filters)
        sig = sigmoid(pre)
        inside = (c * BLOCK + iota((BLOCK, GROUP), 0)) < length[0]
        grad = jnp.where(inside, pre_grad[rows] * (sig * (1.0 + pre * (1.0 - sig))), 0.0)
        pre_grad[rows] = grad
        return tuple(
            carry[k]
            + jnp.sum(grad * window[5 + k : 5 + k + BLOCK], axis=0, keepdims=True)
            for k in range(4)
        )

    zero = jnp.zeros((1, GROUP), f32)
    filter_sums = lax.fori_loop(0, chunks, conv_back, (zero,) * 4)
    filters_grad[...] = jnp.concatenate(filter_sums, axis=0)

    def conv_shift(c, carry):
        rows = chunk(c)
        window = pre_grad[halo(c)]
        total = window[:BLOCK] * filters[3:4]
        for ahead in range(1, 4):
            total = total + window[ahead : ahead + BLOCK] * filters[3 - ahead : 4 - ahead]
        values_grad[rows] = total.astype(bf16)
        return carry

    lax.fori_loop(0, chunks, conv_shift, 0)
    content_grad[...] = dot(normed_t[...], values_grad[...]).astype(bf16)

    if last:

        @pl.when(step_id == pl.num_programs(0) - 1)
        def _():
            def finish(c, carry):
                rows = chunk(c)
                grad = jnp.where(down != across, gram_grad[c], 0.0)
                b_grad[rows] += dot(grad.astype(bf16), c_rows[rows])
                c_grad[rows] += dot(grad.T.astype(bf16), b_rows[rows])
                return carry

            lax.fori_loop(0, chunks, finish, 0)


def whole(shape):
    return pl.BlockSpec(shape, lambda *_: (0,) * len(shape))


def columns(rows, width=GROUP, after=0):
    return pl.BlockSpec((rows, width), lambda g, *_: (0, g + after))


def planes(shape):
    return pl.BlockSpec(shape, lambda g, *_: (0,) * (len(shape) - 1) + (g,))


def turned(after, rows):
    return pl.BlockSpec((1, 8, rows), lambda g, *_: (g + after, 0, 0))


def lead(shape):
    return pl.BlockSpec((1,) + shape, lambda g, *_: (g,) + (0,) * len(shape))


scalar = pl.BlockSpec(memory_space=pltpu.SMEM)


def shaped(shape, dtype):
    return jax.ShapeDtypeStruct(shape, dtype)


def params(limit=60):
    return pltpu.CompilerParams(vmem_limit_bytes=limit << 20)


def prepare(normed, selector, timestep, kernels, biases, rates, heads):
    rows = normed.shape[0]
    chunks = rows // BLOCK
    groups = heads // (GROUP // HEAD)
    return pl.pallas_call(
        prep_kernel,
        out_shape=(
            shaped((rows, BLOCK), f32),
            shaped((rows, STATE), bf16),
            shaped((rows, STATE), bf16),
            shaped((chunks, BLOCK, BLOCK), bf16),
            shaped((chunks, BLOCK, BLOCK), f32),
            shaped((chunks, BLOCK, BLOCK), f32),
            shaped((rows, BLOCK), f32),
            shaped((rows, BLOCK), f32),
            shaped((rows, BLOCK), f32),
            shaped((groups, 8, rows), f32),
            shaped((groups, 8, rows), f32),
            shaped((groups, 8, rows), f32),
            shaped((groups, 8, rows), f32),
        ),
        scratch_shapes=[pltpu.VMEM((rows + 8, BLOCK), f32)],
        compiler_params=params(),
        name="prep",
    )(normed, selector, timestep, kernels, biases, rates)


def mix_forward(half, length, normed, content, filters, shortcut, prep, inner):
    (_, _, c_rows, select_t, gram, _, ends, starts, steps, ends_t, starts_t, _, _) = prep
    rows, width = normed.shape
    chunks = rows // BLOCK
    grid = inner // GROUP
    return pl.pallas_call(
        functools.partial(mix_kernel, half),
        grid=(grid,),
        in_specs=[
            scalar, whole(normed.shape), columns(width), columns(4), columns(1),
            whole(c_rows.shape), whole(select_t.shape), whole(gram.shape),
            whole(ends.shape), whole(starts.shape), whole(steps.shape),
            turned(half * grid, rows), turned(half * grid, rows),
        ],
        out_specs=(
            columns(rows), columns(rows), columns(rows),
            planes((chunks, STATE, GROUP)), planes((chunks, STATE, GROUP)),
        ),
        out_shape=(
            shaped((rows, inner), f32),
            shaped((rows, inner), bf16),
            shaped((rows, inner), bf16),
            shaped((chunks, STATE, inner), bf16),
            shaped((chunks, STATE, inner), bf16),
        ),
        scratch_shapes=[
            pltpu.VMEM((rows + 8, GROUP), f32),
            pltpu.VMEM((rows, BLOCK), f32),
            pltpu.VMEM((rows, BLOCK), f32),
            pltpu.VMEM((rows, BLOCK), f32),
            pltpu.VMEM((rows, GROUP), f32),
            pltpu.VMEM((chunks, STATE, GROUP), f32),
            pltpu.VMEM((chunks, STATE, GROUP), f32),
            pltpu.VMEM((chunks, 8, GROUP), f32),
        ],
        compiler_params=params(),
        name="mix",
    )(length, normed, content, filters, shortcut, c_rows, select_t, gram, ends, starts, steps, ends_t, starts_t)


def gate_forward(length, normed, weights, amplitude, mixed, carried, finals, inner_width):
    rows, width = normed.shape
    inner = mixed.shape[1]
    grid = inner // GROUP
    first = carried is None
    last = finals is not None
    ins = [length, normed, weights, weights, amplitude, mixed]
    specs = [scalar, whole(normed.shape), columns(width), columns(width, after=grid), columns(1), columns(rows)]
    if not first:
        ins += list(carried)
        specs += [whole(c.shape) for c in carried]
    outs = [shaped((rows, inner), f32)]
    out_specs = [columns(rows)]
    scratch = []
    if last:
        ins += list(finals)
        specs += [whole(c.shape) for c in finals]
        outs += [shaped((rows, BLOCK), f32), shaped((rows, BLOCK), f32), shaped((rows, width), bf16)]
        out_specs += [whole((rows, BLOCK)), whole((rows, BLOCK)), whole((rows, width))]
        scratch = [pltpu.VMEM((rows, BLOCK), f32), pltpu.VMEM((rows, width), f32)]
    else:
        outs += [shaped((rows, BLOCK), f32), shaped((rows, width), f32)]
        out_specs += [whole((rows, BLOCK)), whole((rows, width))]
    return pl.pallas_call(
        functools.partial(gate_kernel, first, last, inner_width),
        grid=(grid,),
        in_specs=specs,
        out_specs=tuple(out_specs),
        out_shape=tuple(outs),
        scratch_shapes=scratch,
        compiler_params=params(),
        name="gate",
    )(*ins)


def gate_backward(
    cotangent, cotangent_t, normed_t, weights, amplitude, mixed, gate_in, x_low, scale, cross
):
    rows, width = cotangent.shape
    inner = mixed.shape[1]
    return pl.pallas_call(
        gate_back_kernel,
        grid=(inner // GROUP,),
        in_specs=[
            whole(cotangent.shape), whole(cotangent_t.shape), whole(normed_t.shape),
            columns(width, after=inner // GROUP), columns(1), columns(rows), columns(rows),
            columns(rows), whole(scale.shape), whole(cross.shape),
        ],
        out_specs=(
            columns(rows), columns(rows), columns(width), columns(width), columns(1), columns(1),
        ),
        out_shape=(
            shaped((rows, inner), bf16),
            shaped((rows, inner), bf16),
            shaped((width, inner), bf16),
            shaped((width, inner), bf16),
            shaped((1, inner), f32),
            shaped((1, inner), f32),
        ),
        scratch_shapes=[pltpu.VMEM((rows, GROUP), bf16)],
        compiler_params=params(),
        name="gate_back",
    )(cotangent, cotangent_t, normed_t, weights, amplitude, mixed, gate_in, x_low, scale, cross)


def mix_backward(half, length, normed_t, filters, shortcut, prep, mixed_grad, kept, carried, last):
    (_, b_rows, c_rows, select_t, _, gram_t, ends, starts, steps, ends_t, starts_t, _, _) = prep
    _, x_low, values, early, late = kept
    width, rows = normed_t.shape
    inner = x_low.shape[1]
    chunks = rows // BLOCK
    grid = inner // GROUP
    first = carried is None
    shared = (b_rows, c_rows, select_t, gram_t, ends, starts, steps, ends_t, starts_t)
    ins = [length, normed_t, filters, shortcut, *shared, mixed_grad, x_low, values, early, late]
    specs = [scalar, whole(normed_t.shape), columns(4), columns(1)]
    specs += [whole(s.shape) for s in shared[:-2]] + [turned(half * grid, rows)] * 2
    specs += [columns(rows)] * 3 + [planes((chunks, STATE, GROUP))] * 2
    if not first:
        ins += list(carried)
        specs += [whole(c.shape) for c in carried]
    tall = 8 * chunks
    return pl.pallas_call(
        functools.partial(mix_back_kernel, half, first, last),
        grid=(grid,),
        in_specs=specs,
        out_specs=(
            columns(rows), columns(width), columns(4), lead((tall, BLOCK)), lead((tall, BLOCK)),
            whole((chunks, BLOCK, BLOCK)), whole((rows, STATE)), whole((rows, STATE)),
        ),
        out_shape=(
            shaped((rows, inner), bf16),
            shaped((width, inner), bf16),
            shaped((4, inner), f32),
            shaped((grid, tall, BLOCK), f32),
            shaped((grid, tall, BLOCK), f32),
            shaped((chunks, BLOCK, BLOCK), f32),
            shaped((rows, STATE), f32),
            shaped((rows, STATE), f32),
        ),
        scratch_shapes=[
            pltpu.VMEM((rows + 8, GROUP), f32),
            pltpu.VMEM((rows, BLOCK), f32),
            pltpu.VMEM((rows, BLOCK), f32),
            pltpu.VMEM((rows, BLOCK), f32),
            pltpu.VMEM((rows + 8, GROUP), f32),
            pltpu.VMEM((chunks, STATE, GROUP), f32),
            pltpu.VMEM((chunks, STATE, GROUP), f32),
            pltpu.VMEM((chunks, 8, GROUP), f32),
            pltpu.VMEM((chunks, STATE, GROUP), bf16),
            pltpu.VMEM((chunks, STATE, GROUP), bf16),
            pltpu.VMEM((5, tall, BLOCK), f32),
            pltpu.VMEM((tall, BLOCK), f32),
            pltpu.VMEM((chunks, GROUP), f32),
        ],
        compiler_params=params(),
        name="mix_back",
    )(*ins)


def shift_down(v, by):
    return jnp.pad(v, ((by, 0), (0, 0)))[: v.shape[0]]


def shift_up(v, by):
    return jnp.pad(v, ((0, by), (0, 0)))[by:]


def select_back(select_in, grad, kernels):
    taps = kernels.shape[0]
    shifted = [shift_down(select_in, taps - 1 - k) for k in range(taps)]
    pre = sum(shifted[k] * kernels[k] for k in range(taps))
    sig = sigmoid(pre)
    grad_pre = grad * (sig * (1.0 + pre * (1.0 - sig)))
    kernels_grad = jnp.stack([jnp.sum(grad_pre * shifted[k], axis=0) for k in range(taps)])
    select_grad = sum(shift_up(grad_pre, taps - 1 - k) * kernels[k] for k in range(taps))
    return select_grad, kernels_grad


def heads_to_rows(tall):
    grid, rows, tokens = tall.shape
    shaped_up = tall.reshape(grid, rows // 8, 8, tokens)[:, :, :4]
    return shaped_up.transpose(0, 2, 1, 3).reshape(grid * 4, (rows // 8) * tokens)


def tree_sum(terms):
    while len(terms) > 1:
        terms = [terms[k] + terms[k + 1] for k in range(0, len(terms), 2)]
    return terms[0]


PLANE = 4


def plane_pairs(size, by):
    return [(i, i - i % PLANE + ((i % PLANE) ^ by)) for i in range(size)]


def column_pairs(size, by):
    return [(i, ((i // PLANE) ^ by) * PLANE + i % PLANE) for i in range(size)]


def place_kernel(count, places, *refs):
    parts, target, sems = refs[:PLANE], refs[PLANE], refs[PLANE + 1]
    copies = []
    for k in range(PLANE):
        for s in range(count):
            slot = k * count + s
            copies.append(
                pltpu.make_async_copy(parts[k].at[s], target.at[places[slot]], sems.at[slot])
            )
    for copy in copies:
        copy.start()
    for copy in copies:
        copy.wait()


def gather_rows(local):
    size = lax.axis_size("dp")
    count = size // PLANE
    me = lax.axis_index("dp")
    pieces = [local] + [
        lax.ppermute(local, "dp", column_pairs(size, s)) for s in range(1, count)
    ]
    column = jnp.stack(pieces)
    parts = [column] + [
        lax.ppermute(column, "dp", plane_pairs(size, k)) for k in range(1, PLANE)
    ]
    high, low = me // PLANE, me % PLANE
    places = jnp.stack([(high ^ s) * PLANE + (low ^ k) for k in range(PLANE) for s in range(count)])
    placed = pl.pallas_call(
        functools.partial(place_kernel, count),
        in_specs=[scalar] + [pl.BlockSpec(memory_space=ANY)] * PLANE,
        out_specs=pl.BlockSpec(memory_space=ANY),
        out_shape=shaped((size,) + local.shape, local.dtype),
        scratch_shapes=[pltpu.SemaphoreType.DMA((PLANE * count,))],
        name="place",
    )(places.astype(jnp.int32), *parts)
    return placed.reshape(size * local.shape[0], local.shape[1])


def reduce_rows(total):
    size = lax.axis_size("dp")
    count = size // PLANE
    me = lax.axis_index("dp")
    high, low = me // PLANE, me % PLANE
    blocks = total.reshape(count, PLANE, total.shape[0] // size, total.shape[1])

    def of_plane(k):
        return lax.dynamic_index_in_dim(blocks, low ^ k, 1, keepdims=False)

    terms = [of_plane(0).astype(f32)] + [
        lax.ppermute(of_plane(k), "dp", plane_pairs(size, k)).astype(f32) for k in range(1, PLANE)
    ]
    column = tree_sum(terms)
    column_low = column.astype(bf16)

    def of_column(s, source):
        return lax.dynamic_index_in_dim(source, high ^ s, 0, keepdims=False)

    terms = [of_column(0, column)] + [
        lax.ppermute(of_column(s, column_low), "dp", column_pairs(size, s)).astype(f32)
        for s in range(1, count)
    ]
    return tree_sum(terms)


def sum_all(vector):
    size = lax.axis_size("dp")
    vector = tree_sum(
        [vector] + [lax.ppermute(vector, "dp", plane_pairs(size, k)) for k in range(1, PLANE)]
    )
    return tree_sum(
        [vector]
        + [lax.ppermute(vector, "dp", column_pairs(size, s)) for s in range(1, size // PLANE)]
    )


def swap(v):
    return lax.ppermute(v, "tensor", [(0, 1), (1, 0)])


def pad_columns(v, width):
    return jnp.pad(v, ((0, 0), (0, width - v.shape[1])))


def on_device(
    layer_in,
    upstream,
    lengths,
    rescale,
    gating,
    content,
    selector,
    timestep,
    filters,
    kernels,
    biases,
    decays,
    shortcut,
    amplitude,
    outgoing,
):
    parts = lax.axis_size("tensor")
    rank = lax.axis_index("tensor")
    micro = lengths.shape[0]
    half_rows = layer_in.shape[0] // micro
    rows = half_rows * parts
    width = layer_in.shape[1]
    inner = gating.shape[1]
    heads = timestep.shape[1]
    state_cols = selector.shape[1]
    inner_width = inner * parts

    first_local = jnp.concatenate((content, selector, pad_columns(timestep, BLOCK)), axis=1)
    second_local = jnp.concatenate((gating, outgoing.T), axis=1)
    first_own = gather_rows(first_local)
    first_other = swap(first_own)
    second_own = gather_rows(second_local)
    second_other = swap(second_own)

    def to_sequence(array):
        blocks = array.reshape(micro, half_rows, width)
        mine = lax.dynamic_index_in_dim(blocks, rank, 0, keepdims=False)
        got = swap(lax.dynamic_index_in_dim(blocks, 1 - rank, 0, keepdims=False))
        return jnp.where(
            rank == 0, jnp.concatenate((mine, got)), jnp.concatenate((got, mine))
        )

    def from_sequence(array):
        mine = lax.dynamic_slice_in_dim(array, rank * half_rows, half_rows, 0)
        got = swap(lax.dynamic_slice_in_dim(array, (1 - rank) * half_rows, half_rows, 0))
        return jnp.where(
            rank == 0, jnp.concatenate((mine, got)), jnp.concatenate((got, mine))
        )

    tokens = to_sequence(layer_in)
    cotangent = to_sequence(upstream)
    length = lax.dynamic_slice_in_dim(lengths, rank, 1, 0)

    flat = jnp.concatenate((filters.reshape(-1), amplitude, biases, decays, shortcut))
    flat_other = swap(flat)
    taps = filters.shape[0]

    def unpack(vector):
        edges = [0, taps * inner, (taps + 1) * inner]
        edges += [edges[-1] + heads * k for k in range(1, 4)]
        cut = [vector[a:b] for a, b in zip(edges[:-1], edges[1:])]
        return (cut[0].reshape(taps, inner), cut[1].reshape(1, inner), *cut[2:])

    filters_2, amplitude_2, biases_2, decays_2, shortcut_2 = zip(unpack(flat), unpack(flat_other))

    def head_lanes(pair):
        return pad_columns(jnp.concatenate(pair).reshape(1, -1), BLOCK)

    rates = jnp.exp(jnp.concatenate(decays_2))
    rate_lanes = pad_columns(rates.reshape(1, -1), BLOCK)
    shortcut_lanes = [jnp.repeat(s, HEAD).reshape(1, inner) for s in shortcut_2]
    split = inner + state_cols
    selector_full = first_own[:, inner:split]
    timestep_full = jnp.concatenate(
        (first_own[:, split : split + heads], first_other[:, split : split + heads]), axis=1
    )

    tok = tokens.astype(f32)
    inverse = lax.rsqrt(jnp.mean(tok * tok, axis=-1, keepdims=True) + epsilon)
    unit = tok * inverse
    normed = (unit * rescale).astype(bf16)
    inside = jnp.arange(rows)[:, None] < length[0]
    dbranch = jnp.where(inside, cotangent, jnp.zeros_like(cotangent))
    normed_t = normed.T
    dbranch_t = dbranch.T

    prep = prepare(
        normed, selector_full, pad_columns(timestep_full, BLOCK), kernels,
        head_lanes(biases_2), rate_lanes, 2 * heads,
    )
    firsts = (first_own, first_other)
    seconds = (second_own, second_other)
    kept = [
        mix_forward(h, length, normed, firsts[h], filters_2[h], shortcut_lanes[h], prep, inner)
        for h in range(2)
    ]
    gate_own, squares, total = gate_forward(
        length, normed, seconds[0], amplitude_2[0], kept[0][0], None, None, inner_width
    )
    gate_other, scale, cross, layer_seq = gate_forward(
        length, normed, seconds[1], amplitude_2[1], kept[1][0], (squares, total),
        (tokens, dbranch), inner_width,
    )
    gates = (gate_own, gate_other)
    layer_out = from_sequence(layer_seq)

    back = [None, None]
    for h in (1, 0):
        back[h] = gate_backward(
            dbranch, dbranch_t, normed_t, seconds[h], amplitude_2[h], kept[h][0], gates[h],
            kept[h][1], scale, cross,
        )
    second_grads = jnp.concatenate(
        [(back[0][k].astype(f32) + swap(back[1][k]).astype(f32)).astype(bf16) for k in (2, 3)],
        axis=1,
    )
    second_total = reduce_rows(second_grads)

    deep = [None, None]
    deep[1] = mix_backward(
        1, length, normed_t, filters_2[1], shortcut_lanes[1], prep, back[1][0], kept[1], None, False
    )
    deep[0] = mix_backward(
        0, length, normed_t, filters_2[0], shortcut_lanes[0], prep, back[0][0], kept[0],
        deep[1][5:8], True,
    )
    content_total = deep[0][1].astype(f32) + swap(deep[1][1]).astype(f32)

    select_grad, kernels_part = select_back(
        prep[0], jnp.concatenate((deep[0][6], deep[0][7]), axis=1), kernels
    )
    select_grad = select_grad.astype(bf16)
    decay_rows = jnp.concatenate([heads_to_rows(deep[h][3]) for h in range(2)])
    direct_rows = jnp.concatenate([heads_to_rows(deep[h][4]) for h in range(2)])

    def all_heads(tiles):
        return tiles[:, : GROUP // HEAD].reshape(2 * heads, rows)

    step_rows = (direct_rows - rates[:, None] * decay_rows) * all_heads(prep[12])
    biases_part = jnp.sum(step_rows, axis=1)
    decays_part = -rates * jnp.sum(all_heads(prep[11]) * decay_rows, axis=1)
    step_rows = step_rows.astype(bf16)
    selector_part = dot(normed_t, select_grad)
    timestep_part = dot_nt(normed_t, step_rows)
    timestep_sum = timestep_part[:, :heads] + swap(timestep_part[:, heads:])
    selector_sum = selector_part + swap(selector_part)
    first_grads = jnp.concatenate(
        (content_total, selector_sum, pad_columns(timestep_sum, BLOCK)), axis=1
    ).astype(bf16)
    first_total = reduce_rows(first_grads)

    grad_normed = dot_nt(select_grad, selector_full) + lax.dot_general(
        step_rows, timestep_full, (((0,), (1,)), ((), ())), preferred_element_type=f32
    )
    for h in range(2):
        grad_normed = grad_normed + dot_nt(deep[h][0], firsts[h][:, :inner])
        grad_normed = grad_normed + dot_nt(back[h][1], seconds[h][:, :inner])
    weighted = grad_normed * rescale
    grad_seq = (
        dbranch.astype(f32)
        + inverse * weighted
        - unit * inverse * jnp.mean(weighted * unit, axis=-1, keepdims=True)
    ).astype(bf16)
    input_grad = from_sequence(grad_seq)
    rescale_part = jnp.sum(grad_normed * unit, axis=0)

    def split_part(own, other):
        return own + swap(other)

    def per_head(row):
        return jnp.sum(row.reshape(heads, HEAD), axis=1)

    tensor_split = split_part(
        *[
            jnp.concatenate(
                (
                    deep[h][2].reshape(-1),
                    back[h][4].reshape(-1),
                    biases_part[h * heads : (h + 1) * heads],
                    decays_part[h * heads : (h + 1) * heads],
                    per_head(back[h][5]),
                )
            )
            for h in range(2)
        ]
    )
    copied = jnp.concatenate((rescale_part, kernels_part.reshape(-1)))
    copied = copied + swap(copied)
    small = sum_all(jnp.concatenate((tensor_split, copied)))
    cut = tensor_split.shape[0]
    filters_grad, amplitude_grad, biases_grad, decays_grad, shortcut_grad = unpack(small[:cut])
    return (
        layer_out,
        input_grad,
        small[cut : cut + width],
        second_total[:, :inner],
        first_total[:, :inner],
        first_total[:, inner:split],
        first_total[:, split : split + heads],
        filters_grad,
        small[cut + width :].reshape(taps, state_cols),
        biases_grad,
        decays_grad,
        shortcut_grad,
        amplitude_grad.reshape(inner),
        second_total[:, inner:].T,
    )


def solution(mesh):
    return jax.shard_map(
        on_device,
        mesh=mesh,
        in_specs=(
            P(("dp", "tensor"), None),
            P(("dp", "tensor"), None),
            P("dp"),
            P(),
            P("dp", "tensor"),
            P("dp", "tensor"),
            P("dp", None),
            P("dp", "tensor"),
            P(None, "tensor"),
            P(),
            P("tensor"),
            P("tensor"),
            P("tensor"),
            P("tensor"),
            P("tensor", "dp"),
        ),
        out_specs=(
            P(("dp", "tensor"), None),
            P(("dp", "tensor"), None),
            P(),
            P("dp", "tensor"),
            P("dp", "tensor"),
            P("dp", None),
            P("dp", "tensor"),
            P(None, "tensor"),
            P(),
            P("tensor"),
            P("tensor"),
            P("tensor"),
            P("tensor"),
            P("tensor", "dp"),
        ),
        check_vma=False,
    )
```

```python
import functools

import jax
import jax.numpy as jnp
from jax import lax
from jax.experimental import pallas as pl
from jax.experimental.pallas import tpu as pltpu
from jax.sharding import Mesh
from jax.sharding import PartitionSpec as P

BLOCK = 128
HEAD = 64
STATE = 64
GROUP = 256
LOG2E = 1.4426950408889634
epsilon = 1e-05
f32 = jnp.float32
bf16 = jnp.bfloat16
ANY = pl.ANY


def dot(a, b):
    return lax.dot_general(a, b, (((1,), (0,)), ((), ())), preferred_element_type=f32)


def dot_nt(a, b):
    return lax.dot_general(a, b, (((1,), (1,)), ((), ())), preferred_element_type=f32)


def dot_full(a, b):
    return lax.dot_general(
        a, b, (((1,), (0,)), ((), ())), preferred_element_type=f32, precision=lax.Precision.HIGHEST
    )


def iota(shape, axis):
    return lax.broadcasted_iota(jnp.int32, shape, axis)


def chunk(c, after=0):
    return slice(c * BLOCK + after, (c + 1) * BLOCK + after)


def each_chunk(chunks, body, carry):
    for c in range(chunks):
        carry = body(c, carry)
    return carry


def sigmoid(v):
    return 1.0 / (1.0 + jnp.exp(-v))


def conv_taps(padded, c, taps_ref):
    total = padded[chunk(c, 8)] * taps_ref[3:4]
    for back in range(1, 4):
        total = total + padded[chunk(c, 8 - back)] * taps_ref[3 - back : 4 - back]
    return total


def lane_low():
    return iota((BLOCK, 2 * HEAD), 1) < HEAD


def spread(block, column):
    index = jnp.full((BLOCK, BLOCK), column, jnp.int32)
    return jnp.take_along_axis(block, index, axis=1, mode="promise_in_bounds")


def pair_rows(piece, low):
    return jnp.concatenate(
        (jnp.where(low, piece, 0.0), jnp.where(low, 0.0, piece)), axis=0
    ).astype(bf16)


def prep_kernel(
    heads, rank, normed, extra_own, extra_other, kernels, biases, rates,
    select_in, b_rows, c_rows, select_t, gram, gram_t,
    ends, starts, steps, ends_t, starts_t, steps_t, slope_t, padded, logits_s,
):
    chunks = normed.shape[0] // BLOCK
    groups = ends_t.shape[0]
    per = GROUP // HEAD
    down = iota((BLOCK, BLOCK), 0)
    across = iota((BLOCK, BLOCK), 1)
    tri = (down >= across).astype(f32)
    off = (down != across).astype(f32)
    padded[0:8] = jnp.zeros((8, BLOCK), f32)

    own = dot(normed[...], extra_own[...])
    other = dot(normed[...], extra_other[...])
    lane = iota(own.shape, 1)
    first = jnp.where(rank[0] == 0, own, other)
    second = jnp.where(rank[0] == 0, other, own)
    selected = jnp.where(lane < STATE, first, pltpu.roll(second, STATE, 1))
    select_in[...] = selected
    padded[8:] = selected
    logits_s[...] = jnp.where(
        lane < heads, pltpu.roll(own, BLOCK - STATE, 1), pltpu.roll(other, BLOCK - STATE + heads, 1)
    )

    def body(c, carry):
        rows = chunk(c)
        pre = conv_taps(padded, c, kernels)
        act = pre * sigmoid(pre)
        act_t = act.T.astype(bf16)
        act = act.astype(bf16)
        b_rows[rows] = act[:, :STATE]
        c_rows[rows] = act[:, STATE:]
        select_t[c] = act_t
        gram[c] = dot(act[:, STATE:], act_t[:STATE]) * off
        gram_t[c] = dot(act[:, :STATE], act_t[STATE:]) * off
        logits = logits_s[rows] + biases[...]
        small = jnp.exp(-jnp.abs(logits))
        whole = 1.0 + small
        log_part = jnp.where(
            whole == 1.0, small, jnp.log(whole) * (small / jnp.where(whole == 1.0, 1.0, whole - 1.0))
        )
        step = jnp.maximum(logits, 0.0) + log_part
        decay = -rates[...] * step
        inclusive = dot_full(tri, decay)
        end = inclusive * LOG2E
        start = (inclusive - decay) * LOG2E
        ends[rows] = end
        starts[rows] = start
        steps[rows] = step
        turned = ((ends_t, end), (starts_t, start), (steps_t, step), (slope_t, sigmoid(logits)))
        for target, value in turned:
            value_t = value.T
            for g in range(groups):
                target[g, 0:per, rows] = value_t[g * per : (g + 1) * per]
        return carry

    each_chunk(chunks, body, 0)


def mix_kernel(
    half, length, normed, content, filters, shortcut, c_rows, select_t, gram,
    ends, starts, steps, ends_t, starts_t,
    mixed, x_low, values, early, late,
    ends_w, starts_w, padded, scaled, gain_e, gain_l, totals,
):
    heads_half = pl.num_programs(0) * (GROUP // HEAD)
    base = half * heads_half + pl.program_id(0) * (GROUP // HEAD)
    chunks = normed.shape[0] // BLOCK
    pairs = GROUP // (2 * HEAD)
    padded[0:8] = jnp.zeros((8, GROUP), f32)
    block = dot(normed[...], content[...])
    padded[8:] = block
    values[...] = block.astype(bf16)

    def gains(c, carry):
        rows = chunk(c)
        pre = conv_taps(padded, c, filters)
        inside = (c * BLOCK + iota((BLOCK, GROUP), 0)) < length[0]
        act = jnp.where(inside, pre * sigmoid(pre), 0.0).astype(bf16)
        x_low[rows] = act
        low = lane_low()
        end_block = ends[rows]
        start_block = starts[rows]
        step_block = steps[rows]
        for p in range(pairs):
            lanes = slice(2 * HEAD * p, 2 * HEAD * (p + 1))
            ends_p = [spread(end_block, base + 2 * p + k) for k in range(2)]
            starts_p = [spread(start_block, base + 2 * p + k) for k in range(2)]
            steps_p = [spread(step_block, base + 2 * p + k) for k in range(2)]
            for k in range(2):
                wide = slice(BLOCK * (2 * p + k), BLOCK * (2 * p + k + 1))
                ends_w[rows, wide] = ends_p[k]
                starts_w[rows, wide] = starts_p[k]
            end = jnp.where(low, *ends_p)
            start = jnp.where(low, *starts_p)
            step = jnp.where(low, *steps_p)
            total = end[BLOCK - 1 : BLOCK]
            xs = act[:, lanes].astype(f32) * step
            scaled[rows, lanes] = xs
            totals[c, :, lanes] = jnp.broadcast_to(total, (8, 2 * HEAD))
            both = jnp.concatenate((jnp.exp2(total - end) * xs, jnp.exp2(start) * xs), axis=1)
            gain = dot(select_t[c, :STATE], both.astype(bf16))
            gain_e[c, :, lanes] = gain[:, : 2 * HEAD]
            gain_l[c, :, lanes] = gain[:, 2 * HEAD :]
        return carry

    each_chunk(chunks, gains, 0)

    state = jnp.zeros((STATE, GROUP), f32)
    for c in range(chunks):
        early[c] = state.astype(bf16)
        state = jnp.exp2(totals[c, :1]) * state + gain_e[c]
    state = jnp.zeros((STATE, GROUP), f32)
    for c in reversed(range(chunks)):
        late[c] = state.astype(bf16)
        state = jnp.exp2(totals[c, :1]) * state + gain_l[c]

    def mix(c, carry):
        rows = chunk(c)
        low = lane_low()
        coupled = gram[c]
        for p in range(pairs):
            lanes = slice(2 * HEAD * p, 2 * HEAD * (p + 1))
            wides = [slice(BLOCK * (2 * p + k), BLOCK * (2 * p + k + 1)) for k in range(2)]
            ends_p = [ends_w[rows, w] for w in wides]
            starts_p = [starts_w[rows, w] for w in wides]
            coupling = []
            for k in range(2):
                end_row = ends_t[0, 2 * p + k : 2 * p + k + 1, rows]
                start_row = starts_t[0, 2 * p + k : 2 * p + k + 1, rows]
                power = jnp.exp2(jnp.minimum(ends_p[k] - end_row, start_row - starts_p[k]))
                coupling.append((coupled * power).astype(bf16))
            xs = scaled[rows, lanes]
            inner = dot(jnp.concatenate(coupling, axis=1), pair_rows(xs, low))
            states = jnp.concatenate((early[c, :, lanes], late[c, :, lanes]), axis=1)
            outer = dot(c_rows[rows], states)
            end = jnp.where(low, *ends_p)
            start = jnp.where(low, *starts_p)
            total = end[BLOCK - 1 : BLOCK]
            mixed[rows, lanes] = (
                inner
                + jnp.exp2(end) * outer[:, : 2 * HEAD]
                + jnp.exp2(total - start) * outer[:, 2 * HEAD :]
                + shortcut[:, lanes] * x_low[rows, lanes].astype(f32)
            ).astype(bf16)
        return carry

    each_chunk(chunks, mix, 0)


def gate_kernel(
    first, last, inner_width, *refs
):
    refs = list(refs)
    length, normed, gating, out_t, amplitude, mixed = refs[:6]
    refs = refs[6:]
    if not first:
        squares_in, total_in = refs[:2]
        refs = refs[2:]
    if last:
        tokens, cotangent = refs[:2]
        refs = refs[2:]
        gate_out, scale_out, cross_out, layer_out, squares, total, gated_s, gate_s = refs
    else:
        gate_out, squares, total, gated_s, gate_s = refs
    chunks = normed.shape[0] // BLOCK
    step = pl.program_id(0)

    @pl.when(step == 0)
    def _():
        if first:
            squares[...] = jnp.zeros(squares.shape, f32)
            total[...] = jnp.zeros(total.shape, f32)
        else:
            squares[...] = squares_in[...]
            total[...] = total_in[...]

    gate_s[...] = dot(normed[...], gating[...])

    def body(c, carry):
        rows = chunk(c)
        gate = gate_s[rows]
        gate_out[rows] = gate
        gated = mixed[rows].astype(f32) * (gate * sigmoid(gate))
        square = gated * gated
        squares[rows] += square[:, : GROUP // 2] + square[:, GROUP // 2 :]
        gated_s[rows] = (gated * amplitude[...]).astype(bf16)
        return carry

    each_chunk(chunks, body, 0)
    total[...] += dot_nt(gated_s[...], out_t[...])

    if last:

        @pl.when(step == pl.num_programs(0) - 1)
        def _():
            def finish(c, carry):
                rows = chunk(c)
                mean = jnp.sum(squares[rows], axis=1, keepdims=True) / inner_width
                scale = lax.rsqrt(mean + epsilon)
                inside = (c * BLOCK + iota((BLOCK, 1), 0)) < length[0]
                projected = total[rows]
                sum_out = tokens[rows].astype(f32) + scale * projected
                layer_out[rows] = jnp.where(inside, sum_out, 0.0).astype(bf16)
                inner = jnp.sum(cotangent[rows].astype(f32) * projected, axis=1, keepdims=True)
                cross = scale * scale * scale * inner / inner_width
                scale_out[rows] = jnp.broadcast_to(scale, (BLOCK, BLOCK))
                cross_out[rows] = jnp.broadcast_to(cross, (BLOCK, BLOCK))
                return carry

            each_chunk(chunks, finish, 0)


def gate_back_kernel(
    cotangent, cotangent_t, normed_t, out_t, amplitude, mixed, gate_in, x_low, scale_in, cross_in,
    mixed_grad, gate_grad, gating_grad, out_grad, amplitude_grad, shortcut_grad, gated_s, dgated_s,
):
    chunks = cotangent.shape[0] // BLOCK
    dgated_s[...] = dot(cotangent[...], out_t[...])

    def body(c, carry):
        amplitude_sum, shortcut_sum = carry
        rows = chunk(c)
        dgated = dgated_s[rows]
        gate = gate_in[rows].astype(f32)
        sig = sigmoid(gate)
        act = gate * sig
        slope = sig * (1.0 + gate * (1.0 - sig))
        y = mixed[rows].astype(f32)
        gz = y * act
        scale = jnp.concatenate((scale_in[rows], scale_in[rows]), axis=1)
        cross = jnp.concatenate((cross_in[rows], cross_in[rows]), axis=1)
        unit = gz * scale
        gated_s[rows] = (unit * amplitude[...]).astype(bf16)
        dgz = scale * (amplitude[...] * dgated) - gz * cross
        gate_grad[rows] = (dgz * y * slope).astype(bf16)
        dmix = dgz * act
        mixed_grad[rows] = dmix.astype(bf16)
        amplitude_sum = amplitude_sum + jnp.sum(dgated * unit, axis=0, keepdims=True)
        shortcut_sum = shortcut_sum + jnp.sum(
            dmix * x_low[rows].astype(f32), axis=0, keepdims=True
        )
        return amplitude_sum, shortcut_sum

    zero = jnp.zeros((1, GROUP), f32)
    amplitude_sum, shortcut_sum = each_chunk(chunks, body, (zero, zero))
    amplitude_grad[...] = amplitude_sum
    shortcut_grad[...] = shortcut_sum
    gating_grad[...] = dot(normed_t[...], gate_grad[...]).astype(bf16)
    out_grad[...] = dot(cotangent_t[...], gated_s[...]).astype(bf16)


def mix_back_kernel(half, first, last, *refs):
    refs = list(refs)
    (
        length, normed_t, filters, shortcut, b_rows, c_rows, select_t, gram_t,
        ends, starts, steps, ends_t, starts_t, mixed_grad, x_low, values, early, late,
    ) = refs[:18]
    refs = refs[18:]
    if not first:
        gram_in, b_in, c_in = refs[:3]
        refs = refs[3:]
    (
        values_grad, content_grad, filters_grad, decay_grad, direct_grad, gram_grad, b_grad, c_grad,
        ends_w, starts_w, steps_w, padded, pre_grad, gain_e, gain_l, totals,
        early_grad, late_grad, sums, local_rows, through,
    ) = refs
    step_id = pl.program_id(0)
    heads_half = pl.num_programs(0) * (GROUP // HEAD)
    base = half * heads_half + step_id * (GROUP // HEAD)
    rows_all = x_low.shape[0]
    chunks = rows_all // BLOCK
    pairs = GROUP // (2 * HEAD)

    @pl.when(step_id == 0)
    def _():
        if first:
            gram_grad[...] = jnp.zeros(gram_grad.shape, f32)
            b_grad[...] = jnp.zeros(b_grad.shape, f32)
            c_grad[...] = jnp.zeros(c_grad.shape, f32)
        else:
            gram_grad[...] = gram_in[...]
            b_grad[...] = b_in[...]
            c_grad[...] = c_in[...]

    padded[0:8] = jnp.zeros((8, GROUP), f32)
    padded[8:] = values[...].astype(f32)
    pre_grad[rows_all : rows_all + 8] = jnp.zeros((8, GROUP), f32)

    def gains(c, carry):
        rows = chunk(c)
        low = lane_low()
        end_block = ends[rows]
        start_block = starts[rows]
        step_block = steps[rows]
        for p in range(pairs):
            lanes = slice(2 * HEAD * p, 2 * HEAD * (p + 1))
            ends_p = [spread(end_block, base + 2 * p + k) for k in range(2)]
            starts_p = [spread(start_block, base + 2 * p + k) for k in range(2)]
            for k in range(2):
                wide = slice(BLOCK * (2 * p + k), BLOCK * (2 * p + k + 1))
                ends_w[rows, wide] = ends_p[k]
                starts_w[rows, wide] = starts_p[k]
            steps_w[rows, lanes] = jnp.where(
                low, *[spread(step_block, base + 2 * p + k) for k in range(2)]
            )
            end = jnp.where(low, *ends_p)
            start = jnp.where(low, *starts_p)
            total = end[BLOCK - 1 : BLOCK]
            totals[c, :, lanes] = jnp.broadcast_to(total, (8, 2 * HEAD))
            dy = mixed_grad[rows, lanes].astype(f32)
            both = jnp.concatenate((jnp.exp2(end) * dy, jnp.exp2(total - start) * dy), axis=1)
            gain = dot(select_t[c, STATE:], both.astype(bf16))
            gain_e[c, :, lanes] = gain[:, : 2 * HEAD]
            gain_l[c, :, lanes] = gain[:, 2 * HEAD :]
        return carry

    each_chunk(chunks, gains, 0)

    state = jnp.zeros((STATE, GROUP), f32)
    for c in reversed(range(chunks)):
        early_grad[c] = state.astype(bf16)
        kept = jnp.exp2(totals[c, :1]) * state
        through[c] = jnp.broadcast_to(
            jnp.sum(kept * early[c].astype(f32), axis=0, keepdims=True), (8, GROUP)
        )
        state = kept + gain_e[c]
    state = jnp.zeros((STATE, GROUP), f32)
    for c in range(chunks):
        late_grad[c] = state.astype(bf16)
        kept = jnp.exp2(totals[c, :1]) * state
        through[c] += jnp.broadcast_to(
            jnp.sum(kept * late[c].astype(f32), axis=0, keepdims=True), (8, GROUP)
        )
        state = kept + gain_l[c]

    down = iota((BLOCK, BLOCK), 0)
    across = iota((BLOCK, BLOCK), 1)

    def mix(c, carry):
        rows = chunk(c)
        low = lane_low()
        coupled = gram_t[c]
        gram_sum = gram_grad[c]
        b_sum = b_grad[rows]
        c_sum = c_grad[rows]
        row_id = iota((8, BLOCK), 0)
        lane_id = iota((8, BLOCK), 1)
        flow = jnp.zeros((8, BLOCK), f32)
        apart = jnp.zeros((16, BLOCK), f32)
        columns_sum = jnp.zeros((BLOCK, BLOCK), f32)
        below_rows = []
        above_rows = []
        for p in range(pairs):
            lanes = slice(2 * HEAD * p, 2 * HEAD * (p + 1))
            wides = [slice(BLOCK * (2 * p + k), BLOCK * (2 * p + k + 1)) for k in range(2)]
            ends_p = [ends_w[rows, w] for w in wides]
            starts_p = [starts_w[rows, w] for w in wides]
            end = jnp.where(low, *ends_p)
            start = jnp.where(low, *starts_p)
            total = end[BLOCK - 1 : BLOCK]
            step = steps_w[rows, lanes]
            x = x_low[rows, lanes].astype(f32)
            dy = mixed_grad[rows, lanes].astype(f32)
            xs = x * step
            dy_rows = pair_rows(dy, low)
            powers = []
            coupling = []
            for k in range(2):
                end_row = ends_t[0, 2 * p + k : 2 * p + k + 1, rows]
                start_row = starts_t[0, 2 * p + k : 2 * p + k + 1, rows]
                power = jnp.exp2(jnp.minimum(end_row - ends_p[k], starts_p[k] - start_row))
                powers.append(power)
                coupling.append(coupled * power)
            inner = dot(jnp.concatenate(coupling, axis=1).astype(bf16), dy_rows)
            pair_products = dot_nt(xs.astype(bf16), dy_rows)
            for k in range(2):
                product = pair_products[:, BLOCK * k : BLOCK * (k + 1)]
                gram_sum = gram_sum + product * powers[k]
                spread_log = product * coupling[k]
                below = jnp.where(down < across, spread_log, 0.0)
                above = spread_log - below
                below_rows.append(jnp.sum(below, axis=0, keepdims=True))
                above_rows.append(jnp.sum(above, axis=0, keepdims=True))
                below_cols = jnp.sum(below, axis=1, keepdims=True)
                above_cols = jnp.sum(above, axis=1, keepdims=True)
                lane = 2 * p + k
                columns_sum = jnp.where(across == lane, below_cols, columns_sum)
                columns_sum = jnp.where(across == lane + 8, above_cols, columns_sum)
            states = jnp.concatenate((early[c, :, lanes], late[c, :, lanes]), axis=1)
            states_grad = jnp.concatenate((early_grad[c, :, lanes], late_grad[c, :, lanes]), axis=1)
            raw_y = dot(c_rows[rows], states)
            raw_x = dot(b_rows[rows], states_grad)
            dy_both = jnp.concatenate((jnp.exp2(end) * dy, jnp.exp2(total - start) * dy), axis=1)
            weight_both = jnp.concatenate((jnp.exp2(total - end), jnp.exp2(start)), axis=1)
            xs_both = jnp.concatenate((xs, xs), axis=1) * weight_both
            outer_both = weight_both * raw_x
            c_sum = c_sum + dot_nt(dy_both.astype(bf16), states)
            b_sum = b_sum + dot_nt(xs_both.astype(bf16), states_grad)
            grad_xs = inner + outer_both[:, : 2 * HEAD] + outer_both[:, 2 * HEAD :]
            from_y = dy_both * raw_y
            from_x = xs_both * raw_x
            local = from_y[:, 2 * HEAD :] - from_x[:, 2 * HEAD :]
            moving = from_y[:, : 2 * HEAD] - from_x[:, : 2 * HEAD] - local
            passed = from_x[:, : 2 * HEAD] + from_y[:, 2 * HEAD :]
            through[c, :, lanes] += jnp.broadcast_to(
                jnp.sum(passed, axis=0, keepdims=True), (8, 2 * HEAD)
            )
            pick = (row_id == 2 * p + lane_id // HEAD).astype(f32)
            none = jnp.zeros((8, BLOCK), f32)
            pick_same = jnp.concatenate((pick, pick), axis=1).astype(bf16)
            pick_apart = jnp.concatenate(
                (
                    jnp.concatenate((pick, none), axis=1),
                    jnp.concatenate((none, pick), axis=1),
                ),
                axis=0,
            ).astype(bf16)
            high = moving.astype(bf16)
            rest = (moving - high.astype(f32)).astype(bf16)
            flow = flow + dot_nt(pick_same, jnp.concatenate((high, rest), axis=1))
            apart = apart + dot_nt(
                pick_apart, jnp.concatenate((local, x * grad_xs), axis=1).astype(bf16)
            )
            pre_grad[rows, lanes] = step * grad_xs + shortcut[:, lanes] * dy
        gram_grad[c] = gram_sum
        b_grad[rows] = b_sum
        c_grad[rows] = c_sum
        tile = slice(c * 8, c * 8 + 8)
        flat = columns_sum.T
        pad = jnp.zeros((4, BLOCK), f32)
        below_all = jnp.concatenate(below_rows + [pad], axis=0)
        above_all = jnp.concatenate(above_rows + [pad], axis=0)
        below_flat = flat[0:8]
        above_flat = flat[8:16]
        sums[tile] = flow + (below_all - below_flat) - (above_all - above_flat)
        local_rows[tile] = apart[:8] + (above_all - above_flat)
        direct_grad[0, tile] = apart[8:]
        return carry

    each_chunk(chunks, mix, 0)

    head_cols = (iota((GROUP, BLOCK), 0) // HEAD == iota((GROUP, BLOCK), 1)).astype(f32)
    tall = 8 * chunks
    through_tall = dot_full(through[...].reshape(tall, GROUP), head_cols)
    own = iota((tall, BLOCK), 1) == iota((tall, BLOCK), 0) % 8
    through_rows = jnp.sum(jnp.where(own, through_tall, 0.0), axis=1, keepdims=True)
    decay_grad[0] = (
        dot_full(sums[...], (down >= across).astype(f32)) + local_rows[...] + through_rows
    )

    def conv_back(c, carry):
        rows = chunk(c)
        pre = conv_taps(padded, c, filters)
        sig = sigmoid(pre)
        inside = (c * BLOCK + iota((BLOCK, GROUP), 0)) < length[0]
        grad = jnp.where(inside, pre_grad[rows] * (sig * (1.0 + pre * (1.0 - sig))), 0.0)
        pre_grad[rows] = grad
        return tuple(
            carry[k]
            + jnp.sum(grad * padded[chunk(c, 5 + k)], axis=0, keepdims=True)
            for k in range(4)
        )

    zero = jnp.zeros((1, GROUP), f32)
    filter_sums = each_chunk(chunks, conv_back, (zero,) * 4)
    filters_grad[...] = jnp.concatenate(filter_sums, axis=0)

    def conv_shift(c, carry):
        rows = chunk(c)
        total = pre_grad[rows] * filters[3:4]
        for ahead in range(1, 4):
            total = total + pre_grad[chunk(c, ahead)] * filters[3 - ahead : 4 - ahead]
        values_grad[rows] = total.astype(bf16)
        return carry

    each_chunk(chunks, conv_shift, 0)
    content_grad[...] = dot(normed_t[...], values_grad[...]).astype(bf16)

    if last:

        @pl.when(step_id == pl.num_programs(0) - 1)
        def _():
            def finish(c, carry):
                rows = chunk(c)
                grad = jnp.where(down != across, gram_grad[c], 0.0)
                b_grad[rows] += dot(grad.astype(bf16), c_rows[rows])
                c_grad[rows] += dot(grad.T.astype(bf16), b_rows[rows])
                return carry

            each_chunk(chunks, finish, 0)


def whole(shape):
    return pl.BlockSpec(shape, lambda *_: (0,) * len(shape), pipeline_mode=pl.Buffered(1))


def columns(rows, width=GROUP, after=0):
    return pl.BlockSpec((rows, width), lambda g, *_: (0, g + after))


def planes(shape):
    return pl.BlockSpec(shape, lambda g, *_: (0,) * (len(shape) - 1) + (g,))


def turned(after, rows):
    return pl.BlockSpec((1, 8, rows), lambda g, *_: (g + after, 0, 0))


def lead(shape):
    return pl.BlockSpec((1,) + shape, lambda g, *_: (g,) + (0,) * len(shape))


scalar = pl.BlockSpec(memory_space=pltpu.SMEM)


def shaped(shape, dtype):
    return jax.ShapeDtypeStruct(shape, dtype)


def params(limit=60):
    return pltpu.CompilerParams(vmem_limit_bytes=limit << 20)


def cost(micros):
    return pl.CostEstimate(flops=0, bytes_accessed=int(micros * 3.0e6), transcendentals=0)


def prepare(rank, normed, first_own, first_other, kernels, biases, rates, heads):
    rows, width = normed.shape
    chunks = rows // BLOCK
    groups = 2 * heads // (GROUP // HEAD)
    extra_at = first_own.shape[1] // BLOCK - 1
    extra = pl.BlockSpec((width, BLOCK), lambda g: (0, extra_at))
    shapes = (
        shaped((rows, BLOCK), f32),
        shaped((rows, STATE), bf16),
        shaped((rows, STATE), bf16),
        shaped((chunks, BLOCK, BLOCK), bf16),
        shaped((chunks, BLOCK, BLOCK), f32),
        shaped((chunks, BLOCK, BLOCK), f32),
        shaped((rows, BLOCK), f32),
        shaped((rows, BLOCK), f32),
        shaped((rows, BLOCK), f32),
        shaped((groups, 8, rows), f32),
        shaped((groups, 8, rows), f32),
        shaped((groups, 8, rows), f32),
        shaped((groups, 8, rows), f32),
    )
    return pl.pallas_call(
        functools.partial(prep_kernel, heads),
        grid=(1,),
        in_specs=[
            scalar, whole(normed.shape), extra, extra,
            whole(kernels.shape), whole(biases.shape), whole(rates.shape),
        ],
        out_specs=tuple(whole(o.shape) for o in shapes),
        out_shape=shapes,
        scratch_shapes=[pltpu.VMEM((rows + 8, BLOCK), f32), pltpu.VMEM((rows, BLOCK), f32)],
        compiler_params=params(),
        cost_estimate=cost(4),
        name="prep",
    )(rank, normed, first_own, first_other, kernels, biases, rates)


def front_kernel(tokens, rescale, normed, normed_t, inverse_out):
    width = tokens.shape[1]

    def body(c, carry):
        rows = chunk(c)
        tok = tokens[rows].astype(f32)
        inverse = lax.rsqrt(jnp.sum(tok * tok, axis=1, keepdims=True) / width + epsilon)
        scaled = tok * inverse * rescale[...]
        normed[rows] = scaled.astype(bf16)
        inverse_out[rows] = jnp.broadcast_to(inverse, (BLOCK, BLOCK))
        for k in range(width // BLOCK):
            normed_t[chunk(k), rows] = scaled[:, chunk(k)].T.astype(bf16)
        return carry

    each_chunk(tokens.shape[0] // BLOCK, body, 0)


def front(tokens, rescale):
    rows, width = tokens.shape
    vmem = pl.BlockSpec(memory_space=pltpu.VMEM)
    return pl.pallas_call(
        front_kernel,
        in_specs=[vmem, vmem],
        out_specs=(vmem, vmem, vmem),
        out_shape=(
            shaped((rows, width), bf16), shaped((width, rows), bf16), shaped((rows, BLOCK), f32)
        ),
        compiler_params=params(),
        cost_estimate=cost(5),
        name="front",
    )(tokens, rescale.reshape(1, width))


def mask_kernel(length, cotangent, masked, masked_t):
    width = cotangent.shape[1]

    def body(c, carry):
        rows = chunk(c)
        inside = (c * BLOCK + iota((BLOCK, width), 0)) < length[0]
        kept = jnp.where(inside, cotangent[rows].astype(f32), 0.0)
        masked[rows] = kept.astype(bf16)
        for k in range(width // BLOCK):
            masked_t[chunk(k), rows] = kept[:, chunk(k)].T.astype(bf16)
        return carry

    each_chunk(cotangent.shape[0] // BLOCK, body, 0)


def mask_rows(length, cotangent):
    rows, width = cotangent.shape
    vmem = pl.BlockSpec(memory_space=pltpu.VMEM)
    return pl.pallas_call(
        mask_kernel,
        in_specs=[scalar, vmem],
        out_specs=(vmem, vmem),
        out_shape=(shaped((rows, width), bf16), shaped((width, rows), bf16)),
        compiler_params=params(),
        cost_estimate=cost(5),
        name="mask_rows",
    )(length, cotangent)


def finish_kernel(
    heads, rank, normed_t, select_in, b_grad, c_grad, kernels, rates, decay_own, decay_other,
    direct_own, direct_other, slope_t, steps_t,
    select_grad, step_grad, extra_own, extra_other, kernels_grad, biases_grad, decays_grad,
    padded, grad_s, tall,
):
    rows = select_in.shape[0]
    chunks = rows // BLOCK
    half = decay_own.shape[0]
    padded[0:8] = jnp.zeros((8, BLOCK), f32)
    padded[8:] = select_in[...]
    grad_s[rows : rows + 8] = jnp.zeros((8, BLOCK), f32)

    def back(c, carry):
        here = chunk(c)
        pre = conv_taps(padded, c, kernels)
        sig = sigmoid(pre)
        grad = jnp.concatenate((b_grad[here], c_grad[here]), axis=1)
        grad = grad * (sig * (1.0 + pre * (1.0 - sig)))
        grad_s[here] = grad
        return tuple(
            carry[k] + jnp.sum(grad * padded[chunk(c, 5 + k)], axis=0, keepdims=True)
            for k in range(4)
        )

    zero = jnp.zeros((1, BLOCK), f32)
    kernels_grad[...] = jnp.concatenate(each_chunk(chunks, back, (zero,) * 4), axis=0)

    def shift(c, carry):
        here = chunk(c)
        total = grad_s[here] * kernels[3:4]
        for ahead in range(1, 4):
            total = total + grad_s[chunk(c, ahead)] * kernels[3 - ahead : 4 - ahead]
        select_grad[here] = total.astype(bf16)
        return carry

    each_chunk(chunks, shift, 0)

    for g in range(2 * half):
        decay = decay_own if g < half else decay_other
        direct = direct_own if g < half else direct_other
        k = g % half
        sum_step = jnp.zeros((8, BLOCK), f32)
        sum_decay = jnp.zeros((8, BLOCK), f32)
        rate = rates[g]
        for c in range(chunks):
            tile = slice(8 * c, 8 * c + 8)
            here = chunk(c)
            valid = iota((8, BLOCK), 0) < GROUP // HEAD
            fall = jnp.where(valid, decay[k, tile], 0.0)
            slope = jnp.where(valid, slope_t[g, :, here], 0.0)
            size = jnp.where(valid, steps_t[g, :, here], 0.0)
            step = (direct[k, tile] - rate * fall) * slope
            tall[8 * g : 8 * g + 8, here] = step
            sum_step = sum_step + step
            sum_decay = sum_decay - rate * size * fall
        biases_grad[g] = sum_step
        decays_grad[g] = sum_decay
    step_grad[...] = tall[...].astype(bf16)
    selector_part = dot(normed_t[...], select_grad[...])
    steps_part = dot_nt(normed_t[...], step_grad[...])
    lane = iota(selector_part.shape, 1)
    turned = pltpu.roll(selector_part, STATE, 1)
    first = jnp.where(rank[0] == 0, selector_part, turned)
    second = jnp.where(rank[0] == 0, turned, selector_part)
    width = 8 * half
    blank = jnp.zeros((selector_part.shape[0], BLOCK - 2 * width), f32)
    wide = jnp.concatenate((steps_part, blank), axis=1)
    extra_own[...] = jnp.where(
        lane < STATE, first, jnp.where(lane < STATE + width, pltpu.roll(wide, STATE, 1), 0.0)
    )
    extra_other[...] = jnp.where(
        lane < STATE,
        second,
        jnp.where(lane < STATE + width, pltpu.roll(wide, STATE - width, 1), 0.0),
    ).astype(bf16)


def finish(rank, normed_t, prep, b_grad, c_grad, kernels, rates, deep, heads):
    width, rows = normed_t.shape
    groups = prep[11].shape[0]
    vmem = pl.BlockSpec(memory_space=pltpu.VMEM)
    shapes = (
        shaped((rows, BLOCK), bf16),
        shaped((8 * groups, rows), bf16),
        shaped((width, BLOCK), f32),
        shaped((width, BLOCK), bf16),
        shaped(kernels.shape, f32),
        shaped((groups, 8, BLOCK), f32),
        shaped((groups, 8, BLOCK), f32),
    )
    per = GROUP // HEAD
    rate_tiles = jnp.broadcast_to(
        jnp.pad(rates.reshape(groups, per), ((0, 0), (0, 8 - per)))[:, :, None], (groups, 8, BLOCK)
    )
    return pl.pallas_call(
        functools.partial(finish_kernel, heads),
        in_specs=[scalar] + [vmem] * 12,
        out_specs=(vmem,) * len(shapes),
        out_shape=shapes,
        scratch_shapes=[
            pltpu.VMEM((rows + 8, BLOCK), f32),
            pltpu.VMEM((rows + 8, BLOCK), f32),
            pltpu.VMEM((8 * groups, rows), f32),
        ],
        compiler_params=params(),
        cost_estimate=cost(5),
        name="finish",
    )(
        rank, normed_t, prep[0], b_grad, c_grad, kernels, rate_tiles, deep[0][3], deep[1][3],
        deep[0][4], deep[1][4], prep[12], prep[11],
    )


def mix_forward(half, length, normed, content, filters, shortcut, prep, inner):
    (_, _, c_rows, select_t, gram, _, ends, starts, steps, ends_t, starts_t, _, _) = prep
    rows, width = normed.shape
    chunks = rows // BLOCK
    grid = inner // GROUP
    wide = GROUP // HEAD * BLOCK
    return pl.pallas_call(
        functools.partial(mix_kernel, half),
        grid=(grid,),
        in_specs=[
            scalar, whole(normed.shape), columns(width), columns(4), columns(1),
            whole(c_rows.shape), whole(select_t.shape), whole(gram.shape),
            whole(ends.shape), whole(starts.shape), whole(steps.shape),
            turned(half * grid, rows), turned(half * grid, rows),
        ],
        out_specs=(
            columns(rows), columns(rows), columns(rows),
            planes((chunks, STATE, GROUP)), planes((chunks, STATE, GROUP)),
        ),
        out_shape=(
            shaped((rows, inner), bf16),
            shaped((rows, inner), bf16),
            shaped((rows, inner), bf16),
            shaped((chunks, STATE, inner), bf16),
            shaped((chunks, STATE, inner), bf16),
        ),
        scratch_shapes=[
            pltpu.VMEM((rows, wide), f32),
            pltpu.VMEM((rows, wide), f32),
            pltpu.VMEM((rows + 8, GROUP), f32),
            pltpu.VMEM((rows, GROUP), f32),
            pltpu.VMEM((chunks, STATE, GROUP), f32),
            pltpu.VMEM((chunks, STATE, GROUP), f32),
            pltpu.VMEM((chunks, 8, GROUP), f32),
        ],
        compiler_params=params(),
        cost_estimate=cost(14),
        name="mix",
    )(length, normed, content, filters, shortcut, c_rows, select_t, gram, ends, starts, steps, ends_t, starts_t)


def gate_forward(length, normed, weights, amplitude, mixed, carried, finals, inner_width):
    rows, width = normed.shape
    inner = mixed.shape[1]
    grid = inner // GROUP
    first = carried is None
    last = finals is not None
    ins = [length, normed, weights, weights, amplitude, mixed]
    specs = [scalar, whole(normed.shape), columns(width), columns(width, after=grid), columns(1), columns(rows)]
    if not first:
        ins += list(carried)
        specs += [whole(c.shape) for c in carried]
    outs = [shaped((rows, inner), f32)]
    out_specs = [columns(rows)]
    scratch = [pltpu.VMEM((rows, GROUP), bf16), pltpu.VMEM((rows, GROUP), f32)]
    if last:
        ins += list(finals)
        specs += [whole(c.shape) for c in finals]
        outs += [shaped((rows, BLOCK), f32), shaped((rows, BLOCK), f32), shaped((rows, width), bf16)]
        out_specs += [whole((rows, BLOCK)), whole((rows, BLOCK)), whole((rows, width))]
        scratch = [pltpu.VMEM((rows, BLOCK), f32), pltpu.VMEM((rows, width), f32)] + scratch
    else:
        outs += [shaped((rows, BLOCK), f32), shaped((rows, width), f32)]
        out_specs += [whole((rows, BLOCK)), whole((rows, width))]
    return pl.pallas_call(
        functools.partial(gate_kernel, first, last, inner_width),
        grid=(grid,),
        in_specs=specs,
        out_specs=tuple(out_specs),
        out_shape=tuple(outs),
        scratch_shapes=scratch,
        compiler_params=params(),
        cost_estimate=cost(7),
        name="gate",
    )(*ins)


def gate_backward(
    cotangent, cotangent_t, normed_t, weights, amplitude, mixed, gate_in, x_low, scale, cross
):
    rows, width = cotangent.shape
    inner = mixed.shape[1]
    return pl.pallas_call(
        gate_back_kernel,
        grid=(inner // GROUP,),
        in_specs=[
            whole(cotangent.shape), whole(cotangent_t.shape), whole(normed_t.shape),
            columns(width, after=inner // GROUP), columns(1), columns(rows), columns(rows),
            columns(rows), whole(scale.shape), whole(cross.shape),
        ],
        out_specs=(
            columns(rows), columns(rows), columns(width), columns(width), columns(1), columns(1),
        ),
        out_shape=(
            shaped((rows, inner), bf16),
            shaped((rows, inner), bf16),
            shaped((width, inner), bf16),
            shaped((width, inner), bf16),
            shaped((1, inner), f32),
            shaped((1, inner), f32),
        ),
        scratch_shapes=[pltpu.VMEM((rows, GROUP), bf16), pltpu.VMEM((rows, GROUP), f32)],
        compiler_params=params(),
        cost_estimate=cost(8),
        name="gate_back",
    )(cotangent, cotangent_t, normed_t, weights, amplitude, mixed, gate_in, x_low, scale, cross)


def mix_backward(half, length, normed_t, filters, shortcut, prep, mixed_grad, kept, carried, last):
    (_, b_rows, c_rows, select_t, _, gram_t, ends, starts, steps, ends_t, starts_t, _, _) = prep
    _, x_low, values, early, late = kept
    width, rows = normed_t.shape
    inner = x_low.shape[1]
    chunks = rows // BLOCK
    grid = inner // GROUP
    first = carried is None
    wide = GROUP // HEAD * BLOCK
    shared = (b_rows, c_rows, select_t, gram_t, ends, starts, steps, ends_t, starts_t)
    ins = [length, normed_t, filters, shortcut, *shared, mixed_grad, x_low, values, early, late]
    specs = [scalar, whole(normed_t.shape), columns(4), columns(1)]
    specs += [whole(s.shape) for s in shared[:-2]] + [turned(half * grid, rows)] * 2
    specs += [columns(rows)] * 3 + [planes((chunks, STATE, GROUP))] * 2
    if not first:
        ins += list(carried)
        specs += [whole(c.shape) for c in carried]
    tall = 8 * chunks
    return pl.pallas_call(
        functools.partial(mix_back_kernel, half, first, last),
        grid=(grid,),
        in_specs=specs,
        out_specs=(
            columns(rows), columns(width), columns(4), lead((tall, BLOCK)), lead((tall, BLOCK)),
            whole((chunks, BLOCK, BLOCK)), whole((rows, STATE)), whole((rows, STATE)),
        ),
        out_shape=(
            shaped((rows, inner), bf16),
            shaped((width, inner), bf16),
            shaped((4, inner), f32),
            shaped((grid, tall, BLOCK), f32),
            shaped((grid, tall, BLOCK), f32),
            shaped((chunks, BLOCK, BLOCK), f32),
            shaped((rows, STATE), f32),
            shaped((rows, STATE), f32),
        ),
        scratch_shapes=[
            pltpu.VMEM((rows, wide), f32),
            pltpu.VMEM((rows, wide), f32),
            pltpu.VMEM((rows, GROUP), f32),
            pltpu.VMEM((rows + 8, GROUP), f32),
            pltpu.VMEM((rows + 8, GROUP), f32),
            pltpu.VMEM((chunks, STATE, GROUP), f32),
            pltpu.VMEM((chunks, STATE, GROUP), f32),
            pltpu.VMEM((chunks, 8, GROUP), f32),
            pltpu.VMEM((chunks, STATE, GROUP), bf16),
            pltpu.VMEM((chunks, STATE, GROUP), bf16),
            pltpu.VMEM((tall, BLOCK), f32),
            pltpu.VMEM((tall, BLOCK), f32),
            pltpu.VMEM((chunks, 8, GROUP), f32),
        ],
        compiler_params=params(),
        cost_estimate=cost(28),
        name="mix_back",
    )(*ins)


def shift_down(v, by):
    return jnp.pad(v, ((by, 0), (0, 0)))[: v.shape[0]]


def shift_up(v, by):
    return jnp.pad(v, ((0, by), (0, 0)))[by:]


def select_back(select_in, grad, kernels):
    taps = kernels.shape[0]
    shifted = [shift_down(select_in, taps - 1 - k) for k in range(taps)]
    pre = sum(shifted[k] * kernels[k] for k in range(taps))
    sig = sigmoid(pre)
    grad_pre = grad * (sig * (1.0 + pre * (1.0 - sig)))
    kernels_grad = jnp.stack([jnp.sum(grad_pre * shifted[k], axis=0) for k in range(taps)])
    select_grad = sum(shift_up(grad_pre, taps - 1 - k) * kernels[k] for k in range(taps))
    return select_grad, kernels_grad


def heads_to_rows(tall):
    grid, rows, tokens = tall.shape
    shaped_up = tall.reshape(grid, rows // 8, 8, tokens)[:, :, :4]
    return shaped_up.transpose(0, 2, 1, 3).reshape(grid * 4, (rows // 8) * tokens)


def place_kernel(count, places, *refs):
    parts, target = refs[:PLANE], refs[PLANE]
    for k in range(PLANE):
        for s in range(count):
            target[places[k * count + s]] = parts[k][s]


PLANE = 4
DP = ("column", "plane")


def pairs_by(size, by):
    return [(i, i ^ by) for i in range(size)]


def gather_column(local):
    count = lax.axis_size("column")
    others = [lax.ppermute(local, "column", pairs_by(count, s)) for s in range(1, count)]
    return jnp.stack([local] + others)


def gather_plane(column):
    return [column] + [
        lax.ppermute(column, "plane", pairs_by(PLANE, k)) for k in range(1, PLANE)
    ]


def place(parts):
    count, block, width = parts[0].shape
    high, low = lax.axis_index("column"), lax.axis_index("plane")
    places = jnp.stack([(high ^ s) * PLANE + (low ^ k) for k in range(PLANE) for s in range(count)])
    vmem = pl.BlockSpec(memory_space=pltpu.VMEM)
    placed = pl.pallas_call(
        functools.partial(place_kernel, count),
        in_specs=[scalar] + [vmem] * PLANE,
        out_specs=vmem,
        out_shape=shaped((PLANE * count, block, width), parts[0].dtype),
        compiler_params=params(),
        cost_estimate=cost(2),
        name="place",
    )(places.astype(jnp.int32), *parts)
    return placed.reshape(PLANE * count * block, width)


def block_of(blocks, index, axis):
    return lax.dynamic_index_in_dim(blocks, index, axis, keepdims=False)


def plane_send(v, by):
    return lax.ppermute(v, "plane", pairs_by(PLANE, by))


def start_sum(total):
    count = lax.axis_size("column")
    low = lax.axis_index("plane")
    rows, width = total.shape
    blocks = total.reshape(count, PLANE, rows // (count * PLANE), width)
    half = width // 2
    parts = (blocks[..., :half], blocks[..., half:])
    sent = []
    for part, near, far in ((parts[0], 1, 2), (parts[1], 2, 1)):
        away = jnp.stack((block_of(part, low ^ near, 1), block_of(part, low ^ 3, 1)))
        keep = jnp.stack((block_of(part, low, 1), block_of(part, low ^ far, 1)))
        sent.append((keep, plane_send(away, near)))
    return sent


def middle_sum(sent):
    moved = []
    for (keep, got), by in zip(sent, (2, 1)):
        both = (keep.astype(f32) + got.astype(f32)).astype(bf16)
        moved.append((both[0], plane_send(both[1], by)))
    return moved


def last_sum(moved):
    count = lax.axis_size("column")
    high = lax.axis_index("column")
    column = jnp.concatenate(
        [(keep.astype(f32) + got.astype(f32)).astype(bf16) for keep, got in moved], axis=-1
    )
    return [block_of(column, high, 0)] + [
        lax.ppermute(block_of(column, high ^ s, 0), "column", pairs_by(count, s))
        for s in range(1, count)
    ]


def finish_sum(terms):
    return tree_sum([t.astype(f32) for t in terms])


def tree_sum(terms):
    while len(terms) > 1:
        terms = [terms[k] + terms[k + 1] for k in range(0, len(terms), 2)]
    return terms[0]


def exchange(total):
    return lax.all_to_all(total, DP, 0, 0, tiled=True)


def sum_blocks(received, blocks):
    cut = received.reshape(blocks, received.shape[0] // blocks, received.shape[1])
    return jnp.sum(cut.astype(f32), axis=0)


def swap(v):
    return lax.ppermute(v, "tensor", [(0, 1), (1, 0)])


def pad_columns(v, width):
    return jnp.pad(v, ((0, 0), (0, width - v.shape[1])))


def tie(value, *others):
    return lax.optimization_barrier((value, *others))[0]


def on_device(
    layer_in,
    upstream,
    lengths,
    rescale,
    gating,
    content,
    selector,
    timestep,
    filters,
    kernels,
    biases,
    decays,
    shortcut,
    amplitude,
    outgoing,
):
    parts = lax.axis_size("tensor")
    rank = lax.axis_index("tensor")
    micro = lengths.shape[0]
    half_rows = layer_in.shape[0] // micro
    rows = half_rows * parts
    width = layer_in.shape[1]
    inner = gating.shape[1]
    heads = timestep.shape[1]
    state_cols = selector.shape[1]
    inner_width = inner * parts

    state_half = state_cols // parts
    own_select = lax.dynamic_slice_in_dim(selector, rank * state_half, state_half, 1)
    first_local = jnp.concatenate(
        (content, pad_columns(jnp.concatenate((own_select, timestep), axis=1), BLOCK)), axis=1
    )
    second_local = jnp.concatenate((gating, outgoing.T), axis=1)
    first_column = gather_column(first_local)
    second_own = lax.all_gather(second_local, DP, axis=0, tiled=True)

    def across(array):
        blocks = array.reshape(micro, half_rows, width)
        return lax.all_to_all(blocks, "tensor", 0, 0, tiled=True).reshape(rows, width)

    def outputs_of(array):
        mine = lax.dynamic_slice_in_dim(array, rank * half_rows, half_rows, 0)
        theirs = lax.dynamic_slice_in_dim(array, (1 - rank) * half_rows, half_rows, 0)
        return mine, swap(theirs)

    def join(mine, got):
        return jnp.where(
            rank == 0, jnp.concatenate((mine, got)), jnp.concatenate((got, mine))
        )

    tokens = across(layer_in)
    cotangent = across(upstream)
    length = lax.dynamic_slice_in_dim(lengths, rank, 1, 0)
    rank_1 = rank.reshape(1)

    flat = jnp.concatenate((filters.reshape(-1), amplitude, biases, decays, shortcut))
    flat_other = swap(flat)
    taps = filters.shape[0]

    def unpack(vector):
        edges = [0, taps * inner, (taps + 1) * inner]
        edges += [edges[-1] + heads * k for k in range(1, 4)]
        cut = [vector[a:b] for a, b in zip(edges[:-1], edges[1:])]
        return (cut[0].reshape(taps, inner), cut[1].reshape(1, inner), *cut[2:])

    filters_2, amplitude_2, biases_2, decays_2, shortcut_2 = zip(unpack(flat), unpack(flat_other))

    def head_lanes(pair):
        return pad_columns(jnp.concatenate(pair).reshape(1, -1), BLOCK)

    rates = jnp.exp(jnp.concatenate(decays_2))
    rate_lanes = pad_columns(rates.reshape(1, -1), BLOCK)
    shortcut_lanes = [jnp.repeat(s, HEAD).reshape(1, inner) for s in shortcut_2]
    normed, normed_t, inverse_wide = front(tokens, rescale)
    dbranch, dbranch_t = mask_rows(length, cotangent)
    first_column, normed = lax.optimization_barrier((first_column, normed))
    first_parts = gather_plane(first_column)
    first_parts[0] = tie(first_parts[0], dbranch)
    first_own = place(first_parts)
    first_other = swap(first_own)
    firsts = (first_own, first_other)
    prep = prepare(
        rank_1, normed, first_own, first_other, kernels, head_lanes(biases_2), rate_lanes, heads
    )
    kept = [None, None]
    kept[0] = mix_forward(
        0, length, normed, first_own, filters_2[0], shortcut_lanes[0], prep, inner
    )
    second_own = tie(second_own, kept[0][0])
    second_other = swap(second_own)
    seconds = (second_own, second_other)
    kept[1] = mix_forward(
        1, length, normed, tie(first_other, second_own), filters_2[1], shortcut_lanes[1], prep, inner
    )
    gate_own, squares, total = gate_forward(
        length, normed, seconds[0], amplitude_2[0], kept[0][0], None, None, inner_width
    )
    gate_other, scale, cross, layer_seq = gate_forward(
        length, normed, seconds[1], amplitude_2[1], kept[1][0], (squares, total),
        (tokens, dbranch), inner_width,
    )
    gates = (gate_own, gate_other)
    layer_pair = outputs_of(layer_seq)

    back = [None, None]
    for h in (1, 0):
        back[h] = gate_backward(
            dbranch, dbranch_t, normed_t, seconds[h], amplitude_2[h], kept[h][0], gates[h],
            kept[h][1], scale, cross,
        )
    second_grads = jnp.concatenate(
        [(back[0][k].astype(f32) + swap(back[1][k]).astype(f32)).astype(bf16) for k in (2, 3)],
        axis=1,
    )
    second_grads, later_grad = lax.optimization_barrier((second_grads, back[1][0]))
    second_sent = start_sum(second_grads)

    deep = [None, None]
    deep[1] = mix_backward(
        1, length, normed_t, filters_2[1], shortcut_lanes[1], prep, later_grad, kept[1], None, False
    )
    content_swapped = swap(deep[1][1])
    early_grad, *landed = lax.optimization_barrier((back[0][0], *[got for _, got in second_sent]))
    second_sent = [(keep, got) for (keep, _), got in zip(second_sent, landed)]
    second_sent[0] = (second_sent[0][0], tie(second_sent[0][1], deep[1][1]))
    second_moved = middle_sum(second_sent)
    deep[0] = mix_backward(
        0, length, normed_t, filters_2[0], shortcut_lanes[0], prep, early_grad, kept[0],
        deep[1][5:8], True,
    )
    content_own, *landed = lax.optimization_barrier((deep[0][1], *[got for _, got in second_moved]))
    second_moved = [(keep, got) for (keep, _), got in zip(second_moved, landed)]
    second_terms = last_sum(second_moved)

    (select_grad, step_rows, extra_own, extra_other, kernels_part, biases_tile, decays_tile) = finish(
        rank_1, normed_t, prep, deep[0][6], deep[0][7], kernels, rates, deep, heads
    )

    def compact(tiles):
        return jnp.sum(tiles[:, : GROUP // HEAD], axis=2).reshape(2 * heads)

    biases_part, decays_part = compact(biases_tile), compact(decays_tile)
    extra_sum = extra_own + swap(extra_other).astype(f32)
    content_sum = content_own.astype(f32) + content_swapped.astype(f32)
    first_grads = jnp.concatenate((content_sum, extra_sum), axis=1).astype(bf16)
    first_terms = last_sum(middle_sum(start_sum(first_grads)))

    spaced = 2 * heads
    select_2 = [first[:, inner : inner + state_half] for first in firsts]
    selector_full = jnp.where(
        rank == 0,
        jnp.concatenate(select_2, axis=1),
        jnp.concatenate(select_2[::-1], axis=1),
    )

    def space_heads(weights):
        per = GROUP // HEAD
        cut = weights[:, inner + state_half : inner + state_half + heads]
        cut = jnp.pad(cut.reshape(width, heads // per, per), ((0, 0), (0, 0), (0, 8 - per)))
        return cut.reshape(width, spaced)

    timestep_full = jnp.concatenate([space_heads(first) for first in firsts], axis=1)

    def weight_rows(weights, grads):
        return jnp.sum(weights.astype(f32) * grads.astype(f32), axis=1)

    extra_local = jnp.concatenate(
        (select_2[0], timestep_full[:, :spaced], select_2[1], timestep_full[:, spaced:]), axis=1
    )
    used_cols = state_half + spaced
    extra_part = jnp.concatenate(
        (extra_own[:, :used_cols], extra_other[:, :used_cols].astype(f32)), axis=1
    )
    scaled_rows = weight_rows(extra_local, extra_part)
    for h in range(2):
        scaled_rows = scaled_rows + weight_rows(firsts[h][:, :inner], tie(deep[h][1], content_own))
        scaled_rows = scaled_rows + weight_rows(
            seconds[h][:, :inner], tie(back[h][2], content_own)
        )
    rescale_part = scaled_rows / rescale

    grad_normed = dot_nt(select_grad, selector_full) + lax.dot_general(
        step_rows, timestep_full, (((0,), (1,)), ((), ())), preferred_element_type=f32
    )
    for h in range(2):
        grad_normed = grad_normed + dot_nt(tie(deep[h][0], content_own), firsts[h][:, :inner])
        grad_normed = grad_normed + dot_nt(tie(back[h][1], content_own), seconds[h][:, :inner])
    inverse = inverse_wide[:, :1]
    unit = tokens.astype(f32) * inverse
    weighted = grad_normed * rescale
    grad_seq = (
        dbranch.astype(f32)
        + inverse * weighted
        - unit * inverse * jnp.mean(weighted * unit, axis=-1, keepdims=True)
    ).astype(bf16)
    input_grad = join(*outputs_of(grad_seq))
    layer_out = join(*lax.optimization_barrier((*layer_pair, content_own))[:2])

    def per_head(row):
        return jnp.sum(row.reshape(heads, HEAD), axis=1)

    small_own, small_other = (
        jnp.concatenate(
            (
                deep[h][2].reshape(-1),
                back[h][4].reshape(-1),
                biases_part[h * heads : (h + 1) * heads],
                decays_part[h * heads : (h + 1) * heads],
                per_head(back[h][5]),
                rescale_part,
                kernels_part.reshape(-1),
            )
        )
        for h in range(2)
    )
    small = small_own + swap(small_other)
    used = small.shape[0]
    lines = -(-used // (8 * BLOCK)) * 8
    small = jnp.pad(small, (0, lines * BLOCK - used)).reshape(1, lines, BLOCK)
    blocks = lax.axis_size(DP)
    small_got = exchange(
        jnp.broadcast_to(small, (blocks, lines, BLOCK)).reshape(blocks * lines, BLOCK)
    )
    summed = sum_blocks(small_got, blocks).reshape(-1)
    cut = (taps + 1) * inner + 3 * heads
    filters_grad, amplitude_grad, biases_grad, decays_grad, shortcut_grad = unpack(summed[:cut])
    second_total = finish_sum(second_terms)
    first_total = finish_sum(first_terms)
    state_own = first_total[:, inner : inner + state_half]
    state_other = swap(state_own)
    selector_grad = jnp.where(
        rank == 0,
        jnp.concatenate((state_own, state_other), axis=1),
        jnp.concatenate((state_other, state_own), axis=1),
    )
    return (
        layer_out,
        input_grad,
        summed[cut : cut + width],
        second_total[:, :inner],
        first_total[:, :inner],
        selector_grad,
        first_total[:, inner + state_half : inner + state_half + spaced]
        .reshape(-1, spaced // 8, 8)[:, :, : GROUP // HEAD]
        .reshape(-1, heads),
        filters_grad,
        summed[cut + width : used].reshape(taps, state_cols),
        biases_grad,
        decays_grad,
        shortcut_grad,
        amplitude_grad.reshape(inner),
        second_total[:, inner:].T,
    )


def solution(mesh):
    devices = mesh.devices
    split = Mesh(
        devices.reshape(devices.shape[0] // PLANE, PLANE, devices.shape[1]), (*DP, "tensor")
    )
    return jax.shard_map(
        on_device,
        mesh=split,
        in_specs=(
            P((*DP, "tensor"), None),
            P((*DP, "tensor"), None),
            P(DP),
            P(),
            P(DP, "tensor"),
            P(DP, "tensor"),
            P(DP, None),
            P(DP, "tensor"),
            P(None, "tensor"),
            P(),
            P("tensor"),
            P("tensor"),
            P("tensor"),
            P("tensor"),
            P("tensor", DP),
        ),
        out_specs=(
            P((*DP, "tensor"), None),
            P((*DP, "tensor"), None),
            P(),
            P(DP, "tensor"),
            P(DP, "tensor"),
            P(DP, None),
            P(DP, "tensor"),
            P(None, "tensor"),
            P(),
            P("tensor"),
            P("tensor"),
            P("tensor"),
            P("tensor"),
            P("tensor", DP),
        ),
        check_vma=False,
    )
```

```python
import functools

import jax
import jax.numpy as jnp
from jax import lax
from jax.experimental import pallas as pl
from jax.experimental.pallas import tpu as pltpu
from jax.sharding import Mesh
from jax.sharding import PartitionSpec as P

BLOCK = 128
HEAD = 64
STATE = 64
GROUP = 256
SLOTS = 8
LIM_prep = 60
LIM_mix = 60
LIM_gate = 60
LIM_gate_back = 60
LIM_mix_back = 60
LIM_finish = 60
LIM_back = 60
LIM_front = 60
LIM_mask_rows = 60
LIM_place = 60
LOG2E = 1.4426950408889634
epsilon = 1e-05
f32 = jnp.float32
bf16 = jnp.bfloat16
ANY = pl.ANY


def dot(a, b):
    return lax.dot_general(a, b, (((1,), (0,)), ((), ())), preferred_element_type=f32)


def dot_nt(a, b):
    return lax.dot_general(a, b, (((1,), (1,)), ((), ())), preferred_element_type=f32)


def dot_full(a, b):
    return lax.dot_general(
        a, b, (((1,), (0,)), ((), ())), preferred_element_type=f32, precision=lax.Precision.HIGHEST
    )


def iota(shape, axis):
    return lax.broadcasted_iota(jnp.int32, shape, axis)


def chunk(c, after=0):
    return slice(c * BLOCK + after, (c + 1) * BLOCK + after)


def each_chunk(chunks, body, carry):
    for c in range(chunks):
        carry = body(c, carry)
    return carry


def sigmoid(v):
    return 1.0 / (1.0 + jnp.exp(-v))


def conv_taps(padded, c, taps_ref):
    total = padded[chunk(c, 8)] * taps_ref[3:4]
    for back in range(1, 4):
        total = total + padded[chunk(c, 8 - back)] * taps_ref[3 - back : 4 - back]
    return total


def lane_low():
    return iota((BLOCK, 2 * HEAD), 1) < HEAD


def spread(block, column):
    index = jnp.full((BLOCK, BLOCK), column, jnp.int32)
    return jnp.take_along_axis(block, index, axis=1, mode="promise_in_bounds")


def spread_pair(block, column):
    index = column + iota((BLOCK, BLOCK), 1) // HEAD
    return jnp.take_along_axis(block, index, axis=1, mode="promise_in_bounds")


def pair_rows(piece, low):
    return jnp.concatenate(
        (jnp.where(low, piece, 0.0), jnp.where(low, 0.0, piece)), axis=0
    ).astype(bf16)


def prep_kernel(
    heads, rank, normed, extra_own, extra_other, kernels, biases, rates,
    select_in, b_rows, c_rows, select_t, gram, gram_t,
    ends, starts, steps, ends_t, starts_t, steps_t, slope_t, padded, logits_s,
):
    chunks = normed.shape[0] // BLOCK
    groups = ends_t.shape[0]
    down = iota((BLOCK, BLOCK), 0)
    across = iota((BLOCK, BLOCK), 1)
    tri = (down >= across).astype(f32)
    off = (down != across).astype(f32)
    padded[0:8] = jnp.zeros((8, BLOCK), f32)

    own = dot(normed[...], extra_own[...])
    other = dot(normed[...], extra_other[...])
    lane = iota(own.shape, 1)
    first = jnp.where(rank[0] == 0, own, other)
    second = jnp.where(rank[0] == 0, other, own)
    selected = jnp.where(lane < STATE, first, pltpu.roll(second, STATE, 1))
    select_in[...] = selected
    padded[8:] = selected
    logits_s[...] = jnp.where(
        lane < heads, pltpu.roll(own, BLOCK - STATE, 1), pltpu.roll(other, BLOCK - STATE + heads, 1)
    )

    def body(c, carry):
        rows = chunk(c)
        pre = conv_taps(padded, c, kernels)
        act = pre * sigmoid(pre)
        act_t = act.T.astype(bf16)
        act = act.astype(bf16)
        b_rows[rows] = act[:, :STATE]
        c_rows[rows] = act[:, STATE:]
        select_t[c] = act_t
        gram[c] = dot(act[:, STATE:], act_t[:STATE]) * off
        gram_t[c] = dot(act[:, :STATE], act_t[STATE:]) * off
        logits = logits_s[rows] + biases[...]
        small = jnp.exp(-jnp.abs(logits))
        whole = 1.0 + small
        log_part = jnp.where(
            whole == 1.0, small, jnp.log(whole) * (small / jnp.where(whole == 1.0, 1.0, whole - 1.0))
        )
        step = jnp.maximum(logits, 0.0) + log_part
        decay = -rates[...] * step
        inclusive = dot_full(tri, decay)
        end = inclusive * LOG2E
        start = (inclusive - decay) * LOG2E
        ends[rows] = end
        starts[rows] = start
        steps[rows] = step
        turned = ((ends_t, end), (starts_t, start), (steps_t, step), (slope_t, sigmoid(logits)))
        for target, value in turned:
            value_t = value.T
            for g in range(groups):
                target[g, :, rows] = value_t[g * SLOTS : (g + 1) * SLOTS]
        return carry

    each_chunk(chunks, body, 0)


def mix_kernel(
    half, length, normed, content, filters, shortcut, c_rows, select_t, gram,
    ends, starts, steps, ends_t, starts_t,
    mixed, x_low, values, early, late,
    ends_w, starts_w, padded, scaled, gain_e, gain_l, totals,
):
    base = (half * pl.num_programs(0) + pl.program_id(0)) * SLOTS
    chunks = normed.shape[0] // BLOCK
    pairs = GROUP // (2 * HEAD)
    padded[0:8] = jnp.zeros((8, GROUP), f32)
    block = dot(normed[...], content[...])
    padded[8:] = block
    values[...] = block.astype(bf16)

    def gains(c, carry):
        rows = chunk(c)
        pre = conv_taps(padded, c, filters)
        inside = (c * BLOCK + iota((BLOCK, GROUP), 0)) < length[0]
        act = jnp.where(inside, pre * sigmoid(pre), 0.0).astype(bf16)
        x_low[rows] = act
        low = lane_low()
        end_block = ends[rows]
        start_block = starts[rows]
        step_block = steps[rows]
        for p in range(pairs):
            lanes = slice(2 * HEAD * p, 2 * HEAD * (p + 1))
            ends_p = [spread(end_block, base + 2 * p + k) for k in range(2)]
            starts_p = [spread(start_block, base + 2 * p + k) for k in range(2)]
            for k in range(2):
                wide = slice(BLOCK * (2 * p + k), BLOCK * (2 * p + k + 1))
                ends_w[rows, wide] = ends_p[k]
                starts_w[rows, wide] = starts_p[k]
            end = jnp.where(low, *ends_p)
            start = jnp.where(low, *starts_p)
            step = spread_pair(step_block, base + 2 * p)
            total = end[BLOCK - 1 : BLOCK]
            xs = act[:, lanes].astype(f32) * step
            scaled[rows, lanes] = xs
            totals[c, :, lanes] = jnp.broadcast_to(total, (8, 2 * HEAD))
            both = jnp.concatenate((jnp.exp2(total - end) * xs, jnp.exp2(start) * xs), axis=1)
            gain = dot(select_t[c, :STATE], both.astype(bf16))
            gain_e[c, :, lanes] = gain[:, : 2 * HEAD]
            gain_l[c, :, lanes] = gain[:, 2 * HEAD :]
        return carry

    each_chunk(chunks, gains, 0)

    state = jnp.zeros((STATE, GROUP), f32)
    for c in range(chunks):
        early[c] = state.astype(bf16)
        state = jnp.exp2(totals[c, :1]) * state + gain_e[c]
    state = jnp.zeros((STATE, GROUP), f32)
    for c in reversed(range(chunks)):
        late[c] = state.astype(bf16)
        state = jnp.exp2(totals[c, :1]) * state + gain_l[c]

    def mix(c, carry):
        rows = chunk(c)
        low = lane_low()
        coupled = gram[c]
        for p in range(pairs):
            lanes = slice(2 * HEAD * p, 2 * HEAD * (p + 1))
            wides = [slice(BLOCK * (2 * p + k), BLOCK * (2 * p + k + 1)) for k in range(2)]
            ends_p = [ends_w[rows, w] for w in wides]
            starts_p = [starts_w[rows, w] for w in wides]
            coupling = []
            for k in range(2):
                end_row = ends_t[0, 2 * p + k : 2 * p + k + 1, rows]
                start_row = starts_t[0, 2 * p + k : 2 * p + k + 1, rows]
                power = jnp.exp2(jnp.minimum(ends_p[k] - end_row, start_row - starts_p[k]))
                coupling.append((coupled * power).astype(bf16))
            xs = scaled[rows, lanes]
            inner = dot(jnp.concatenate(coupling, axis=1), pair_rows(xs, low))
            states = jnp.concatenate((early[c, :, lanes], late[c, :, lanes]), axis=1)
            outer = dot(c_rows[rows], states)
            end = jnp.where(low, *ends_p)
            start = jnp.where(low, *starts_p)
            total = end[BLOCK - 1 : BLOCK]
            mixed[rows, lanes] = (
                inner
                + jnp.exp2(end) * outer[:, : 2 * HEAD]
                + jnp.exp2(total - start) * outer[:, 2 * HEAD :]
                + shortcut[:, lanes] * x_low[rows, lanes].astype(f32)
            ).astype(bf16)
        return carry

    each_chunk(chunks, mix, 0)


def add_products(target, grads, weights):
    @pl.when(pl.program_id(0) == 0)
    def _():
        target[...] = jnp.zeros(target.shape, f32)

    products = grads * weights[...].astype(f32)
    target[...] += products[:, :BLOCK] + products[:, BLOCK:]


def gate_kernel(
    inner_width,
    length, normed, normed_t, tokens, cotangent, cotangent_t,
    gating_own, gating_other, out_own, out_other, amplitude,
    mixed_own, mixed_other, x_own, x_other,
    mixed_grad_own, mixed_grad_other, gate_grad_own, gate_grad_other,
    gating_grad_own, gating_grad_other, out_grad_own, out_grad_other,
    amplitude_grad_own, amplitude_grad_other, shortcut_grad_own, shortcut_grad_other,
    layer_out, row_sums,
    squares, total, gates, scale_s, cross_s, gated_s, dgated_s, mixed_grad_s, gate_grad_s,
):
    chunks = normed.shape[0] // BLOCK
    step = pl.program_id(0)
    groups = pl.num_programs(0) // 2
    group = lax.rem(step, groups)
    own = group < groups // 2

    def pick(first, second):
        return jnp.where(own, first, second)

    @pl.when(step == 0)
    def _():
        squares[...] = jnp.zeros(squares.shape, f32)
        total[...] = jnp.zeros(total.shape, f32)
        row_sums[...] = jnp.zeros(row_sums.shape, f32)

    @pl.when(step < groups)
    def _():
        gates[group] = dot(normed[...], pick(gating_own[...], gating_other[...]))

        def body(c, carry):
            rows = chunk(c)
            gate = gates[group, rows]
            gated = pick(mixed_own[rows], mixed_other[rows]).astype(f32) * (gate * sigmoid(gate))
            square = gated * gated
            squares[rows] += square[:, : GROUP // 2] + square[:, GROUP // 2 :]
            gated_s[rows] = (gated * amplitude[...]).astype(bf16)
            return carry

        each_chunk(chunks, body, 0)
        total[...] += dot_nt(gated_s[...], pick(out_own[...], out_other[...]))

    @pl.when(step == groups - 1)
    def _():
        def finish(c, carry):
            rows = chunk(c)
            mean = jnp.sum(squares[rows], axis=1, keepdims=True) / inner_width
            scale = lax.rsqrt(mean + epsilon)
            inside = (c * BLOCK + iota((BLOCK, 1), 0)) < length[0]
            projected = total[rows]
            sum_out = tokens[rows].astype(f32) + scale * projected
            layer_out[rows] = jnp.where(inside, sum_out, 0.0).astype(bf16)
            inner = jnp.sum(cotangent[rows].astype(f32) * projected, axis=1, keepdims=True)
            cross = scale * scale * scale * inner / inner_width
            scale_s[rows] = jnp.broadcast_to(scale, (BLOCK, BLOCK))
            cross_s[rows] = jnp.broadcast_to(cross, (BLOCK, BLOCK))
            return carry

        each_chunk(chunks, finish, 0)

    @pl.when(step >= groups)
    def _():
        dgated_s[...] = dot(cotangent[...], pick(out_own[...], out_other[...]))

        def body(c, carry):
            amplitude_sum, shortcut_sum = carry
            rows = chunk(c)
            dgated = dgated_s[rows]
            gate = gates[group, rows]
            sig = sigmoid(gate)
            act = gate * sig
            slope = sig * (1.0 + gate * (1.0 - sig))
            y = pick(mixed_own[rows], mixed_other[rows]).astype(f32)
            x = pick(x_own[rows], x_other[rows]).astype(f32)
            gz = y * act
            scale = jnp.concatenate((scale_s[rows], scale_s[rows]), axis=1)
            cross = jnp.concatenate((cross_s[rows], cross_s[rows]), axis=1)
            unit = gz * scale
            gated_s[rows] = (unit * amplitude[...]).astype(bf16)
            dgz = scale * (amplitude[...] * dgated) - gz * cross
            gate_grad_s[rows] = (dgz * y * slope).astype(bf16)
            dmix = dgz * act
            mixed_grad_s[rows] = dmix.astype(bf16)
            amplitude_sum = amplitude_sum + jnp.sum(dgated * unit, axis=0, keepdims=True)
            shortcut_sum = shortcut_sum + jnp.sum(dmix * x, axis=0, keepdims=True)
            return amplitude_sum, shortcut_sum

        zero = jnp.zeros((1, GROUP), f32)
        amplitude_sum, shortcut_sum = each_chunk(chunks, body, (zero, zero))
        grads = dot(normed_t[...], gate_grad_s[...])
        products = grads * pick(gating_own[...], gating_other[...]).astype(f32)
        row_sums[...] += products[:, :BLOCK] + products[:, BLOCK:]
        gating = grads.astype(bf16)
        out = dot(cotangent_t[...], gated_s[...]).astype(bf16)

        @pl.when(own)
        def _():
            mixed_grad_own[...] = mixed_grad_s[...]
            gate_grad_own[...] = gate_grad_s[...]
            gating_grad_own[...] = gating
            out_grad_own[...] = out
            amplitude_grad_own[...] = amplitude_sum
            shortcut_grad_own[...] = shortcut_sum

        @pl.when(jnp.logical_not(own))
        def _():
            mixed_grad_other[...] = mixed_grad_s[...]
            gate_grad_other[...] = gate_grad_s[...]
            gating_grad_other[...] = gating
            out_grad_other[...] = out
            amplitude_grad_other[...] = amplitude_sum
            shortcut_grad_other[...] = shortcut_sum


def mix_back_kernel(half, first, last, *refs):
    refs = list(refs)
    (
        length, normed_t, content, filters, shortcut, b_rows, c_rows, select_t, gram_t,
        ends, starts, steps, ends_t, starts_t, mixed_grad, x_low, values, early, late,
    ) = refs[:19]
    refs = refs[19:]
    if not first:
        gram_in, b_in, c_in = refs[:3]
        refs = refs[3:]
    (
        values_grad, content_grad, filters_grad, decay_grad, direct_grad, gram_grad, b_grad, c_grad,
        row_sums,
        ends_w, starts_w, steps_w, padded, pre_grad, gain_e, gain_l, totals,
        early_grad, late_grad, sums, local_rows, through,
    ) = refs
    step_id = pl.program_id(0)
    base = (half * pl.num_programs(0) + step_id) * SLOTS
    rows_all = x_low.shape[0]
    chunks = rows_all // BLOCK
    pairs = GROUP // (2 * HEAD)

    @pl.when(step_id == 0)
    def _():
        if first:
            gram_grad[...] = jnp.zeros(gram_grad.shape, f32)
            b_grad[...] = jnp.zeros(b_grad.shape, f32)
            c_grad[...] = jnp.zeros(c_grad.shape, f32)
        else:
            gram_grad[...] = gram_in[...]
            b_grad[...] = b_in[...]
            c_grad[...] = c_in[...]

    padded[0:8] = jnp.zeros((8, GROUP), f32)
    padded[8:] = values[...].astype(f32)
    pre_grad[rows_all : rows_all + 8] = jnp.zeros((8, GROUP), f32)

    def gains(c, carry):
        rows = chunk(c)
        low = lane_low()
        end_block = ends[rows]
        start_block = starts[rows]
        step_block = steps[rows]
        for p in range(pairs):
            lanes = slice(2 * HEAD * p, 2 * HEAD * (p + 1))
            ends_p = [spread(end_block, base + 2 * p + k) for k in range(2)]
            starts_p = [spread(start_block, base + 2 * p + k) for k in range(2)]
            for k in range(2):
                wide = slice(BLOCK * (2 * p + k), BLOCK * (2 * p + k + 1))
                ends_w[rows, wide] = ends_p[k]
                starts_w[rows, wide] = starts_p[k]
            steps_w[rows, lanes] = spread_pair(step_block, base + 2 * p)
            end = jnp.where(low, *ends_p)
            start = jnp.where(low, *starts_p)
            total = end[BLOCK - 1 : BLOCK]
            totals[c, :, lanes] = jnp.broadcast_to(total, (8, 2 * HEAD))
            dy = mixed_grad[rows, lanes].astype(f32)
            both = jnp.concatenate((jnp.exp2(end) * dy, jnp.exp2(total - start) * dy), axis=1)
            gain = dot(select_t[c, STATE:], both.astype(bf16))
            gain_e[c, :, lanes] = gain[:, : 2 * HEAD]
            gain_l[c, :, lanes] = gain[:, 2 * HEAD :]
        return carry

    each_chunk(chunks, gains, 0)

    state = jnp.zeros((STATE, GROUP), f32)
    for c in reversed(range(chunks)):
        early_grad[c] = state.astype(bf16)
        kept = jnp.exp2(totals[c, :1]) * state
        through[c] = jnp.broadcast_to(
            jnp.sum(kept * early[c].astype(f32), axis=0, keepdims=True), (8, GROUP)
        )
        state = kept + gain_e[c]
    state = jnp.zeros((STATE, GROUP), f32)
    for c in range(chunks):
        late_grad[c] = state.astype(bf16)
        kept = jnp.exp2(totals[c, :1]) * state
        through[c] += jnp.broadcast_to(
            jnp.sum(kept * late[c].astype(f32), axis=0, keepdims=True), (8, GROUP)
        )
        state = kept + gain_l[c]

    down = iota((BLOCK, BLOCK), 0)
    across = iota((BLOCK, BLOCK), 1)

    def mix(c, carry):
        rows = chunk(c)
        low = lane_low()
        coupled = gram_t[c]
        gram_sum = gram_grad[c]
        b_sum = b_grad[rows]
        c_sum = c_grad[rows]
        row_id = iota((8, BLOCK), 0)
        lane_id = iota((8, BLOCK), 1)
        flow = jnp.zeros((8, BLOCK), f32)
        apart = jnp.zeros((16, BLOCK), f32)
        columns_sum = jnp.zeros((BLOCK, BLOCK), f32)
        below_rows = []
        above_rows = []
        for p in range(pairs):
            lanes = slice(2 * HEAD * p, 2 * HEAD * (p + 1))
            wides = [slice(BLOCK * (2 * p + k), BLOCK * (2 * p + k + 1)) for k in range(2)]
            ends_p = [ends_w[rows, w] for w in wides]
            starts_p = [starts_w[rows, w] for w in wides]
            end = jnp.where(low, *ends_p)
            start = jnp.where(low, *starts_p)
            total = end[BLOCK - 1 : BLOCK]
            step = steps_w[rows, lanes]
            x = x_low[rows, lanes].astype(f32)
            dy = mixed_grad[rows, lanes].astype(f32)
            xs = x * step
            dy_rows = pair_rows(dy, low)
            powers = []
            coupling = []
            for k in range(2):
                end_row = ends_t[0, 2 * p + k : 2 * p + k + 1, rows]
                start_row = starts_t[0, 2 * p + k : 2 * p + k + 1, rows]
                power = jnp.exp2(jnp.minimum(end_row - ends_p[k], starts_p[k] - start_row))
                powers.append(power)
                coupling.append(coupled * power)
            inner = dot(jnp.concatenate(coupling, axis=1).astype(bf16), dy_rows)
            pair_products = dot_nt(xs.astype(bf16), dy_rows)
            for k in range(2):
                product = pair_products[:, BLOCK * k : BLOCK * (k + 1)]
                gram_sum = gram_sum + product * powers[k]
                spread_log = product * coupling[k]
                below = jnp.where(down < across, spread_log, 0.0)
                above = spread_log - below
                below_rows.append(jnp.sum(below, axis=0, keepdims=True))
                above_rows.append(jnp.sum(above, axis=0, keepdims=True))
                below_cols = jnp.sum(below, axis=1, keepdims=True)
                above_cols = jnp.sum(above, axis=1, keepdims=True)
                lane = 2 * p + k
                columns_sum = jnp.where(across == lane, below_cols, columns_sum)
                columns_sum = jnp.where(across == lane + 8, above_cols, columns_sum)
            states = jnp.concatenate((early[c, :, lanes], late[c, :, lanes]), axis=1)
            states_grad = jnp.concatenate((early_grad[c, :, lanes], late_grad[c, :, lanes]), axis=1)
            raw_y = dot(c_rows[rows], states)
            raw_x = dot(b_rows[rows], states_grad)
            dy_both = jnp.concatenate((jnp.exp2(end) * dy, jnp.exp2(total - start) * dy), axis=1)
            weight_both = jnp.concatenate((jnp.exp2(total - end), jnp.exp2(start)), axis=1)
            xs_both = jnp.concatenate((xs, xs), axis=1) * weight_both
            outer_both = weight_both * raw_x
            c_sum = c_sum + dot_nt(dy_both.astype(bf16), states)
            b_sum = b_sum + dot_nt(xs_both.astype(bf16), states_grad)
            grad_xs = inner + outer_both[:, : 2 * HEAD] + outer_both[:, 2 * HEAD :]
            from_y = dy_both * raw_y
            from_x = xs_both * raw_x
            local = from_y[:, 2 * HEAD :] - from_x[:, 2 * HEAD :]
            moving = from_y[:, : 2 * HEAD] - from_x[:, : 2 * HEAD] - local
            passed = from_x[:, : 2 * HEAD] + from_y[:, 2 * HEAD :]
            through[c, :, lanes] += jnp.broadcast_to(
                jnp.sum(passed, axis=0, keepdims=True), (8, 2 * HEAD)
            )
            pick = (row_id == 2 * p + lane_id // HEAD).astype(f32)
            none = jnp.zeros((8, BLOCK), f32)
            pick_same = jnp.concatenate((pick, pick), axis=1).astype(bf16)
            pick_apart = jnp.concatenate(
                (
                    jnp.concatenate((pick, none), axis=1),
                    jnp.concatenate((none, pick), axis=1),
                ),
                axis=0,
            ).astype(bf16)
            high = moving.astype(bf16)
            rest = (moving - high.astype(f32)).astype(bf16)
            flow = flow + dot_nt(pick_same, jnp.concatenate((high, rest), axis=1))
            apart = apart + dot_nt(
                pick_apart, jnp.concatenate((local, x * grad_xs), axis=1).astype(bf16)
            )
            pre_grad[rows, lanes] = step * grad_xs + shortcut[:, lanes] * dy
        gram_grad[c] = gram_sum
        b_grad[rows] = b_sum
        c_grad[rows] = c_sum
        tile = slice(c * 8, c * 8 + 8)
        flat = columns_sum.T
        pad = jnp.zeros((4, BLOCK), f32)
        below_all = jnp.concatenate(below_rows + [pad], axis=0)
        above_all = jnp.concatenate(above_rows + [pad], axis=0)
        below_flat = flat[0:8]
        above_flat = flat[8:16]
        sums[tile] = flow + (below_all - below_flat) - (above_all - above_flat)
        local_rows[tile] = apart[:8] + (above_all - above_flat)
        direct_grad[0, tile] = apart[8:]
        return carry

    each_chunk(chunks, mix, 0)

    head_cols = (iota((GROUP, BLOCK), 0) // HEAD == iota((GROUP, BLOCK), 1)).astype(f32)
    tall = 8 * chunks
    through_tall = dot_full(through[...].reshape(tall, GROUP), head_cols)
    own = iota((tall, BLOCK), 1) == iota((tall, BLOCK), 0) % 8
    through_rows = jnp.sum(jnp.where(own, through_tall, 0.0), axis=1, keepdims=True)
    decay_grad[0] = (
        dot_full(sums[...], (down >= across).astype(f32)) + local_rows[...] + through_rows
    )

    def conv_back(c, carry):
        rows = chunk(c)
        pre = conv_taps(padded, c, filters)
        sig = sigmoid(pre)
        inside = (c * BLOCK + iota((BLOCK, GROUP), 0)) < length[0]
        grad = jnp.where(inside, pre_grad[rows] * (sig * (1.0 + pre * (1.0 - sig))), 0.0)
        pre_grad[rows] = grad
        return tuple(
            carry[k]
            + jnp.sum(grad * padded[chunk(c, 5 + k)], axis=0, keepdims=True)
            for k in range(4)
        )

    zero = jnp.zeros((1, GROUP), f32)
    filter_sums = each_chunk(chunks, conv_back, (zero,) * 4)
    filters_grad[...] = jnp.concatenate(filter_sums, axis=0)

    def conv_shift(c, carry):
        rows = chunk(c)
        total = pre_grad[rows] * filters[3:4]
        for ahead in range(1, 4):
            total = total + pre_grad[chunk(c, ahead)] * filters[3 - ahead : 4 - ahead]
        values_grad[rows] = total.astype(bf16)
        return carry

    each_chunk(chunks, conv_shift, 0)
    grads = dot(normed_t[...], values_grad[...])
    content_grad[...] = grads.astype(bf16)
    add_products(row_sums, grads, content)

    if last:

        @pl.when(step_id == pl.num_programs(0) - 1)
        def _():
            def finish(c, carry):
                rows = chunk(c)
                grad = jnp.where(down != across, gram_grad[c], 0.0)
                b_grad[rows] += dot(grad.astype(bf16), c_rows[rows])
                c_grad[rows] += dot(grad.T.astype(bf16), b_rows[rows])
                return carry

            each_chunk(chunks, finish, 0)


def whole(shape):
    return pl.BlockSpec(shape, lambda *_: (0,) * len(shape), pipeline_mode=pl.Buffered(1))


def columns(rows, width=GROUP, after=0):
    return pl.BlockSpec((rows, width), lambda g, *_: (0, g + after))


def planes(shape):
    return pl.BlockSpec(shape, lambda g, *_: (0,) * (len(shape) - 1) + (g,))


def turned(after, rows):
    return pl.BlockSpec((1, 8, rows), lambda g, *_: (g + after, 0, 0))


def lead(shape):
    return pl.BlockSpec((1,) + shape, lambda g, *_: (g,) + (0,) * len(shape))


scalar = pl.BlockSpec(memory_space=pltpu.SMEM)


def shaped(shape, dtype):
    return jax.ShapeDtypeStruct(shape, dtype)


def params(limit=60):
    return pltpu.CompilerParams(vmem_limit_bytes=limit << 20)


def cost(micros):
    return pl.CostEstimate(flops=0, bytes_accessed=int(micros * 3.0e6), transcendentals=0)


def prepare(rank, normed, first_own, first_other, kernels, biases, rates, heads):
    rows, width = normed.shape
    chunks = rows // BLOCK
    groups = 2 * heads // SLOTS
    extra_at = first_own.shape[1] // BLOCK - 1
    extra = pl.BlockSpec((width, BLOCK), lambda g: (0, extra_at))
    shapes = (
        shaped((rows, BLOCK), f32),
        shaped((rows, STATE), bf16),
        shaped((rows, STATE), bf16),
        shaped((chunks, BLOCK, BLOCK), bf16),
        shaped((chunks, BLOCK, BLOCK), f32),
        shaped((chunks, BLOCK, BLOCK), f32),
        shaped((rows, BLOCK), f32),
        shaped((rows, BLOCK), f32),
        shaped((rows, BLOCK), f32),
        shaped((groups, 8, rows), f32),
        shaped((groups, 8, rows), f32),
        shaped((groups, 8, rows), f32),
        shaped((groups, 8, rows), f32),
    )
    return pl.pallas_call(
        functools.partial(prep_kernel, heads),
        grid=(1,),
        in_specs=[
            scalar, whole(normed.shape), extra, extra,
            whole(kernels.shape), whole(biases.shape), whole(rates.shape),
        ],
        out_specs=tuple(whole(o.shape) for o in shapes),
        out_shape=shapes,
        scratch_shapes=[pltpu.VMEM((rows + 8, BLOCK), f32), pltpu.VMEM((rows, BLOCK), f32)],
        compiler_params=params(LIM_prep),
        cost_estimate=cost(4),
        name="prep",
    )(rank, normed, first_own, first_other, kernels, biases, rates)


def front_kernel(tokens, rescale, normed, normed_t, inverse_out):
    width = tokens.shape[1]

    def body(c, carry):
        rows = chunk(c)
        tok = tokens[rows].astype(f32)
        inverse = lax.rsqrt(jnp.sum(tok * tok, axis=1, keepdims=True) / width + epsilon)
        scaled = tok * inverse * rescale[...]
        normed[rows] = scaled.astype(bf16)
        inverse_out[rows] = jnp.broadcast_to(inverse, (BLOCK, BLOCK))
        for k in range(width // BLOCK):
            normed_t[chunk(k), rows] = scaled[:, chunk(k)].T.astype(bf16)
        return carry

    each_chunk(tokens.shape[0] // BLOCK, body, 0)


def front(tokens, rescale):
    rows, width = tokens.shape
    vmem = pl.BlockSpec(memory_space=pltpu.VMEM)
    return pl.pallas_call(
        front_kernel,
        in_specs=[vmem, vmem],
        out_specs=(vmem, vmem, vmem),
        out_shape=(
            shaped((rows, width), bf16), shaped((width, rows), bf16), shaped((rows, BLOCK), f32)
        ),
        compiler_params=params(LIM_front),
        cost_estimate=cost(5),
        name="front",
    )(tokens, rescale.reshape(1, width))


def mask_kernel(length, cotangent, masked, masked_t):
    width = cotangent.shape[1]

    def body(c, carry):
        rows = chunk(c)
        inside = (c * BLOCK + iota((BLOCK, width), 0)) < length[0]
        kept = jnp.where(inside, cotangent[rows].astype(f32), 0.0)
        masked[rows] = kept.astype(bf16)
        for k in range(width // BLOCK):
            masked_t[chunk(k), rows] = kept[:, chunk(k)].T.astype(bf16)
        return carry

    each_chunk(cotangent.shape[0] // BLOCK, body, 0)


def mask_rows(length, cotangent):
    rows, width = cotangent.shape
    vmem = pl.BlockSpec(memory_space=pltpu.VMEM)
    return pl.pallas_call(
        mask_kernel,
        in_specs=[scalar, vmem],
        out_specs=(vmem, vmem),
        out_shape=(shaped((rows, width), bf16), shaped((width, rows), bf16)),
        compiler_params=params(LIM_mask_rows),
        cost_estimate=cost(5),
        name="mask_rows",
    )(length, cotangent)


def finish_kernel(
    rank, normed_t, weights_own, weights_other, select_in, b_grad, c_grad, kernels, rates,
    decay_own, decay_other, direct_own, direct_other, slope_t, steps_t, sums_0, sums_1, sums_2,
    grad_own, grad_other, extra_own, extra_other, kernels_grad, biases_grad, decays_grad, row_sums,
    padded, grad_s,
):
    rows = select_in.shape[0]
    chunks = rows // BLOCK
    half = decay_own.shape[0]
    padded[0:8] = jnp.zeros((8, BLOCK), f32)
    padded[8:] = select_in[...]
    grad_s[rows : rows + 8] = jnp.zeros((8, BLOCK), f32)

    def back(c, carry):
        here = chunk(c)
        pre = conv_taps(padded, c, kernels)
        sig = sigmoid(pre)
        grad = jnp.concatenate((b_grad[here], c_grad[here]), axis=1)
        grad = grad * (sig * (1.0 + pre * (1.0 - sig)))
        grad_s[here] = grad
        return tuple(
            carry[k] + jnp.sum(grad * padded[chunk(c, 5 + k)], axis=0, keepdims=True)
            for k in range(4)
        )

    zero = jnp.zeros((1, BLOCK), f32)
    kernels_grad[...] = jnp.concatenate(each_chunk(chunks, back, (zero,) * 4), axis=0)
    lane = iota((BLOCK, BLOCK), 1)
    used = SLOTS * half

    def turn(c, carry):
        here = chunk(c)
        total = grad_s[here] * kernels[3:4]
        for ahead in range(1, 4):
            total = total + grad_s[chunk(c, ahead)] * kernels[3 - ahead : 4 - ahead]
        tile = slice(SLOTS * c, SLOTS * (c + 1))
        tiles = []
        sums = []
        valid = iota((SLOTS, BLOCK), 0) < GROUP // HEAD
        for g in range(2 * half):
            decay = decay_own if g < half else decay_other
            direct = direct_own if g < half else direct_other
            fall = jnp.where(valid, decay[g % half, tile], 0.0)
            slope = jnp.where(valid, slope_t[g, :, here], 0.0)
            step = (direct[g % half, tile] - rates[g] * fall) * slope
            tiles.append(step)
            sums.append((step, rates[g] * steps_t[g, :, here] * fall))
        blank = jnp.zeros((BLOCK - 2 * used, BLOCK), f32)
        steps = jnp.concatenate(tiles + [blank], axis=0).T
        turned = pltpu.roll(total, STATE, 1)
        first = jnp.where(rank[0] == 0, total, turned)
        second = jnp.where(rank[0] == 0, turned, total)
        keep = lane < STATE + used
        grad_own[here] = jnp.where(
            lane < STATE, first, jnp.where(keep, pltpu.roll(steps, STATE, 1), 0.0)
        ).astype(bf16)
        grad_other[here] = jnp.where(
            lane < STATE, second, jnp.where(keep, pltpu.roll(steps, STATE - used, 1), 0.0)
        ).astype(bf16)
        return [(a + x, b - y) for (a, b), (x, y) in zip(carry, sums)]

    empty = jnp.zeros((SLOTS, BLOCK), f32)
    sums = each_chunk(chunks, turn, [(empty, empty)] * (2 * half))
    for g in range(2 * half):
        biases_grad[g] = sums[g][0]
        decays_grad[g] = sums[g][1]
    own = dot(normed_t[...], grad_own[...])
    other = dot(normed_t[...], grad_other[...])
    extra_own[...] = own
    extra_other[...] = other.astype(bf16)
    row_sums[...] = (
        own * weights_own[...].astype(f32)
        + other * weights_other[...].astype(f32)
        + (sums_0[...] + sums_1[...] + sums_2[...])
    )


def extra_columns(weights):
    at = weights.shape[1] // BLOCK - 1
    return pl.BlockSpec((weights.shape[0], BLOCK), lambda *_: (0, at))


def finish(rank, normed_t, firsts, prep, b_grad, c_grad, kernels, rate_tiles, deep, row_sums):
    width, rows = normed_t.shape
    groups = prep[11].shape[0]
    shapes = (
        shaped((rows, BLOCK), bf16),
        shaped((rows, BLOCK), bf16),
        shaped((width, BLOCK), f32),
        shaped((width, BLOCK), bf16),
        shaped(kernels.shape, f32),
        shaped((groups, SLOTS, BLOCK), f32),
        shaped((groups, SLOTS, BLOCK), f32),
        shaped((width, BLOCK), f32),
    )
    rest = (
        prep[0], b_grad, c_grad, kernels, rate_tiles, deep[0][3], deep[1][3], deep[0][4], deep[1][4],
        prep[12], prep[11], *row_sums,
    )
    return pl.pallas_call(
        finish_kernel,
        grid=(1,),
        in_specs=[scalar, whole(normed_t.shape)]
        + [extra_columns(w) for w in firsts]
        + [whole(r.shape) for r in rest],
        out_specs=tuple(whole(o.shape) for o in shapes),
        out_shape=shapes,
        scratch_shapes=[pltpu.VMEM((rows + 8, BLOCK), f32), pltpu.VMEM((rows + 8, BLOCK), f32)],
        compiler_params=params(LIM_finish),
        cost_estimate=cost(6),
        name="finish",
    )(rank, normed_t, *firsts, *rest)


def back_kernel(
    values_own, values_other, gate_own, gate_other, content_own, content_other, gating_own,
    gating_other, extra_own, extra_other, weights_own, weights_other, tokens, inverse_in, rescale,
    cotangent, grad_out, total,
):
    step = pl.program_id(0)

    def products():
        return (
            dot_nt(values_own[...], content_own[...])
            + dot_nt(values_other[...], content_other[...])
            + dot_nt(gate_own[...], gating_own[...])
            + dot_nt(gate_other[...], gating_other[...])
        )

    @pl.when(step == 0)
    def _():
        total[...] = (
            products()
            + dot_nt(extra_own[...], weights_own[...])
            + dot_nt(extra_other[...], weights_other[...])
        )

    @pl.when(step > 0)
    def _():
        total[...] += products()

    @pl.when(step == pl.num_programs(0) - 1)
    def _():
        width = tokens.shape[1]

        def body(c, carry):
            rows = chunk(c)
            inverse = inverse_in[rows, :1]
            unit = tokens[rows].astype(f32) * inverse
            weighted = total[rows] * rescale[...]
            mean = jnp.sum(weighted * unit, axis=1, keepdims=True) / width
            grad = cotangent[rows].astype(f32) + inverse * (weighted - unit * mean)
            grad_out[rows] = grad.astype(bf16)
            return carry

        each_chunk(tokens.shape[0] // BLOCK, body, 0)


def backward_rows(deep, back, firsts, seconds, extras, tokens, inverse_wide, rescale, cotangent):
    rows, width = tokens.shape
    inner = deep[0][0].shape[1]
    fixed = (tokens, inverse_wide, rescale.reshape(1, width), cotangent)
    return pl.pallas_call(
        back_kernel,
        grid=(inner // GROUP,),
        in_specs=[columns(rows)] * 4
        + [columns(width)] * 4
        + [whole((rows, BLOCK))] * 2
        + [extra_columns(w) for w in firsts]
        + [whole(f.shape) for f in fixed],
        out_specs=whole((rows, width)),
        out_shape=shaped((rows, width), bf16),
        scratch_shapes=[pltpu.VMEM((rows, width), f32)],
        compiler_params=params(LIM_back),
        cost_estimate=cost(14),
        name="back",
    )(
        deep[0][0], deep[1][0], back[0][1], back[1][1], *firsts, *seconds, *extras, *firsts, *fixed
    )


def mix_forward(half, length, normed, content, filters, shortcut, prep, inner):
    (_, _, c_rows, select_t, gram, _, ends, starts, steps, ends_t, starts_t, _, _) = prep
    rows, width = normed.shape
    chunks = rows // BLOCK
    grid = inner // GROUP
    wide = GROUP // HEAD * BLOCK
    return pl.pallas_call(
        functools.partial(mix_kernel, half),
        grid=(grid,),
        in_specs=[
            scalar, whole(normed.shape), columns(width), columns(4), columns(1),
            whole(c_rows.shape), whole(select_t.shape), whole(gram.shape),
            whole(ends.shape), whole(starts.shape), whole(steps.shape),
            turned(half * grid, rows), turned(half * grid, rows),
        ],
        out_specs=(
            columns(rows), columns(rows), columns(rows),
            planes((chunks, STATE, GROUP)), planes((chunks, STATE, GROUP)),
        ),
        out_shape=(
            shaped((rows, inner), bf16),
            shaped((rows, inner), bf16),
            shaped((rows, inner), bf16),
            shaped((chunks, STATE, inner), bf16),
            shaped((chunks, STATE, inner), bf16),
        ),
        scratch_shapes=[
            pltpu.VMEM((rows, wide), f32),
            pltpu.VMEM((rows, wide), f32),
            pltpu.VMEM((rows + 8, GROUP), f32),
            pltpu.VMEM((rows, GROUP), f32),
            pltpu.VMEM((chunks, STATE, GROUP), f32),
            pltpu.VMEM((chunks, STATE, GROUP), f32),
            pltpu.VMEM((chunks, 8, GROUP), f32),
        ],
        compiler_params=params(LIM_mix),
        cost_estimate=cost(14),
        name="mix",
    )(length, normed, content, filters, shortcut, c_rows, select_t, gram, ends, starts, steps, ends_t, starts_t)


def gate_both(length, normed, normed_t, tokens, cotangent, cotangent_t, seconds, amplitude, kept, inner_width):
    rows, width = normed.shape
    inner = kept[0][0].shape[1]
    half = inner // GROUP
    groups = 2 * half

    def read(h):
        def at(g):
            k = g % groups
            return jnp.minimum(k, half - 1) if h == 0 else jnp.maximum(k - half, 0)

        return at

    def write(h):
        return lambda g: jnp.clip(g - groups - h * half, 0, half - 1)

    def blocks(height, at, after=0):
        return pl.BlockSpec((height, GROUP), lambda g: (0, at(g) + after))

    fixed = (normed, normed_t, tokens, cotangent, cotangent_t)
    ins = [length, *fixed, *seconds, *seconds, amplitude]
    ins += [kept[0][0], kept[1][0], kept[0][1], kept[1][1]]
    specs = [scalar] + [whole(f.shape) for f in fixed]
    specs += [blocks(width, read(h)) for h in range(2)]
    specs += [blocks(width, read(h), half) for h in range(2)]
    specs += [pl.BlockSpec((1, GROUP), lambda g: (0, g % groups))]
    specs += [blocks(rows, read(h)) for h in range(2)] * 2
    heights = (rows, rows, width, width, 1, 1)
    kinds = (bf16, bf16, bf16, bf16, f32, f32)
    outs = [shaped((n, inner), k) for n, k in zip(heights, kinds) for _ in range(2)]
    out_specs = [blocks(n, write(h)) for n in heights for h in range(2)]
    outs += [shaped((rows, width), bf16), shaped((width, BLOCK), f32)]
    out_specs += [whole((rows, width)), whole((width, BLOCK))]
    got = pl.pallas_call(
        functools.partial(gate_kernel, inner_width),
        grid=(2 * groups,),
        in_specs=specs,
        out_specs=tuple(out_specs),
        out_shape=tuple(outs),
        scratch_shapes=[
            pltpu.VMEM((rows, BLOCK), f32),
            pltpu.VMEM((rows, width), f32),
            pltpu.VMEM((groups, rows, GROUP), f32),
            pltpu.VMEM((rows, BLOCK), f32),
            pltpu.VMEM((rows, BLOCK), f32),
            pltpu.VMEM((rows, GROUP), bf16),
            pltpu.VMEM((rows, GROUP), f32),
            pltpu.VMEM((rows, GROUP), bf16),
            pltpu.VMEM((rows, GROUP), bf16),
        ],
        compiler_params=params(LIM_gate),
        cost_estimate=cost(35),
        name="gate",
    )(*ins)
    return [got[h:12:2] for h in range(2)], got[12], got[13]


def mix_backward(half, length, normed_t, weights, filters, shortcut, prep, mixed_grad, kept, carried, last):
    (_, b_rows, c_rows, select_t, _, gram_t, ends, starts, steps, ends_t, starts_t, _, _) = prep
    _, x_low, values, early, late = kept
    width, rows = normed_t.shape
    inner = x_low.shape[1]
    chunks = rows // BLOCK
    grid = inner // GROUP
    first = carried is None
    wide = GROUP // HEAD * BLOCK
    shared = (b_rows, c_rows, select_t, gram_t, ends, starts, steps, ends_t, starts_t)
    ins = [length, normed_t, weights, filters, shortcut, *shared]
    ins += [mixed_grad, x_low, values, early, late]
    specs = [scalar, whole(normed_t.shape), columns(width), columns(4), columns(1)]
    specs += [whole(s.shape) for s in shared[:-2]] + [turned(half * grid, rows)] * 2
    specs += [columns(rows)] * 3 + [planes((chunks, STATE, GROUP))] * 2
    if not first:
        ins += list(carried)
        specs += [whole(c.shape) for c in carried]
    tall = 8 * chunks
    return pl.pallas_call(
        functools.partial(mix_back_kernel, half, first, last),
        grid=(grid,),
        in_specs=specs,
        out_specs=(
            columns(rows), columns(width), columns(4), lead((tall, BLOCK)), lead((tall, BLOCK)),
            whole((chunks, BLOCK, BLOCK)), whole((rows, STATE)), whole((rows, STATE)),
            whole((width, BLOCK)),
        ),
        out_shape=(
            shaped((rows, inner), bf16),
            shaped((width, inner), bf16),
            shaped((4, inner), f32),
            shaped((grid, tall, BLOCK), f32),
            shaped((grid, tall, BLOCK), f32),
            shaped((chunks, BLOCK, BLOCK), f32),
            shaped((rows, STATE), f32),
            shaped((rows, STATE), f32),
            shaped((width, BLOCK), f32),
        ),
        scratch_shapes=[
            pltpu.VMEM((rows, wide), f32),
            pltpu.VMEM((rows, wide), f32),
            pltpu.VMEM((rows, GROUP), f32),
            pltpu.VMEM((rows + 8, GROUP), f32),
            pltpu.VMEM((rows + 8, GROUP), f32),
            pltpu.VMEM((chunks, STATE, GROUP), f32),
            pltpu.VMEM((chunks, STATE, GROUP), f32),
            pltpu.VMEM((chunks, 8, GROUP), f32),
            pltpu.VMEM((chunks, STATE, GROUP), bf16),
            pltpu.VMEM((chunks, STATE, GROUP), bf16),
            pltpu.VMEM((tall, BLOCK), f32),
            pltpu.VMEM((tall, BLOCK), f32),
            pltpu.VMEM((chunks, 8, GROUP), f32),
        ],
        compiler_params=params(LIM_mix_back),
        cost_estimate=cost(28),
        name="mix_back",
    )(*ins)


def shift_down(v, by):
    return jnp.pad(v, ((by, 0), (0, 0)))[: v.shape[0]]


def shift_up(v, by):
    return jnp.pad(v, ((0, by), (0, 0)))[by:]


def select_back(select_in, grad, kernels):
    taps = kernels.shape[0]
    shifted = [shift_down(select_in, taps - 1 - k) for k in range(taps)]
    pre = sum(shifted[k] * kernels[k] for k in range(taps))
    sig = sigmoid(pre)
    grad_pre = grad * (sig * (1.0 + pre * (1.0 - sig)))
    kernels_grad = jnp.stack([jnp.sum(grad_pre * shifted[k], axis=0) for k in range(taps)])
    select_grad = sum(shift_up(grad_pre, taps - 1 - k) * kernels[k] for k in range(taps))
    return select_grad, kernels_grad


def heads_to_rows(tall):
    grid, rows, tokens = tall.shape
    shaped_up = tall.reshape(grid, rows // 8, 8, tokens)[:, :, :4]
    return shaped_up.transpose(0, 2, 1, 3).reshape(grid * 4, (rows // 8) * tokens)


def place_kernel(count, places, *refs):
    parts, target = refs[:PLANE], refs[PLANE]
    for k in range(PLANE):
        for s in range(count):
            target[places[k * count + s]] = parts[k][s]


PLANE = 4
DP = ("column", "plane")


def pairs_by(size, by):
    return [(i, i ^ by) for i in range(size)]


def gather_column(local):
    count = lax.axis_size("column")
    others = [lax.ppermute(local, "column", pairs_by(count, s)) for s in range(1, count)]
    return jnp.stack([local] + others)


def gather_plane(column):
    return [column] + [
        lax.ppermute(column, "plane", pairs_by(PLANE, k)) for k in range(1, PLANE)
    ]


def place(parts):
    count, block, width = parts[0].shape
    high, low = lax.axis_index("column"), lax.axis_index("plane")
    places = jnp.stack([(high ^ s) * PLANE + (low ^ k) for k in range(PLANE) for s in range(count)])
    vmem = pl.BlockSpec(memory_space=pltpu.VMEM)
    placed = pl.pallas_call(
        functools.partial(place_kernel, count),
        in_specs=[scalar] + [vmem] * PLANE,
        out_specs=vmem,
        out_shape=shaped((PLANE * count, block, width), parts[0].dtype),
        compiler_params=params(LIM_place),
        cost_estimate=cost(2),
        name="place",
    )(places.astype(jnp.int32), *parts)
    return placed.reshape(PLANE * count * block, width)


def block_of(blocks, index, axis):
    return lax.dynamic_index_in_dim(blocks, index, axis, keepdims=False)


def plane_send(v, by):
    return lax.ppermute(v, "plane", pairs_by(PLANE, by))


def start_sum(total):
    count = lax.axis_size("column")
    low = lax.axis_index("plane")
    rows, width = total.shape
    blocks = total.reshape(count, PLANE, rows // (count * PLANE), width)
    half = width // 2
    parts = (blocks[..., :half], blocks[..., half:])
    sent = []
    for part, near, far in ((parts[0], 1, 2), (parts[1], 2, 1)):
        away = jnp.stack((block_of(part, low ^ near, 1), block_of(part, low ^ 3, 1)))
        keep = jnp.stack((block_of(part, low, 1), block_of(part, low ^ far, 1)))
        sent.append((keep, plane_send(away, near)))
    return sent


def middle_sum(sent):
    moved = []
    for (keep, got), by in zip(sent, (2, 1)):
        both = (keep.astype(f32) + got.astype(f32)).astype(bf16)
        moved.append((both[0], plane_send(both[1], by)))
    return moved


def last_sum(moved):
    count = lax.axis_size("column")
    high = lax.axis_index("column")
    column = jnp.concatenate(
        [(keep.astype(f32) + got.astype(f32)).astype(bf16) for keep, got in moved], axis=-1
    )
    return [block_of(column, high, 0)] + [
        lax.ppermute(block_of(column, high ^ s, 0), "column", pairs_by(count, s))
        for s in range(1, count)
    ]


def finish_sum(terms):
    return tree_sum([t.astype(f32) for t in terms])


def tree_sum(terms):
    while len(terms) > 1:
        terms = [terms[k] + terms[k + 1] for k in range(0, len(terms), 2)]
    return terms[0]


def exchange(total):
    return lax.all_to_all(total, DP, 0, 0, tiled=True)


def sum_blocks(received, blocks):
    cut = received.reshape(blocks, received.shape[0] // blocks, received.shape[1])
    return jnp.sum(cut.astype(f32), axis=0)


def swap(v):
    return lax.ppermute(v, "tensor", [(0, 1), (1, 0)])


def pad_columns(v, width):
    return jnp.pad(v, ((0, 0), (0, width - v.shape[1])))


def tie(value, *others):
    return lax.optimization_barrier((value, *others))[0]


def on_device(
    layer_in,
    upstream,
    lengths,
    rescale,
    gating,
    content,
    selector,
    timestep,
    filters,
    kernels,
    biases,
    decays,
    shortcut,
    amplitude,
    outgoing,
):
    parts = lax.axis_size("tensor")
    rank = lax.axis_index("tensor")
    micro = lengths.shape[0]
    half_rows = layer_in.shape[0] // micro
    rows = half_rows * parts
    width = layer_in.shape[1]
    inner = gating.shape[1]
    heads = timestep.shape[1]
    state_cols = selector.shape[1]
    inner_width = inner * parts

    state_half = state_cols // parts
    own_select = lax.dynamic_slice_in_dim(selector, rank * state_half, state_half, 1)
    spaced = heads // (GROUP // HEAD) * SLOTS
    step_local = jnp.pad(
        timestep.reshape(-1, spaced // SLOTS, GROUP // HEAD),
        ((0, 0), (0, 0), (0, SLOTS - GROUP // HEAD)),
    ).reshape(-1, spaced)
    first_local = jnp.concatenate(
        (content, pad_columns(jnp.concatenate((own_select, step_local), axis=1), BLOCK)), axis=1
    )
    second_local = jnp.concatenate((gating, outgoing.T), axis=1)
    first_column = gather_column(first_local)
    second_own = lax.all_gather(second_local, DP, axis=0, tiled=True)

    def across(array):
        blocks = array.reshape(micro, half_rows, width)
        return lax.all_to_all(blocks, "tensor", 0, 0, tiled=True).reshape(rows, width)

    def outputs_of(array):
        mine = lax.dynamic_slice_in_dim(array, rank * half_rows, half_rows, 0)
        theirs = lax.dynamic_slice_in_dim(array, (1 - rank) * half_rows, half_rows, 0)
        return mine, swap(theirs)

    def join(mine, got):
        return jnp.where(
            rank == 0, jnp.concatenate((mine, got)), jnp.concatenate((got, mine))
        )

    tokens = across(layer_in)
    cotangent = across(upstream)
    length = lax.dynamic_slice_in_dim(lengths, rank, 1, 0)
    rank_1 = rank.reshape(1)

    flat = jnp.concatenate((filters.reshape(-1), amplitude, biases, decays, shortcut))
    flat_other = swap(flat)
    taps = filters.shape[0]

    def unpack(vector):
        edges = [0, taps * inner, (taps + 1) * inner]
        edges += [edges[-1] + heads * k for k in range(1, 4)]
        cut = [vector[a:b] for a, b in zip(edges[:-1], edges[1:])]
        return (cut[0].reshape(taps, inner), cut[1].reshape(1, inner), *cut[2:])

    filters_2, amplitude_2, biases_2, decays_2, shortcut_2 = zip(unpack(flat), unpack(flat_other))

    per = GROUP // HEAD

    def head_lanes(pair):
        cut = jnp.concatenate(pair).reshape(-1, per)
        return pad_columns(jnp.pad(cut, ((0, 0), (0, SLOTS - per))).reshape(1, -1), BLOCK)

    rates = jnp.exp(jnp.concatenate(decays_2))
    rate_lanes = head_lanes((rates,))
    shortcut_lanes = [jnp.repeat(s, HEAD).reshape(1, inner) for s in shortcut_2]
    normed, normed_t, inverse_wide = front(tie(tokens, first_column), rescale)
    dbranch, dbranch_t = mask_rows(length, cotangent)
    first_parts = gather_plane(first_column)
    first_parts[0] = tie(first_parts[0], dbranch, normed)
    first_own = place(first_parts)
    first_other = swap(first_own)
    firsts = (first_own, first_other)
    prep = prepare(
        rank_1, normed, first_own, first_other, kernels, head_lanes(biases_2), rate_lanes, spaced
    )
    kept = [None, None]
    kept[0] = mix_forward(
        0, length, normed, first_own, filters_2[0], shortcut_lanes[0], prep, inner
    )
    second_own = tie(second_own, kept[0][0])
    second_other = swap(second_own)
    seconds = (second_own, second_other)
    kept[1] = mix_forward(
        1, length, normed, tie(first_other, second_own), filters_2[1], shortcut_lanes[1], prep, inner
    )
    back, layer_seq, gate_sums = gate_both(
        length, normed, normed_t, tokens, dbranch, dbranch_t, seconds,
        jnp.concatenate(amplitude_2, axis=1), kept, inner_width,
    )
    layer_pair = outputs_of(layer_seq)
    second_grads = jnp.concatenate(
        [(back[0][k].astype(f32) + swap(back[1][k]).astype(f32)).astype(bf16) for k in (2, 3)],
        axis=1,
    )
    second_grads, later_grad = lax.optimization_barrier((second_grads, back[1][0]))
    second_sent = start_sum(second_grads)

    deep = [None, None]
    deep[1] = mix_backward(
        1, length, normed_t, firsts[1], filters_2[1], shortcut_lanes[1], prep, later_grad, kept[1], None, False
    )
    content_swapped = swap(deep[1][1])
    early_grad, *landed = lax.optimization_barrier((back[0][0], *[got for _, got in second_sent]))
    second_sent = [(keep, got) for (keep, _), got in zip(second_sent, landed)]
    second_sent[0] = (second_sent[0][0], tie(second_sent[0][1], deep[1][1]))
    second_moved = middle_sum(second_sent)
    deep[0] = mix_backward(
        0, length, normed_t, firsts[0], filters_2[0], shortcut_lanes[0], prep, early_grad, kept[0],
        deep[1][5:8], True,
    )
    content_own, *landed = lax.optimization_barrier((deep[0][1], *[got for _, got in second_moved]))
    second_moved = [(keep, got) for (keep, _), got in zip(second_moved, landed)]
    second_terms = last_sum(second_moved)

    content_grads = (content_own.astype(f32) + content_swapped.astype(f32)).astype(bf16)
    content_grads, b_sum = lax.optimization_barrier((content_grads, deep[0][6]))
    first_sent = start_sum(content_grads)
    rate_tiles = jnp.broadcast_to(
        jnp.pad(rates.reshape(-1, per), ((0, 0), (0, SLOTS - per)))[:, :, None],
        (2 * heads // per, SLOTS, BLOCK),
    )
    row_sums = (deep[0][8], deep[1][8], gate_sums)
    (
        grad_own, grad_other, extra_own, extra_other, kernels_part, biases_tile, decays_tile, rows_sum
    ) = finish(
        rank_1, normed_t, firsts, prep, b_sum, deep[0][7], kernels, rate_tiles, deep, row_sums
    )

    def compact(tiles):
        return jnp.sum(tiles[:, :per], axis=2).reshape(2 * heads)

    biases_part, decays_part = compact(biases_tile), compact(decays_tile)
    grad_own, *landed = lax.optimization_barrier((grad_own, *[got for _, got in first_sent]))
    first_sent = [(keep, got) for (keep, _), got in zip(first_sent, landed)]
    first_moved = middle_sum(first_sent)
    rows_sum, extra_other = lax.optimization_barrier((rows_sum, extra_other, first_moved[0][0]))[:2]
    extra_sum = (extra_own + swap(extra_other).astype(f32)).astype(bf16)
    rescale_part = jnp.sum(rows_sum, axis=1) / rescale
    grad_seq = backward_rows(
        deep, back, firsts, seconds, (grad_own, grad_other), tokens, inverse_wide, rescale, dbranch
    )
    grad_seq, *landed = lax.optimization_barrier((grad_seq, *[got for _, got in first_moved]))
    first_moved = [(keep, got) for (keep, _), got in zip(first_moved, landed)]
    first_terms = last_sum(first_moved)
    input_grad = join(*outputs_of(grad_seq))
    layer_out = join(*lax.optimization_barrier((*layer_pair, grad_seq))[:2])

    def per_head(row):
        return jnp.sum(row.reshape(heads, HEAD), axis=1)

    small_own, small_other = (
        jnp.concatenate(
            (
                deep[h][2].reshape(-1),
                back[h][4].reshape(-1),
                biases_part[h * heads : (h + 1) * heads],
                decays_part[h * heads : (h + 1) * heads],
                per_head(back[h][5]),
                rescale_part,
                kernels_part.reshape(-1),
            )
        )
        for h in range(2)
    )
    small = small_own + swap(small_other)
    used = small.shape[0]
    lines = -(-used // (16 * BLOCK)) * 16
    small = jnp.pad(small, (0, lines * BLOCK - used)).reshape(1, lines, BLOCK)
    small_high = small.astype(bf16)
    small_low = (small - small_high.astype(f32)).astype(bf16)
    blocks = lax.axis_size(DP)
    own_rows = width // blocks
    both = jnp.concatenate((small_high, small_low), axis=1)
    sent = jnp.concatenate(
        (
            extra_sum.reshape(blocks, own_rows, BLOCK),
            jnp.broadcast_to(both, (blocks, 2 * lines, BLOCK)),
        ),
        axis=1,
    )
    got = lax.all_to_all(sent, DP, 0, 0, tiled=True)
    gathered = jnp.sum(got.astype(f32), axis=0)
    extra_total = gathered[:own_rows]
    summed = (gathered[own_rows : own_rows + lines] + gathered[own_rows + lines :]).reshape(-1)
    cut = (taps + 1) * inner + 3 * heads
    filters_grad, amplitude_grad, biases_grad, decays_grad, shortcut_grad = unpack(summed[:cut])
    second_total = finish_sum(second_terms)
    first_total = finish_sum(first_terms)
    state_own = extra_total[:, :state_half]
    state_other = swap(state_own)
    selector_grad = jnp.where(
        rank == 0,
        jnp.concatenate((state_own, state_other), axis=1),
        jnp.concatenate((state_other, state_own), axis=1),
    )
    return (
        layer_out,
        input_grad,
        summed[cut : cut + width],
        second_total[:, :inner],
        first_total,
        selector_grad,
        extra_total[:, state_half : state_half + spaced]
        .reshape(-1, spaced // SLOTS, SLOTS)[:, :, :per]
        .reshape(-1, heads),
        filters_grad,
        summed[cut + width : used].reshape(taps, state_cols),
        biases_grad,
        decays_grad,
        shortcut_grad,
        amplitude_grad.reshape(inner),
        second_total[:, inner:].T,
    )


def solution(mesh):
    devices = mesh.devices
    split = Mesh(
        devices.reshape(devices.shape[0] // PLANE, PLANE, devices.shape[1]), (*DP, "tensor")
    )
    return jax.shard_map(
        on_device,
        mesh=split,
        in_specs=(
            P((*DP, "tensor"), None),
            P((*DP, "tensor"), None),
            P(DP),
            P(),
            P(DP, "tensor"),
            P(DP, "tensor"),
            P(DP, None),
            P(DP, "tensor"),
            P(None, "tensor"),
            P(),
            P("tensor"),
            P("tensor"),
            P("tensor"),
            P("tensor"),
            P("tensor", DP),
        ),
        out_specs=(
            P((*DP, "tensor"), None),
            P((*DP, "tensor"), None),
            P(),
            P(DP, "tensor"),
            P(DP, "tensor"),
            P(DP, None),
            P(DP, "tensor"),
            P(None, "tensor"),
            P(),
            P("tensor"),
            P("tensor"),
            P("tensor"),
            P("tensor"),
            P("tensor", DP),
        ),
        check_vma=False,
    )
```

```python
import functools

import jax
import jax.numpy as jnp
from jax import lax
from jax.experimental import pallas as pl
from jax.experimental.pallas import tpu as pltpu
from jax.sharding import Mesh
from jax.sharding import PartitionSpec as P

BLOCK = 128
HEAD = 64
STATE = 64
GROUP = 256
SLOTS = 8
LIM_prep = 60
LIM_mix = 60
LIM_gate = 60
LIM_gate_back = 60
LIM_mix_back = 60
LIM_finish = 60
LIM_back = 60
LIM_front = 60
LIM_mask_rows = 60
LIM_place = 60
LOG2E = 1.4426950408889634
epsilon = 1e-05
f32 = jnp.float32
bf16 = jnp.bfloat16
ANY = pl.ANY


def dot(a, b):
    return lax.dot_general(a, b, (((1,), (0,)), ((), ())), preferred_element_type=f32)


def dot_nt(a, b):
    return lax.dot_general(a, b, (((1,), (1,)), ((), ())), preferred_element_type=f32)


def dot_full(a, b):
    return lax.dot_general(
        a, b, (((1,), (0,)), ((), ())), preferred_element_type=f32, precision=lax.Precision.HIGHEST
    )


def iota(shape, axis):
    return lax.broadcasted_iota(jnp.int32, shape, axis)


def chunk(c, after=0):
    return slice(c * BLOCK + after, (c + 1) * BLOCK + after)


def each_chunk(chunks, body, carry):
    for c in range(chunks):
        carry = body(c, carry)
    return carry


def sigmoid(v):
    return 1.0 / (1.0 + jnp.exp(-v))


def conv_taps(padded, c, taps_ref):
    total = padded[chunk(c, 8)] * taps_ref[3:4]
    for back in range(1, 4):
        total = total + padded[chunk(c, 8 - back)] * taps_ref[3 - back : 4 - back]
    return total


def lane_low():
    return iota((BLOCK, 2 * HEAD), 1) < HEAD


def spread(block, column):
    index = jnp.full((BLOCK, BLOCK), column, jnp.int32)
    return jnp.take_along_axis(block, index, axis=1, mode="promise_in_bounds")


def spread_pair(block, column):
    index = column + iota((BLOCK, BLOCK), 1) // HEAD
    return jnp.take_along_axis(block, index, axis=1, mode="promise_in_bounds")


def pair_rows(piece, low):
    return jnp.concatenate(
        (jnp.where(low, piece, 0.0), jnp.where(low, 0.0, piece)), axis=0
    ).astype(bf16)


def prep_kernel(
    heads, rank, normed, extra_own, extra_other, kernels, biases, rates,
    select_in, b_rows, c_rows, select_t, gram, gram_t,
    ends, starts, steps, ends_t, starts_t, steps_t, slope_t, padded, logits_s,
):
    chunks = normed.shape[0] // BLOCK
    groups = ends_t.shape[0]
    down = iota((BLOCK, BLOCK), 0)
    across = iota((BLOCK, BLOCK), 1)
    tri = (down >= across).astype(f32)
    off = (down != across).astype(f32)
    padded[0:8] = jnp.zeros((8, BLOCK), f32)

    own = dot(normed[...], extra_own[...])
    other = dot(normed[...], extra_other[...])
    lane = iota(own.shape, 1)
    first = jnp.where(rank[0] == 0, own, other)
    second = jnp.where(rank[0] == 0, other, own)
    selected = jnp.where(lane < STATE, first, pltpu.roll(second, STATE, 1))
    select_in[...] = selected
    padded[8:] = selected
    logits_s[...] = jnp.where(
        lane < heads, pltpu.roll(own, BLOCK - STATE, 1), pltpu.roll(other, BLOCK - STATE + heads, 1)
    )

    def body(c, carry):
        rows = chunk(c)
        pre = conv_taps(padded, c, kernels)
        act = pre * sigmoid(pre)
        act_t = act.T.astype(bf16)
        act = act.astype(bf16)
        b_rows[rows] = act[:, :STATE]
        c_rows[rows] = act[:, STATE:]
        select_t[c] = act_t
        gram[c] = dot(act[:, STATE:], act_t[:STATE]) * off
        gram_t[c] = dot(act[:, :STATE], act_t[STATE:]) * off
        logits = logits_s[rows] + biases[...]
        small = jnp.exp(-jnp.abs(logits))
        whole = 1.0 + small
        log_part = jnp.where(
            whole == 1.0, small, jnp.log(whole) * (small / jnp.where(whole == 1.0, 1.0, whole - 1.0))
        )
        step = jnp.maximum(logits, 0.0) + log_part
        decay = -rates[...] * step
        inclusive = dot_full(tri, decay)
        end = inclusive * LOG2E
        start = (inclusive - decay) * LOG2E
        ends[rows] = end
        starts[rows] = start
        steps[rows] = step
        turned = ((ends_t, end), (starts_t, start), (steps_t, step), (slope_t, sigmoid(logits)))
        for target, value in turned:
            value_t = value.T
            for g in range(groups):
                target[g, :, rows] = value_t[g * SLOTS : (g + 1) * SLOTS]
        return carry

    each_chunk(chunks, body, 0)


def mix_kernel(
    half, length, normed, content, filters, shortcut, c_rows, select_t, gram,
    ends, starts, steps, ends_t, starts_t,
    mixed, x_low, values, early, late, ends_w, starts_w, steps_w,
    padded, scaled, gain_e, gain_l, totals,
):
    base = (half * pl.num_programs(0) + pl.program_id(0)) * SLOTS
    chunks = normed.shape[0] // BLOCK
    pairs = GROUP // (2 * HEAD)
    padded[0:8] = jnp.zeros((8, GROUP), f32)
    block = dot(normed[...], content[...])
    padded[8:] = block
    values[...] = block.astype(bf16)

    def gains(c, carry):
        rows = chunk(c)
        pre = conv_taps(padded, c, filters)
        inside = (c * BLOCK + iota((BLOCK, GROUP), 0)) < length[0]
        act = jnp.where(inside, pre * sigmoid(pre), 0.0).astype(bf16)
        x_low[rows] = act
        low = lane_low()
        end_block = ends[rows]
        start_block = starts[rows]
        step_block = steps[rows]
        for p in range(pairs):
            lanes = slice(2 * HEAD * p, 2 * HEAD * (p + 1))
            ends_p = [spread(end_block, base + 2 * p + k) for k in range(2)]
            starts_p = [spread(start_block, base + 2 * p + k) for k in range(2)]
            for k in range(2):
                wide = slice(BLOCK * (2 * p + k), BLOCK * (2 * p + k + 1))
                ends_w[rows, wide] = ends_p[k]
                starts_w[rows, wide] = starts_p[k]
            end = jnp.where(low, *ends_p)
            start = jnp.where(low, *starts_p)
            step = spread_pair(step_block, base + 2 * p)
            steps_w[rows, lanes] = step
            total = end[BLOCK - 1 : BLOCK]
            xs = act[:, lanes].astype(f32) * step
            scaled[rows, lanes] = xs
            totals[c, :, lanes] = jnp.broadcast_to(total, (8, 2 * HEAD))
            both = jnp.concatenate((jnp.exp2(total - end) * xs, jnp.exp2(start) * xs), axis=1)
            gain = dot(select_t[c, :STATE], both.astype(bf16))
            gain_e[c, :, lanes] = gain[:, : 2 * HEAD]
            gain_l[c, :, lanes] = gain[:, 2 * HEAD :]
        return carry

    each_chunk(chunks, gains, 0)

    state = jnp.zeros((STATE, GROUP), f32)
    for c in range(chunks):
        early[c] = state.astype(bf16)
        state = jnp.exp2(totals[c, :1]) * state + gain_e[c]
    state = jnp.zeros((STATE, GROUP), f32)
    for c in reversed(range(chunks)):
        late[c] = state.astype(bf16)
        state = jnp.exp2(totals[c, :1]) * state + gain_l[c]

    def mix(c, carry):
        rows = chunk(c)
        low = lane_low()
        coupled = gram[c]
        for p in range(pairs):
            lanes = slice(2 * HEAD * p, 2 * HEAD * (p + 1))
            wides = [slice(BLOCK * (2 * p + k), BLOCK * (2 * p + k + 1)) for k in range(2)]
            ends_p = [ends_w[rows, w] for w in wides]
            starts_p = [starts_w[rows, w] for w in wides]
            coupling = []
            for k in range(2):
                end_row = ends_t[0, 2 * p + k : 2 * p + k + 1, rows]
                start_row = starts_t[0, 2 * p + k : 2 * p + k + 1, rows]
                power = jnp.exp2(jnp.minimum(ends_p[k] - end_row, start_row - starts_p[k]))
                coupling.append((coupled * power).astype(bf16))
            xs = scaled[rows, lanes]
            inner = dot(jnp.concatenate(coupling, axis=1), pair_rows(xs, low))
            states = jnp.concatenate((early[c, :, lanes], late[c, :, lanes]), axis=1)
            outer = dot(c_rows[rows], states)
            end = jnp.where(low, *ends_p)
            start = jnp.where(low, *starts_p)
            total = end[BLOCK - 1 : BLOCK]
            mixed[rows, lanes] = (
                inner
                + jnp.exp2(end) * outer[:, : 2 * HEAD]
                + jnp.exp2(total - start) * outer[:, 2 * HEAD :]
                + shortcut[:, lanes] * x_low[rows, lanes].astype(f32)
            ).astype(bf16)
        return carry

    each_chunk(chunks, mix, 0)


def add_products(target, grads, weights):
    @pl.when(pl.program_id(0) == 0)
    def _():
        target[...] = jnp.zeros(target.shape, f32)

    products = grads * weights[...].astype(f32)
    target[...] += products[:, :BLOCK] + products[:, BLOCK:]


def gate_kernel(
    inner_width,
    length, normed, normed_t, tokens, cotangent, cotangent_t,
    gating_own, gating_other, out_own, out_other, amplitude,
    mixed_own, mixed_other, x_own, x_other,
    mixed_grad_own, mixed_grad_other, gate_grad_own, gate_grad_other,
    gating_grad_own, gating_grad_other, out_grad_own, out_grad_other,
    amplitude_grad_own, amplitude_grad_other, shortcut_grad_own, shortcut_grad_other,
    layer_out, row_sums,
    squares, total, gates, scale_s, cross_s, gated_s, dgated_s, mixed_grad_s, gate_grad_s,
):
    chunks = normed.shape[0] // BLOCK
    step = pl.program_id(0)
    groups = pl.num_programs(0) // 2
    group = lax.rem(step, groups)
    own = group < groups // 2

    def pick(first, second):
        return jnp.where(own, first, second)

    @pl.when(step == 0)
    def _():
        squares[...] = jnp.zeros(squares.shape, f32)
        total[...] = jnp.zeros(total.shape, f32)
        row_sums[...] = jnp.zeros(row_sums.shape, f32)

    @pl.when(step < groups)
    def _():
        gates[group] = dot(normed[...], pick(gating_own[...], gating_other[...]))

        def body(c, carry):
            rows = chunk(c)
            gate = gates[group, rows]
            gated = pick(mixed_own[rows], mixed_other[rows]).astype(f32) * (gate * sigmoid(gate))
            square = gated * gated
            squares[rows] += square[:, : GROUP // 2] + square[:, GROUP // 2 :]
            gated_s[rows] = (gated * amplitude[...]).astype(bf16)
            return carry

        each_chunk(chunks, body, 0)
        total[...] += dot_nt(gated_s[...], pick(out_own[...], out_other[...]))

    @pl.when(step == groups - 1)
    def _():
        def finish(c, carry):
            rows = chunk(c)
            mean = jnp.sum(squares[rows], axis=1, keepdims=True) / inner_width
            scale = lax.rsqrt(mean + epsilon)
            inside = (c * BLOCK + iota((BLOCK, 1), 0)) < length[0]
            projected = total[rows]
            sum_out = tokens[rows].astype(f32) + scale * projected
            layer_out[rows] = jnp.where(inside, sum_out, 0.0).astype(bf16)
            inner = jnp.sum(cotangent[rows].astype(f32) * projected, axis=1, keepdims=True)
            cross = scale * scale * scale * inner / inner_width
            scale_s[rows] = jnp.broadcast_to(scale, (BLOCK, BLOCK))
            cross_s[rows] = jnp.broadcast_to(cross, (BLOCK, BLOCK))
            return carry

        each_chunk(chunks, finish, 0)

    @pl.when(step >= groups)
    def _():
        dgated_s[...] = dot(cotangent[...], pick(out_own[...], out_other[...]))

        def body(c, carry):
            amplitude_sum, shortcut_sum = carry
            rows = chunk(c)
            dgated = dgated_s[rows]
            gate = gates[group, rows]
            sig = sigmoid(gate)
            act = gate * sig
            slope = sig * (1.0 + gate * (1.0 - sig))
            y = pick(mixed_own[rows], mixed_other[rows]).astype(f32)
            x = pick(x_own[rows], x_other[rows]).astype(f32)
            gz = y * act
            scale = jnp.concatenate((scale_s[rows], scale_s[rows]), axis=1)
            cross = jnp.concatenate((cross_s[rows], cross_s[rows]), axis=1)
            unit = gz * scale
            gated_s[rows] = (unit * amplitude[...]).astype(bf16)
            dgz = scale * (amplitude[...] * dgated) - gz * cross
            gate_grad_s[rows] = (dgz * y * slope).astype(bf16)
            dmix = dgz * act
            mixed_grad_s[rows] = dmix.astype(bf16)
            amplitude_sum = amplitude_sum + jnp.sum(dgated * unit, axis=0, keepdims=True)
            shortcut_sum = shortcut_sum + jnp.sum(dmix * x, axis=0, keepdims=True)
            return amplitude_sum, shortcut_sum

        zero = jnp.zeros((1, GROUP), f32)
        amplitude_sum, shortcut_sum = each_chunk(chunks, body, (zero, zero))
        grads = dot(normed_t[...], gate_grad_s[...])
        products = grads * pick(gating_own[...], gating_other[...]).astype(f32)
        row_sums[...] += products[:, :BLOCK] + products[:, BLOCK:]
        gating = grads.astype(bf16)
        out = dot(cotangent_t[...], gated_s[...]).astype(bf16)

        @pl.when(own)
        def _():
            mixed_grad_own[...] = mixed_grad_s[...]
            gate_grad_own[...] = gate_grad_s[...]
            gating_grad_own[...] = gating
            out_grad_own[...] = out
            amplitude_grad_own[...] = amplitude_sum
            shortcut_grad_own[...] = shortcut_sum

        @pl.when(jnp.logical_not(own))
        def _():
            mixed_grad_other[...] = mixed_grad_s[...]
            gate_grad_other[...] = gate_grad_s[...]
            gating_grad_other[...] = gating
            out_grad_other[...] = out
            amplitude_grad_other[...] = amplitude_sum
            shortcut_grad_other[...] = shortcut_sum


def mix_back_kernel(half, first, last, *refs):
    refs = list(refs)
    (
        length, normed_t, content, filters, shortcut, b_rows, c_rows, select_t, gram_t,
        ends_t, starts_t, mixed_grad, x_low, values, early, late, ends_w, starts_w, steps_w,
    ) = refs[:19]
    refs = refs[19:]
    if not first:
        gram_in, b_in, c_in = refs[:3]
        refs = refs[3:]
    (
        values_grad, content_grad, filters_grad, decay_grad, direct_grad, gram_grad, b_grad, c_grad,
        row_sums,
        padded, pre_grad, gain_e, gain_l, totals,
        early_grad, late_grad, sums, local_rows, through,
    ) = refs
    step_id = pl.program_id(0)
    rows_all = x_low.shape[0]
    chunks = rows_all // BLOCK
    pairs = GROUP // (2 * HEAD)

    @pl.when(step_id == 0)
    def _():
        if first:
            gram_grad[...] = jnp.zeros(gram_grad.shape, f32)
            b_grad[...] = jnp.zeros(b_grad.shape, f32)
            c_grad[...] = jnp.zeros(c_grad.shape, f32)
        else:
            gram_grad[...] = gram_in[...]
            b_grad[...] = b_in[...]
            c_grad[...] = c_in[...]

    padded[0:8] = jnp.zeros((8, GROUP), f32)
    padded[8:] = values[...].astype(f32)
    pre_grad[rows_all : rows_all + 8] = jnp.zeros((8, GROUP), f32)

    def gains(c, carry):
        rows = chunk(c)
        low = lane_low()
        for p in range(pairs):
            lanes = slice(2 * HEAD * p, 2 * HEAD * (p + 1))
            wides = [slice(BLOCK * (2 * p + k), BLOCK * (2 * p + k + 1)) for k in range(2)]
            ends_p = [ends_w[rows, w] for w in wides]
            starts_p = [starts_w[rows, w] for w in wides]
            end = jnp.where(low, *ends_p)
            start = jnp.where(low, *starts_p)
            total = end[BLOCK - 1 : BLOCK]
            totals[c, :, lanes] = jnp.broadcast_to(total, (8, 2 * HEAD))
            dy = mixed_grad[rows, lanes].astype(f32)
            both = jnp.concatenate((jnp.exp2(end) * dy, jnp.exp2(total - start) * dy), axis=1)
            gain = dot(select_t[c, STATE:], both.astype(bf16))
            gain_e[c, :, lanes] = gain[:, : 2 * HEAD]
            gain_l[c, :, lanes] = gain[:, 2 * HEAD :]
        return carry

    each_chunk(chunks, gains, 0)

    state = jnp.zeros((STATE, GROUP), f32)
    for c in reversed(range(chunks)):
        early_grad[c] = state.astype(bf16)
        kept = jnp.exp2(totals[c, :1]) * state
        through[c] = jnp.broadcast_to(
            jnp.sum(kept * early[c].astype(f32), axis=0, keepdims=True), (8, GROUP)
        )
        state = kept + gain_e[c]
    state = jnp.zeros((STATE, GROUP), f32)
    for c in range(chunks):
        late_grad[c] = state.astype(bf16)
        kept = jnp.exp2(totals[c, :1]) * state
        through[c] += jnp.broadcast_to(
            jnp.sum(kept * late[c].astype(f32), axis=0, keepdims=True), (8, GROUP)
        )
        state = kept + gain_l[c]

    down = iota((BLOCK, BLOCK), 0)
    across = iota((BLOCK, BLOCK), 1)

    def mix(c, carry):
        rows = chunk(c)
        low = lane_low()
        coupled = gram_t[c]
        gram_sum = gram_grad[c]
        b_sum = b_grad[rows]
        c_sum = c_grad[rows]
        row_id = iota((8, BLOCK), 0)
        lane_id = iota((8, BLOCK), 1)
        flow = jnp.zeros((8, BLOCK), f32)
        apart = jnp.zeros((16, BLOCK), f32)
        columns_sum = jnp.zeros((BLOCK, BLOCK), f32)
        below_rows = []
        above_rows = []
        for p in range(pairs):
            lanes = slice(2 * HEAD * p, 2 * HEAD * (p + 1))
            wides = [slice(BLOCK * (2 * p + k), BLOCK * (2 * p + k + 1)) for k in range(2)]
            ends_p = [ends_w[rows, w] for w in wides]
            starts_p = [starts_w[rows, w] for w in wides]
            end = jnp.where(low, *ends_p)
            start = jnp.where(low, *starts_p)
            total = end[BLOCK - 1 : BLOCK]
            step = steps_w[rows, lanes]
            x = x_low[rows, lanes].astype(f32)
            dy = mixed_grad[rows, lanes].astype(f32)
            xs = x * step
            dy_rows = pair_rows(dy, low)
            powers = []
            coupling = []
            for k in range(2):
                end_row = ends_t[0, 2 * p + k : 2 * p + k + 1, rows]
                start_row = starts_t[0, 2 * p + k : 2 * p + k + 1, rows]
                power = jnp.exp2(jnp.minimum(end_row - ends_p[k], starts_p[k] - start_row))
                powers.append(power)
                coupling.append(coupled * power)
            inner = dot(jnp.concatenate(coupling, axis=1).astype(bf16), dy_rows)
            pair_products = dot_nt(xs.astype(bf16), dy_rows)
            for k in range(2):
                product = pair_products[:, BLOCK * k : BLOCK * (k + 1)]
                gram_sum = gram_sum + product * powers[k]
                spread_log = product * coupling[k]
                below = jnp.where(down < across, spread_log, 0.0)
                above = spread_log - below
                below_rows.append(jnp.sum(below, axis=0, keepdims=True))
                above_rows.append(jnp.sum(above, axis=0, keepdims=True))
                below_cols = jnp.sum(below, axis=1, keepdims=True)
                above_cols = jnp.sum(above, axis=1, keepdims=True)
                lane = 2 * p + k
                columns_sum = jnp.where(across == lane, below_cols, columns_sum)
                columns_sum = jnp.where(across == lane + 8, above_cols, columns_sum)
            states = jnp.concatenate((early[c, :, lanes], late[c, :, lanes]), axis=1)
            states_grad = jnp.concatenate((early_grad[c, :, lanes], late_grad[c, :, lanes]), axis=1)
            raw_y = dot(c_rows[rows], states)
            raw_x = dot(b_rows[rows], states_grad)
            dy_both = jnp.concatenate((jnp.exp2(end) * dy, jnp.exp2(total - start) * dy), axis=1)
            weight_both = jnp.concatenate((jnp.exp2(total - end), jnp.exp2(start)), axis=1)
            xs_both = jnp.concatenate((xs, xs), axis=1) * weight_both
            outer_both = weight_both * raw_x
            c_sum = c_sum + dot_nt(dy_both.astype(bf16), states)
            b_sum = b_sum + dot_nt(xs_both.astype(bf16), states_grad)
            grad_xs = inner + outer_both[:, : 2 * HEAD] + outer_both[:, 2 * HEAD :]
            from_y = dy_both * raw_y
            from_x = xs_both * raw_x
            local = from_y[:, 2 * HEAD :] - from_x[:, 2 * HEAD :]
            moving = from_y[:, : 2 * HEAD] - from_x[:, : 2 * HEAD] - local
            passed = from_x[:, : 2 * HEAD] + from_y[:, 2 * HEAD :]
            through[c, :, lanes] += jnp.broadcast_to(
                jnp.sum(passed, axis=0, keepdims=True), (8, 2 * HEAD)
            )
            pick = (row_id == 2 * p + lane_id // HEAD).astype(f32)
            none = jnp.zeros((8, BLOCK), f32)
            pick_same = jnp.concatenate((pick, pick), axis=1).astype(bf16)
            pick_apart = jnp.concatenate(
                (
                    jnp.concatenate((pick, none), axis=1),
                    jnp.concatenate((none, pick), axis=1),
                ),
                axis=0,
            ).astype(bf16)
            high = moving.astype(bf16)
            rest = (moving - high.astype(f32)).astype(bf16)
            flow = flow + dot_nt(pick_same, jnp.concatenate((high, rest), axis=1))
            apart = apart + dot_nt(
                pick_apart, jnp.concatenate((local, x * grad_xs), axis=1).astype(bf16)
            )
            pre_grad[rows, lanes] = step * grad_xs + shortcut[:, lanes] * dy
        gram_grad[c] = gram_sum
        b_grad[rows] = b_sum
        c_grad[rows] = c_sum
        tile = slice(c * 8, c * 8 + 8)
        flat = columns_sum.T
        pad = jnp.zeros((4, BLOCK), f32)
        below_all = jnp.concatenate(below_rows + [pad], axis=0)
        above_all = jnp.concatenate(above_rows + [pad], axis=0)
        below_flat = flat[0:8]
        above_flat = flat[8:16]
        sums[tile] = flow + (below_all - below_flat) - (above_all - above_flat)
        local_rows[tile] = apart[:8] + (above_all - above_flat)
        direct_grad[0, tile] = apart[8:]
        return carry

    each_chunk(chunks, mix, 0)

    head_cols = (iota((GROUP, BLOCK), 0) // HEAD == iota((GROUP, BLOCK), 1)).astype(f32)
    tall = 8 * chunks
    through_tall = dot_full(through[...].reshape(tall, GROUP), head_cols)
    own = iota((tall, BLOCK), 1) == iota((tall, BLOCK), 0) % 8
    through_rows = jnp.sum(jnp.where(own, through_tall, 0.0), axis=1, keepdims=True)
    decay_grad[0] = (
        dot_full(sums[...], (down >= across).astype(f32)) + local_rows[...] + through_rows
    )

    def conv_back(c, carry):
        rows = chunk(c)
        pre = conv_taps(padded, c, filters)
        sig = sigmoid(pre)
        inside = (c * BLOCK + iota((BLOCK, GROUP), 0)) < length[0]
        grad = jnp.where(inside, pre_grad[rows] * (sig * (1.0 + pre * (1.0 - sig))), 0.0)
        pre_grad[rows] = grad
        return tuple(
            carry[k]
            + jnp.sum(grad * padded[chunk(c, 5 + k)], axis=0, keepdims=True)
            for k in range(4)
        )

    zero = jnp.zeros((1, GROUP), f32)
    filter_sums = each_chunk(chunks, conv_back, (zero,) * 4)
    filters_grad[...] = jnp.concatenate(filter_sums, axis=0)

    def conv_shift(c, carry):
        rows = chunk(c)
        total = pre_grad[rows] * filters[3:4]
        for ahead in range(1, 4):
            total = total + pre_grad[chunk(c, ahead)] * filters[3 - ahead : 4 - ahead]
        values_grad[rows] = total.astype(bf16)
        return carry

    each_chunk(chunks, conv_shift, 0)
    grads = dot(normed_t[...], values_grad[...])
    content_grad[...] = grads.astype(bf16)
    add_products(row_sums, grads, content)

    if last:

        @pl.when(step_id == pl.num_programs(0) - 1)
        def _():
            def finish(c, carry):
                rows = chunk(c)
                grad = jnp.where(down != across, gram_grad[c], 0.0)
                b_grad[rows] += dot(grad.astype(bf16), c_rows[rows])
                c_grad[rows] += dot(grad.T.astype(bf16), b_rows[rows])
                return carry

            each_chunk(chunks, finish, 0)


def whole(shape):
    return pl.BlockSpec(shape, lambda *_: (0,) * len(shape), pipeline_mode=pl.Buffered(1))


def columns(rows, width=GROUP, after=0):
    return pl.BlockSpec((rows, width), lambda g, *_: (0, g + after))


def planes(shape):
    return pl.BlockSpec(shape, lambda g, *_: (0,) * (len(shape) - 1) + (g,))


def turned(after, rows):
    return pl.BlockSpec((1, 8, rows), lambda g, *_: (g + after, 0, 0))


def lead(shape):
    return pl.BlockSpec((1,) + shape, lambda g, *_: (g,) + (0,) * len(shape))


scalar = pl.BlockSpec(memory_space=pltpu.SMEM)


def shaped(shape, dtype):
    return jax.ShapeDtypeStruct(shape, dtype)


def params(limit=60):
    return pltpu.CompilerParams(vmem_limit_bytes=limit << 20)


def cost(micros):
    return pl.CostEstimate(flops=0, bytes_accessed=int(micros * 3.0e6), transcendentals=0)


def prepare(rank, normed, first_own, first_other, kernels, biases, rates, heads):
    rows, width = normed.shape
    chunks = rows // BLOCK
    groups = 2 * heads // SLOTS
    extra = whole((width, BLOCK))
    shapes = (
        shaped((rows, BLOCK), f32),
        shaped((rows, STATE), bf16),
        shaped((rows, STATE), bf16),
        shaped((chunks, BLOCK, BLOCK), bf16),
        shaped((chunks, BLOCK, BLOCK), f32),
        shaped((chunks, BLOCK, BLOCK), f32),
        shaped((rows, BLOCK), f32),
        shaped((rows, BLOCK), f32),
        shaped((rows, BLOCK), f32),
        shaped((groups, 8, rows), f32),
        shaped((groups, 8, rows), f32),
        shaped((groups, 8, rows), f32),
        shaped((groups, 8, rows), f32),
    )
    return pl.pallas_call(
        functools.partial(prep_kernel, heads),
        grid=(1,),
        in_specs=[
            scalar, whole(normed.shape), extra, extra,
            whole(kernels.shape), whole(biases.shape), whole(rates.shape),
        ],
        out_specs=tuple(whole(o.shape) for o in shapes),
        out_shape=shapes,
        scratch_shapes=[pltpu.VMEM((rows + 8, BLOCK), f32), pltpu.VMEM((rows, BLOCK), f32)],
        compiler_params=params(LIM_prep),
        cost_estimate=cost(4),
        name="prep",
    )(rank, normed, first_own, first_other, kernels, biases, rates)


def front_kernel(tokens, rescale, normed, normed_t, inverse_out):
    width = tokens.shape[1]

    def body(c, carry):
        rows = chunk(c)
        tok = tokens[rows].astype(f32)
        inverse = lax.rsqrt(jnp.sum(tok * tok, axis=1, keepdims=True) / width + epsilon)
        scaled = tok * inverse * rescale[...]
        normed[rows] = scaled.astype(bf16)
        inverse_out[rows] = jnp.broadcast_to(inverse, (BLOCK, BLOCK))
        for k in range(width // BLOCK):
            normed_t[chunk(k), rows] = scaled[:, chunk(k)].T.astype(bf16)
        return carry

    each_chunk(tokens.shape[0] // BLOCK, body, 0)


def front(tokens, rescale):
    rows, width = tokens.shape
    vmem = pl.BlockSpec(memory_space=pltpu.VMEM)
    return pl.pallas_call(
        front_kernel,
        in_specs=[vmem, vmem],
        out_specs=(vmem, vmem, vmem),
        out_shape=(
            shaped((rows, width), bf16), shaped((width, rows), bf16), shaped((rows, BLOCK), f32)
        ),
        compiler_params=params(LIM_front),
        cost_estimate=cost(5),
        name="front",
    )(tokens, rescale.reshape(1, width))


def mask_kernel(length, cotangent, masked, masked_t):
    width = cotangent.shape[1]

    def body(c, carry):
        rows = chunk(c)
        inside = (c * BLOCK + iota((BLOCK, width), 0)) < length[0]
        kept = jnp.where(inside, cotangent[rows].astype(f32), 0.0)
        masked[rows] = kept.astype(bf16)
        for k in range(width // BLOCK):
            masked_t[chunk(k), rows] = kept[:, chunk(k)].T.astype(bf16)
        return carry

    each_chunk(cotangent.shape[0] // BLOCK, body, 0)


def mask_rows(length, cotangent):
    rows, width = cotangent.shape
    vmem = pl.BlockSpec(memory_space=pltpu.VMEM)
    return pl.pallas_call(
        mask_kernel,
        in_specs=[scalar, vmem],
        out_specs=(vmem, vmem),
        out_shape=(shaped((rows, width), bf16), shaped((width, rows), bf16)),
        compiler_params=params(LIM_mask_rows),
        cost_estimate=cost(5),
        name="mask_rows",
    )(length, cotangent)


def finish_kernel(
    rank, normed_t, weights_own, weights_other, select_in, b_grad, c_grad, kernels, rates,
    decay_own, decay_other, direct_own, direct_other, slope_t, steps_t, sums_0, sums_1, sums_2,
    grad_own, grad_other, extra_own, extra_other, kernels_grad, biases_grad, decays_grad, row_sums,
    padded, grad_s,
):
    rows = select_in.shape[0]
    chunks = rows // BLOCK
    half = decay_own.shape[0]
    padded[0:8] = jnp.zeros((8, BLOCK), f32)
    padded[8:] = select_in[...]
    grad_s[rows : rows + 8] = jnp.zeros((8, BLOCK), f32)

    def back(c, carry):
        here = chunk(c)
        pre = conv_taps(padded, c, kernels)
        sig = sigmoid(pre)
        grad = jnp.concatenate((b_grad[here], c_grad[here]), axis=1)
        grad = grad * (sig * (1.0 + pre * (1.0 - sig)))
        grad_s[here] = grad
        return tuple(
            carry[k] + jnp.sum(grad * padded[chunk(c, 5 + k)], axis=0, keepdims=True)
            for k in range(4)
        )

    zero = jnp.zeros((1, BLOCK), f32)
    kernels_grad[...] = jnp.concatenate(each_chunk(chunks, back, (zero,) * 4), axis=0)
    lane = iota((BLOCK, BLOCK), 1)
    used = SLOTS * half

    def turn(c, carry):
        here = chunk(c)
        total = grad_s[here] * kernels[3:4]
        for ahead in range(1, 4):
            total = total + grad_s[chunk(c, ahead)] * kernels[3 - ahead : 4 - ahead]
        tile = slice(SLOTS * c, SLOTS * (c + 1))
        tiles = []
        sums = []
        valid = iota((SLOTS, BLOCK), 0) < GROUP // HEAD
        for g in range(2 * half):
            decay = decay_own if g < half else decay_other
            direct = direct_own if g < half else direct_other
            fall = jnp.where(valid, decay[g % half, tile], 0.0)
            slope = jnp.where(valid, slope_t[g, :, here], 0.0)
            step = (direct[g % half, tile] - rates[g] * fall) * slope
            tiles.append(step)
            sums.append((step, rates[g] * steps_t[g, :, here] * fall))
        blank = jnp.zeros((BLOCK - 2 * used, BLOCK), f32)
        steps = jnp.concatenate(tiles + [blank], axis=0).T
        turned = pltpu.roll(total, STATE, 1)
        first = jnp.where(rank[0] == 0, total, turned)
        second = jnp.where(rank[0] == 0, turned, total)
        keep = lane < STATE + used
        grad_own[here] = jnp.where(
            lane < STATE, first, jnp.where(keep, pltpu.roll(steps, STATE, 1), 0.0)
        ).astype(bf16)
        grad_other[here] = jnp.where(
            lane < STATE, second, jnp.where(keep, pltpu.roll(steps, STATE - used, 1), 0.0)
        ).astype(bf16)
        return [(a + x, b - y) for (a, b), (x, y) in zip(carry, sums)]

    empty = jnp.zeros((SLOTS, BLOCK), f32)
    sums = each_chunk(chunks, turn, [(empty, empty)] * (2 * half))
    for g in range(2 * half):
        biases_grad[g] = sums[g][0]
        decays_grad[g] = sums[g][1]
    own = dot(normed_t[...], grad_own[...])
    other = dot(normed_t[...], grad_other[...])
    extra_own[...] = own
    extra_other[...] = other.astype(bf16)
    row_sums[...] = (
        own * weights_own[...].astype(f32)
        + other * weights_other[...].astype(f32)
        + (sums_0[...] + sums_1[...] + sums_2[...])
    )


def finish(rank, normed_t, narrows, prep, b_grad, c_grad, kernels, rate_tiles, deep, row_sums):
    width, rows = normed_t.shape
    groups = prep[11].shape[0]
    shapes = (
        shaped((rows, BLOCK), bf16),
        shaped((rows, BLOCK), bf16),
        shaped((width, BLOCK), f32),
        shaped((width, BLOCK), bf16),
        shaped(kernels.shape, f32),
        shaped((groups, SLOTS, BLOCK), f32),
        shaped((groups, SLOTS, BLOCK), f32),
        shaped((width, BLOCK), f32),
    )
    rest = (
        prep[0], b_grad, c_grad, kernels, rate_tiles, deep[0][3], deep[1][3], deep[0][4], deep[1][4],
        prep[12], prep[11], *row_sums,
    )
    return pl.pallas_call(
        finish_kernel,
        grid=(1,),
        in_specs=[scalar, whole(normed_t.shape)]
        + [whole(w.shape) for w in narrows]
        + [whole(r.shape) for r in rest],
        out_specs=tuple(whole(o.shape) for o in shapes),
        out_shape=shapes,
        scratch_shapes=[pltpu.VMEM((rows + 8, BLOCK), f32), pltpu.VMEM((rows + 8, BLOCK), f32)],
        compiler_params=params(LIM_finish),
        cost_estimate=cost(6),
        name="finish",
    )(rank, normed_t, *narrows, *rest)


def back_kernel(
    values_own, values_other, gate_own, gate_other, content_own, content_other, gating_own,
    gating_other, extra_own, extra_other, weights_own, weights_other, tokens, inverse_in, rescale,
    cotangent, grad_out, total,
):
    step = pl.program_id(0)

    def products():
        return (
            dot_nt(values_own[...], content_own[...])
            + dot_nt(values_other[...], content_other[...])
            + dot_nt(gate_own[...], gating_own[...])
            + dot_nt(gate_other[...], gating_other[...])
        )

    @pl.when(step == 0)
    def _():
        total[...] = (
            products()
            + dot_nt(extra_own[...], weights_own[...])
            + dot_nt(extra_other[...], weights_other[...])
        )

    @pl.when(step > 0)
    def _():
        total[...] += products()

    @pl.when(step == pl.num_programs(0) - 1)
    def _():
        width = tokens.shape[1]

        def body(c, carry):
            rows = chunk(c)
            inverse = inverse_in[rows, :1]
            unit = tokens[rows].astype(f32) * inverse
            weighted = total[rows] * rescale[...]
            mean = jnp.sum(weighted * unit, axis=1, keepdims=True) / width
            grad = cotangent[rows].astype(f32) + inverse * (weighted - unit * mean)
            grad_out[rows] = grad.astype(bf16)
            return carry

        each_chunk(tokens.shape[0] // BLOCK, body, 0)


def backward_rows(deep, back, firsts, narrows, seconds, extras, tokens, inverse_wide, rescale, cotangent):
    rows, width = tokens.shape
    inner = deep[0][0].shape[1]
    fixed = (tokens, inverse_wide, rescale.reshape(1, width), cotangent)
    return pl.pallas_call(
        back_kernel,
        grid=(inner // GROUP,),
        in_specs=[columns(rows)] * 4
        + [columns(width)] * 4
        + [whole((rows, BLOCK))] * 2
        + [whole(w.shape) for w in narrows]
        + [whole(f.shape) for f in fixed],
        out_specs=whole((rows, width)),
        out_shape=shaped((rows, width), bf16),
        scratch_shapes=[pltpu.VMEM((rows, width), f32)],
        compiler_params=params(LIM_back),
        cost_estimate=cost(14),
        name="back",
    )(
        deep[0][0], deep[1][0], back[0][1], back[1][1], *firsts, *seconds, *extras, *narrows, *fixed
    )


def mix_forward(half, length, normed, content, filters, shortcut, prep, inner):
    (_, _, c_rows, select_t, gram, _, ends, starts, steps, ends_t, starts_t, _, _) = prep
    rows, width = normed.shape
    chunks = rows // BLOCK
    grid = inner // GROUP
    wide = GROUP // HEAD * BLOCK
    return pl.pallas_call(
        functools.partial(mix_kernel, half),
        grid=(grid,),
        in_specs=[
            scalar, whole(normed.shape), columns(width), columns(4), columns(1),
            whole(c_rows.shape), whole(select_t.shape), whole(gram.shape),
            whole(ends.shape), whole(starts.shape), whole(steps.shape),
            turned(half * grid, rows), turned(half * grid, rows),
        ],
        out_specs=(
            columns(rows), columns(rows), columns(rows),
            planes((chunks, STATE, GROUP)), planes((chunks, STATE, GROUP)),
            columns(rows, wide), columns(rows, wide), columns(rows),
        ),
        out_shape=(
            shaped((rows, inner), bf16),
            shaped((rows, inner), bf16),
            shaped((rows, inner), bf16),
            shaped((chunks, STATE, inner), bf16),
            shaped((chunks, STATE, inner), bf16),
            shaped((rows, grid * wide), f32),
            shaped((rows, grid * wide), f32),
            shaped((rows, inner), f32),
        ),
        scratch_shapes=[
            pltpu.VMEM((rows + 8, GROUP), f32),
            pltpu.VMEM((rows, GROUP), f32),
            pltpu.VMEM((chunks, STATE, GROUP), f32),
            pltpu.VMEM((chunks, STATE, GROUP), f32),
            pltpu.VMEM((chunks, 8, GROUP), f32),
        ],
        compiler_params=params(LIM_mix),
        cost_estimate=cost(14),
        name="mix",
    )(length, normed, content, filters, shortcut, c_rows, select_t, gram, ends, starts, steps, ends_t, starts_t)


def gate_both(length, normed, normed_t, tokens, cotangent, cotangent_t, seconds, amplitude, kept, inner_width):
    rows, width = normed.shape
    inner = kept[0][0].shape[1]
    half = inner // GROUP
    groups = 2 * half

    def read(h):
        def at(g):
            k = g % groups
            return jnp.minimum(k, half - 1) if h == 0 else jnp.maximum(k - half, 0)

        return at

    def write(h):
        return lambda g: jnp.clip(g - groups - h * half, 0, half - 1)

    def blocks(height, at, after=0):
        return pl.BlockSpec((height, GROUP), lambda g: (0, at(g) + after))

    fixed = (normed, normed_t, tokens, cotangent, cotangent_t)
    ins = [length, *fixed, *seconds, *seconds, amplitude]
    ins += [kept[0][0], kept[1][0], kept[0][1], kept[1][1]]
    specs = [scalar] + [whole(f.shape) for f in fixed]
    specs += [blocks(width, read(h)) for h in range(2)]
    specs += [blocks(width, read(h), half) for h in range(2)]
    specs += [pl.BlockSpec((1, GROUP), lambda g: (0, g % groups))]
    specs += [blocks(rows, read(h)) for h in range(2)] * 2
    heights = (rows, rows, width, width, 1, 1)
    kinds = (bf16, bf16, bf16, bf16, f32, f32)
    outs = [shaped((n, inner), k) for n, k in zip(heights, kinds) for _ in range(2)]
    out_specs = [blocks(n, write(h)) for n in heights for h in range(2)]
    outs += [shaped((rows, width), bf16), shaped((width, BLOCK), f32)]
    out_specs += [whole((rows, width)), whole((width, BLOCK))]
    got = pl.pallas_call(
        functools.partial(gate_kernel, inner_width),
        grid=(2 * groups,),
        in_specs=specs,
        out_specs=tuple(out_specs),
        out_shape=tuple(outs),
        scratch_shapes=[
            pltpu.VMEM((rows, BLOCK), f32),
            pltpu.VMEM((rows, width), f32),
            pltpu.VMEM((groups, rows, GROUP), f32),
            pltpu.VMEM((rows, BLOCK), f32),
            pltpu.VMEM((rows, BLOCK), f32),
            pltpu.VMEM((rows, GROUP), bf16),
            pltpu.VMEM((rows, GROUP), f32),
            pltpu.VMEM((rows, GROUP), bf16),
            pltpu.VMEM((rows, GROUP), bf16),
        ],
        compiler_params=params(LIM_gate),
        cost_estimate=cost(35),
        name="gate",
    )(*ins)
    return [got[h:12:2] for h in range(2)], got[12], got[13]


def mix_backward(half, length, normed_t, weights, filters, shortcut, prep, mixed_grad, kept, carried, last):
    (_, b_rows, c_rows, select_t, _, gram_t, _, _, _, ends_t, starts_t, _, _) = prep
    _, x_low, values, early, late, *wides = kept
    width, rows = normed_t.shape
    inner = x_low.shape[1]
    chunks = rows // BLOCK
    grid = inner // GROUP
    first = carried is None
    wide = GROUP // HEAD * BLOCK
    shared = (b_rows, c_rows, select_t, gram_t, ends_t, starts_t)
    ins = [length, normed_t, weights, filters, shortcut, *shared]
    ins += [mixed_grad, x_low, values, early, late, *wides]
    specs = [scalar, whole(normed_t.shape), columns(width), columns(4), columns(1)]
    specs += [whole(s.shape) for s in shared[:-2]] + [turned(half * grid, rows)] * 2
    specs += [columns(rows)] * 3 + [planes((chunks, STATE, GROUP))] * 2
    specs += [columns(rows, wide), columns(rows, wide), columns(rows)]
    if not first:
        ins += list(carried)
        specs += [whole(c.shape) for c in carried]
    tall = 8 * chunks
    return pl.pallas_call(
        functools.partial(mix_back_kernel, half, first, last),
        grid=(grid,),
        in_specs=specs,
        out_specs=(
            columns(rows), columns(width), columns(4), lead((tall, BLOCK)), lead((tall, BLOCK)),
            whole((chunks, BLOCK, BLOCK)), whole((rows, STATE)), whole((rows, STATE)),
            whole((width, BLOCK)),
        ),
        out_shape=(
            shaped((rows, inner), bf16),
            shaped((width, inner), bf16),
            shaped((4, inner), f32),
            shaped((grid, tall, BLOCK), f32),
            shaped((grid, tall, BLOCK), f32),
            shaped((chunks, BLOCK, BLOCK), f32),
            shaped((rows, STATE), f32),
            shaped((rows, STATE), f32),
            shaped((width, BLOCK), f32),
        ),
        scratch_shapes=[
            pltpu.VMEM((rows + 8, GROUP), f32),
            pltpu.VMEM((rows + 8, GROUP), f32),
            pltpu.VMEM((chunks, STATE, GROUP), f32),
            pltpu.VMEM((chunks, STATE, GROUP), f32),
            pltpu.VMEM((chunks, 8, GROUP), f32),
            pltpu.VMEM((chunks, STATE, GROUP), bf16),
            pltpu.VMEM((chunks, STATE, GROUP), bf16),
            pltpu.VMEM((tall, BLOCK), f32),
            pltpu.VMEM((tall, BLOCK), f32),
            pltpu.VMEM((chunks, 8, GROUP), f32),
        ],
        compiler_params=params(LIM_mix_back),
        cost_estimate=cost(28),
        name="mix_back",
    )(*ins)


def shift_down(v, by):
    return jnp.pad(v, ((by, 0), (0, 0)))[: v.shape[0]]


def shift_up(v, by):
    return jnp.pad(v, ((0, by), (0, 0)))[by:]


def select_back(select_in, grad, kernels):
    taps = kernels.shape[0]
    shifted = [shift_down(select_in, taps - 1 - k) for k in range(taps)]
    pre = sum(shifted[k] * kernels[k] for k in range(taps))
    sig = sigmoid(pre)
    grad_pre = grad * (sig * (1.0 + pre * (1.0 - sig)))
    kernels_grad = jnp.stack([jnp.sum(grad_pre * shifted[k], axis=0) for k in range(taps)])
    select_grad = sum(shift_up(grad_pre, taps - 1 - k) * kernels[k] for k in range(taps))
    return select_grad, kernels_grad


def heads_to_rows(tall):
    grid, rows, tokens = tall.shape
    shaped_up = tall.reshape(grid, rows // 8, 8, tokens)[:, :, :4]
    return shaped_up.transpose(0, 2, 1, 3).reshape(grid * 4, (rows // 8) * tokens)


def place_kernel(count, places, *refs):
    parts, wide, narrow = refs[:PLANE], refs[PLANE], refs[PLANE + 1]
    cut = wide.shape[2]
    for k in range(PLANE):
        for s in range(count):
            slot = places[k * count + s]
            wide[slot] = parts[k][s, :, :cut]
            narrow[slot] = parts[k][s, :, cut:]


PLANE = 4
DP = ("column", "plane")


def pairs_by(size, by):
    return [(i, i ^ by) for i in range(size)]


def gather_column(local):
    count = lax.axis_size("column")
    others = [lax.ppermute(local, "column", pairs_by(count, s)) for s in range(1, count)]
    return jnp.stack([local] + others)


def gather_plane(column):
    return [column] + [
        lax.ppermute(column, "plane", pairs_by(PLANE, k)) for k in range(1, PLANE)
    ]


def place(parts):
    count, block, width = parts[0].shape
    high, low = lax.axis_index("column"), lax.axis_index("plane")
    places = jnp.stack([(high ^ s) * PLANE + (low ^ k) for k in range(PLANE) for s in range(count)])
    vmem = pl.BlockSpec(memory_space=pltpu.VMEM)
    placed = pl.pallas_call(
        functools.partial(place_kernel, count),
        in_specs=[scalar] + [vmem] * PLANE,
        out_specs=(vmem, vmem),
        out_shape=[shaped((PLANE * count, block, w), bf16) for w in (width - BLOCK, BLOCK)],
        compiler_params=params(LIM_place),
        cost_estimate=cost(2),
        name="place",
    )(places.astype(jnp.int32), *parts)
    return [p.reshape(PLANE * count * block, p.shape[2]) for p in placed]


def block_of(blocks, index, axis):
    return lax.dynamic_index_in_dim(blocks, index, axis, keepdims=False)


def plane_send(v, by):
    return lax.ppermute(v, "plane", pairs_by(PLANE, by))


def start_sum(total):
    count = lax.axis_size("column")
    low = lax.axis_index("plane")
    rows, width = total.shape
    blocks = total.reshape(count, PLANE, rows // (count * PLANE), width)
    half = width // 2
    parts = (blocks[..., :half], blocks[..., half:])
    sent = []
    for part, near, far in ((parts[0], 1, 2), (parts[1], 2, 1)):
        away = jnp.stack((block_of(part, low ^ near, 1), block_of(part, low ^ 3, 1)))
        keep = jnp.stack((block_of(part, low, 1), block_of(part, low ^ far, 1)))
        sent.append((keep, plane_send(away, near)))
    return sent


def middle_sum(sent):
    moved = []
    for (keep, got), by in zip(sent, (2, 1)):
        both = (keep.astype(f32) + got.astype(f32)).astype(bf16)
        moved.append((both[0], plane_send(both[1], by)))
    return moved


def last_sum(moved):
    count = lax.axis_size("column")
    high = lax.axis_index("column")
    column = jnp.concatenate(
        [(keep.astype(f32) + got.astype(f32)).astype(bf16) for keep, got in moved], axis=-1
    )
    terms = [block_of(column, high, 0)] + [
        lax.ppermute(block_of(column, high ^ s, 0), "column", pairs_by(count, s))
        for s in range(1, count)
    ]
    return column, terms


def finish_sum(terms):
    return tree_sum([t.astype(f32) for t in terms])


def tree_sum(terms):
    while len(terms) > 1:
        terms = [terms[k] + terms[k + 1] for k in range(0, len(terms), 2)]
    return terms[0]


def exchange(total):
    return lax.all_to_all(total, DP, 0, 0, tiled=True)


def sum_blocks(received, blocks):
    cut = received.reshape(blocks, received.shape[0] // blocks, received.shape[1])
    return jnp.sum(cut.astype(f32), axis=0)


def swap(v):
    return lax.ppermute(v, "tensor", [(0, 1), (1, 0)])


def pad_columns(v, width):
    return jnp.pad(v, ((0, 0), (0, width - v.shape[1])))


def tie(value, *others):
    return lax.optimization_barrier((value, *others))[0]


def on_device(
    layer_in,
    upstream,
    lengths,
    rescale,
    gating,
    content,
    selector,
    timestep,
    filters,
    kernels,
    biases,
    decays,
    shortcut,
    amplitude,
    outgoing,
):
    parts = lax.axis_size("tensor")
    rank = lax.axis_index("tensor")
    micro = lengths.shape[0]
    half_rows = layer_in.shape[0] // micro
    rows = half_rows * parts
    width = layer_in.shape[1]
    inner = gating.shape[1]
    heads = timestep.shape[1]
    state_cols = selector.shape[1]
    inner_width = inner * parts

    state_half = state_cols // parts
    own_select = lax.dynamic_slice_in_dim(selector, rank * state_half, state_half, 1)
    spaced = heads // (GROUP // HEAD) * SLOTS
    step_local = jnp.pad(
        timestep.reshape(-1, spaced // SLOTS, GROUP // HEAD),
        ((0, 0), (0, 0), (0, SLOTS - GROUP // HEAD)),
    ).reshape(-1, spaced)
    first_local = jnp.concatenate(
        (content, pad_columns(jnp.concatenate((own_select, step_local), axis=1), BLOCK)), axis=1
    )
    second_local = jnp.concatenate((gating, outgoing.T), axis=1)
    first_column = gather_column(first_local)
    second_own = lax.all_gather(second_local, DP, axis=0, tiled=True)

    def across(array):
        blocks = array.reshape(micro, half_rows, width)
        return lax.all_to_all(blocks, "tensor", 0, 0, tiled=True).reshape(rows, width)

    def outputs_of(array):
        mine = lax.dynamic_slice_in_dim(array, rank * half_rows, half_rows, 0)
        theirs = lax.dynamic_slice_in_dim(array, (1 - rank) * half_rows, half_rows, 0)
        return mine, swap(theirs)

    def join(mine, got):
        return jnp.where(
            rank == 0, jnp.concatenate((mine, got)), jnp.concatenate((got, mine))
        )

    tokens = across(layer_in)
    cotangent = across(upstream)
    length = lax.dynamic_slice_in_dim(lengths, rank, 1, 0)
    rank_1 = rank.reshape(1)

    flat = jnp.concatenate((filters.reshape(-1), amplitude, biases, decays, shortcut))
    flat_other = swap(flat)
    taps = filters.shape[0]

    def unpack(vector):
        edges = [0, taps * inner, (taps + 1) * inner]
        edges += [edges[-1] + heads * k for k in range(1, 4)]
        cut = [vector[a:b] for a, b in zip(edges[:-1], edges[1:])]
        return (cut[0].reshape(taps, inner), cut[1].reshape(1, inner), *cut[2:])

    filters_2, amplitude_2, biases_2, decays_2, shortcut_2 = zip(unpack(flat), unpack(flat_other))

    per = GROUP // HEAD

    def head_lanes(pair):
        cut = jnp.concatenate(pair).reshape(-1, per)
        return pad_columns(jnp.pad(cut, ((0, 0), (0, SLOTS - per))).reshape(1, -1), BLOCK)

    rates = jnp.exp(jnp.concatenate(decays_2))
    rate_lanes = head_lanes((rates,))
    shortcut_lanes = [jnp.repeat(s, HEAD).reshape(1, inner) for s in shortcut_2]
    normed, normed_t, inverse_wide = front(tie(tokens, first_column), rescale)
    dbranch, dbranch_t = mask_rows(length, cotangent)
    first_parts = gather_plane(first_column)
    first_parts[0] = tie(first_parts[0], dbranch, normed)
    first_own, narrow_own = place(first_parts)
    narrow_other = swap(narrow_own)
    first_other = swap(first_own)
    firsts = (first_own, first_other)
    narrows = (narrow_own, narrow_other)
    prep = prepare(
        rank_1, normed, *narrows, kernels, head_lanes(biases_2), rate_lanes, spaced
    )
    kept = [None, None]
    kept[0] = mix_forward(
        0, length, normed, first_own, filters_2[0], shortcut_lanes[0], prep, inner
    )
    second_own = tie(second_own, kept[0][0])
    second_other = swap(second_own)
    seconds = (second_own, second_other)
    kept[1] = mix_forward(
        1, length, normed, tie(first_other, second_own), filters_2[1], shortcut_lanes[1], prep, inner
    )
    back, layer_seq, gate_sums = gate_both(
        length, normed, normed_t, tokens, dbranch, dbranch_t, seconds,
        jnp.concatenate(amplitude_2, axis=1), kept, inner_width,
    )
    layer_pair = outputs_of(layer_seq)
    second_grads = jnp.concatenate(
        [(back[0][k].astype(f32) + swap(back[1][k]).astype(f32)).astype(bf16) for k in (2, 3)],
        axis=1,
    )
    second_grads, later_grad = lax.optimization_barrier((second_grads, back[1][0]))
    second_sent = start_sum(second_grads)

    deep = [None, None]
    deep[1] = mix_backward(
        1, length, normed_t, firsts[1], filters_2[1], shortcut_lanes[1], prep, later_grad, kept[1], None, False
    )
    content_swapped = swap(deep[1][1])
    early_grad, *landed = lax.optimization_barrier((back[0][0], *[got for _, got in second_sent]))
    second_sent = [(keep, got) for (keep, _), got in zip(second_sent, landed)]
    second_sent[0] = (second_sent[0][0], tie(second_sent[0][1], deep[1][1]))
    second_moved = middle_sum(second_sent)
    deep[0] = mix_backward(
        0, length, normed_t, firsts[0], filters_2[0], shortcut_lanes[0], prep, early_grad, kept[0],
        deep[1][5:8], True,
    )
    content_own, *landed = lax.optimization_barrier((deep[0][1], *[got for _, got in second_moved]))
    second_moved = [(keep, got) for (keep, _), got in zip(second_moved, landed)]
    _, second_terms = last_sum(second_moved)

    content_grads = (content_own.astype(f32) + content_swapped.astype(f32)).astype(bf16)
    content_grads, b_sum = lax.optimization_barrier((content_grads, deep[0][6]))
    first_sent = start_sum(content_grads)
    rate_tiles = jnp.broadcast_to(
        jnp.pad(rates.reshape(-1, per), ((0, 0), (0, SLOTS - per)))[:, :, None],
        (2 * heads // per, SLOTS, BLOCK),
    )
    row_sums = (deep[0][8], deep[1][8], gate_sums)
    (
        grad_own, grad_other, extra_own, extra_other, kernels_part, biases_tile, decays_tile, rows_sum
    ) = finish(
        rank_1, normed_t, narrows, prep, b_sum, deep[0][7], kernels, rate_tiles, deep, row_sums
    )

    def compact(tiles):
        return jnp.sum(tiles[:, :per], axis=2).reshape(2 * heads)

    biases_part, decays_part = compact(biases_tile), compact(decays_tile)
    first_moved = middle_sum(first_sent)
    extra_sum = (extra_own + swap(extra_other).astype(f32)).astype(bf16)
    rescale_part = jnp.sum(rows_sum, axis=1) / rescale
    column, first_terms = last_sum(first_moved)
    def per_head(row):
        return jnp.sum(row.reshape(heads, HEAD), axis=1)

    small_own, small_other = (
        jnp.concatenate(
            (
                deep[h][2].reshape(-1),
                back[h][4].reshape(-1),
                biases_part[h * heads : (h + 1) * heads],
                decays_part[h * heads : (h + 1) * heads],
                per_head(back[h][5]),
                rescale_part,
                kernels_part.reshape(-1),
            )
        )
        for h in range(2)
    )
    small = small_own + swap(small_other)
    used = small.shape[0]
    lines = -(-used // (16 * BLOCK)) * 16
    small = jnp.pad(small, (0, lines * BLOCK - used)).reshape(1, lines, BLOCK)
    small_high = small.astype(bf16)
    small_low = (small - small_high.astype(f32)).astype(bf16)
    blocks = lax.axis_size(DP)
    own_rows = width // blocks
    both = jnp.concatenate((small_high, small_low), axis=1)
    sent = jnp.concatenate(
        (
            extra_sum.reshape(blocks, own_rows, BLOCK),
            jnp.broadcast_to(both, (blocks, 2 * lines, BLOCK)),
        ),
        axis=1,
    )
    grad_own, *layer_pair, column, sent = lax.optimization_barrier(
        (grad_own, *layer_pair, column, sent)
    )
    grad_seq = backward_rows(
        deep, back, firsts, narrows, seconds, (grad_own, grad_other), tokens, inverse_wide, rescale, dbranch
    )
    input_grad = join(*outputs_of(grad_seq))
    layer_out = join(*layer_pair)

    got = lax.all_to_all(sent, DP, 0, 0, tiled=True)
    gathered = jnp.sum(got.astype(f32), axis=0)
    extra_total = gathered[:own_rows]
    summed = (gathered[own_rows : own_rows + lines] + gathered[own_rows + lines :]).reshape(-1)
    cut = (taps + 1) * inner + 3 * heads
    filters_grad, amplitude_grad, biases_grad, decays_grad, shortcut_grad = unpack(summed[:cut])
    second_total = finish_sum(second_terms)
    first_total = finish_sum(first_terms)
    state_own = extra_total[:, :state_half]
    state_other = swap(state_own)
    selector_grad = jnp.where(
        rank == 0,
        jnp.concatenate((state_own, state_other), axis=1),
        jnp.concatenate((state_other, state_own), axis=1),
    )
    return (
        layer_out,
        input_grad,
        summed[cut : cut + width],
        second_total[:, :inner],
        first_total,
        selector_grad,
        extra_total[:, state_half : state_half + spaced]
        .reshape(-1, spaced // SLOTS, SLOTS)[:, :, :per]
        .reshape(-1, heads),
        filters_grad,
        summed[cut + width : used].reshape(taps, state_cols),
        biases_grad,
        decays_grad,
        shortcut_grad,
        amplitude_grad.reshape(inner),
        second_total[:, inner:].T,
    )


def solution(mesh):
    devices = mesh.devices
    split = Mesh(
        devices.reshape(devices.shape[0] // PLANE, PLANE, devices.shape[1]), (*DP, "tensor")
    )
    return jax.shard_map(
        on_device,
        mesh=split,
        in_specs=(
            P((*DP, "tensor"), None),
            P((*DP, "tensor"), None),
            P(DP),
            P(),
            P(DP, "tensor"),
            P(DP, "tensor"),
            P(DP, None),
            P(DP, "tensor"),
            P(None, "tensor"),
            P(),
            P("tensor"),
            P("tensor"),
            P("tensor"),
            P("tensor"),
            P("tensor", DP),
        ),
        out_specs=(
            P((*DP, "tensor"), None),
            P((*DP, "tensor"), None),
            P(),
            P(DP, "tensor"),
            P(DP, "tensor"),
            P(DP, None),
            P(DP, "tensor"),
            P(None, "tensor"),
            P(),
            P("tensor"),
            P("tensor"),
            P("tensor"),
            P("tensor"),
            P("tensor", DP),
        ),
        check_vma=False,
    )
```

```python
import functools

import jax
import jax.numpy as jnp
from jax import lax
from jax.experimental import pallas as pl
from jax.experimental.pallas import tpu as pltpu
from jax.sharding import Mesh
from jax.sharding import PartitionSpec as P

BLOCK = 128
HEAD = 64
STATE = 64
GROUP = 256
SLOTS = 8
LIM_prep = 60
LIM_mix = 60
LIM_gate = 60
LIM_gate_back = 60
LIM_mix_back = 60
LIM_finish = 60
LIM_back = 60
LIM_front = 60
LIM_mask_rows = 60
LIM_place = 60
LOG2E = 1.4426950408889634
epsilon = 1e-05
f32 = jnp.float32
bf16 = jnp.bfloat16
ANY = pl.ANY


def dot(a, b):
    return lax.dot_general(a, b, (((1,), (0,)), ((), ())), preferred_element_type=f32)


def dot_nt(a, b):
    return lax.dot_general(a, b, (((1,), (1,)), ((), ())), preferred_element_type=f32)


def dot_full(a, b):
    return lax.dot_general(
        a, b, (((1,), (0,)), ((), ())), preferred_element_type=f32, precision=lax.Precision.HIGHEST
    )


def iota(shape, axis):
    return lax.broadcasted_iota(jnp.int32, shape, axis)


def chunk(c, after=0):
    return slice(c * BLOCK + after, (c + 1) * BLOCK + after)


def each_chunk(chunks, body, carry):
    for c in range(chunks):
        carry = body(c, carry)
    return carry


def sigmoid(v):
    return 1.0 / (1.0 + jnp.exp(-v))


def conv_taps(padded, c, taps_ref):
    total = padded[chunk(c, 8)] * taps_ref[3:4]
    for back in range(1, 4):
        total = total + padded[chunk(c, 8 - back)] * taps_ref[3 - back : 4 - back]
    return total


def lane_low():
    return iota((BLOCK, 2 * HEAD), 1) < HEAD


def spread(block, column):
    index = jnp.full((BLOCK, BLOCK), column, jnp.int32)
    return jnp.take_along_axis(block, index, axis=1, mode="promise_in_bounds")


def spread_pair(block, column):
    index = column + iota((BLOCK, BLOCK), 1) // HEAD
    return jnp.take_along_axis(block, index, axis=1, mode="promise_in_bounds")


def pair_rows(piece, low):
    return jnp.concatenate(
        (jnp.where(low, piece, 0.0), jnp.where(low, 0.0, piece)), axis=0
    ).astype(bf16)


def prep_kernel(
    heads, rank, normed, extra_own, extra_other, kernels, biases, rates,
    select_in, b_rows, c_rows, select_t, gram, gram_t,
    ends, starts, steps, ends_t, starts_t, steps_t, slope_t, padded, logits_s,
):
    chunks = normed.shape[0] // BLOCK
    groups = ends_t.shape[0]
    down = iota((BLOCK, BLOCK), 0)
    across = iota((BLOCK, BLOCK), 1)
    tri = (down >= across).astype(f32)
    off = (down != across).astype(f32)
    padded[0:8] = jnp.zeros((8, BLOCK), f32)

    own = dot(normed[...], extra_own[...])
    other = dot(normed[...], extra_other[...])
    lane = iota(own.shape, 1)
    first = jnp.where(rank[0] == 0, own, other)
    second = jnp.where(rank[0] == 0, other, own)
    selected = jnp.where(lane < STATE, first, pltpu.roll(second, STATE, 1))
    select_in[...] = selected
    padded[8:] = selected
    logits_s[...] = jnp.where(
        lane < heads, pltpu.roll(own, BLOCK - STATE, 1), pltpu.roll(other, BLOCK - STATE + heads, 1)
    )

    def body(c, carry):
        rows = chunk(c)
        pre = conv_taps(padded, c, kernels)
        act = pre * sigmoid(pre)
        act_t = act.T.astype(bf16)
        act = act.astype(bf16)
        b_rows[rows] = act[:, :STATE]
        c_rows[rows] = act[:, STATE:]
        select_t[c] = act_t
        gram[c] = dot(act[:, STATE:], act_t[:STATE]) * off
        gram_t[c] = dot(act[:, :STATE], act_t[STATE:]) * off
        logits = logits_s[rows] + biases[...]
        small = jnp.exp(-jnp.abs(logits))
        whole = 1.0 + small
        log_part = jnp.where(
            whole == 1.0, small, jnp.log(whole) * (small / jnp.where(whole == 1.0, 1.0, whole - 1.0))
        )
        step = jnp.maximum(logits, 0.0) + log_part
        decay = -rates[...] * step
        inclusive = dot_full(tri, decay)
        end = inclusive * LOG2E
        start = (inclusive - decay) * LOG2E
        ends[rows] = end
        starts[rows] = start
        steps[rows] = step
        turned = ((ends_t, end), (starts_t, start), (steps_t, step), (slope_t, sigmoid(logits)))
        for target, value in turned:
            value_t = value.T
            for g in range(groups):
                target[g, :, rows] = value_t[g * SLOTS : (g + 1) * SLOTS]
        return carry

    each_chunk(chunks, body, 0)


def mix_kernel(
    half, length, normed, content, filters, shortcut, c_rows, select_t, gram,
    ends, starts, steps, ends_t, starts_t,
    mixed, x_low, values, early, late, ends_w, starts_w, steps_w,
    padded, scaled, gain_e, gain_l, totals,
):
    base = (half * pl.num_programs(0) + pl.program_id(0)) * SLOTS
    chunks = normed.shape[0] // BLOCK
    pairs = GROUP // (2 * HEAD)
    padded[0:8] = jnp.zeros((8, GROUP), f32)
    block = dot(normed[...], content[...])
    padded[8:] = block
    values[...] = block.astype(bf16)

    def gains(c, carry):
        rows = chunk(c)
        pre = conv_taps(padded, c, filters)
        inside = (c * BLOCK + iota((BLOCK, GROUP), 0)) < length[0]
        act = jnp.where(inside, pre * sigmoid(pre), 0.0).astype(bf16)
        x_low[rows] = act
        low = lane_low()
        end_block = ends[rows]
        start_block = starts[rows]
        step_block = steps[rows]
        for p in range(pairs):
            lanes = slice(2 * HEAD * p, 2 * HEAD * (p + 1))
            ends_p = [spread(end_block, base + 2 * p + k) for k in range(2)]
            starts_p = [spread(start_block, base + 2 * p + k) for k in range(2)]
            for k in range(2):
                wide = slice(BLOCK * (2 * p + k), BLOCK * (2 * p + k + 1))
                ends_w[rows, wide] = ends_p[k]
                starts_w[rows, wide] = starts_p[k]
            end = jnp.where(low, *ends_p)
            start = jnp.where(low, *starts_p)
            step = spread_pair(step_block, base + 2 * p)
            steps_w[rows, lanes] = step
            total = end[BLOCK - 1 : BLOCK]
            xs = act[:, lanes].astype(f32) * step
            scaled[rows, lanes] = xs
            totals[c, :, lanes] = jnp.broadcast_to(total, (8, 2 * HEAD))
            both = jnp.concatenate((jnp.exp2(total - end) * xs, jnp.exp2(start) * xs), axis=1)
            gain = dot(select_t[c, :STATE], both.astype(bf16))
            gain_e[c, :, lanes] = gain[:, : 2 * HEAD]
            gain_l[c, :, lanes] = gain[:, 2 * HEAD :]
        return carry

    each_chunk(chunks, gains, 0)

    state = jnp.zeros((STATE, GROUP), f32)
    for c in range(chunks):
        early[c] = state.astype(bf16)
        state = jnp.exp2(totals[c, :1]) * state + gain_e[c]
    state = jnp.zeros((STATE, GROUP), f32)
    for c in reversed(range(chunks)):
        late[c] = state.astype(bf16)
        state = jnp.exp2(totals[c, :1]) * state + gain_l[c]

    def mix(c, carry):
        rows = chunk(c)
        low = lane_low()
        coupled = gram[c]
        for p in range(pairs):
            lanes = slice(2 * HEAD * p, 2 * HEAD * (p + 1))
            wides = [slice(BLOCK * (2 * p + k), BLOCK * (2 * p + k + 1)) for k in range(2)]
            ends_p = [ends_w[rows, w] for w in wides]
            starts_p = [starts_w[rows, w] for w in wides]
            coupling = []
            for k in range(2):
                end_row = ends_t[0, 2 * p + k : 2 * p + k + 1, rows]
                start_row = starts_t[0, 2 * p + k : 2 * p + k + 1, rows]
                power = jnp.exp2(jnp.minimum(ends_p[k] - end_row, start_row - starts_p[k]))
                coupling.append((coupled * power).astype(bf16))
            xs = scaled[rows, lanes]
            inner = dot(jnp.concatenate(coupling, axis=1), pair_rows(xs, low))
            states = jnp.concatenate((early[c, :, lanes], late[c, :, lanes]), axis=1)
            outer = dot(c_rows[rows], states)
            end = jnp.where(low, *ends_p)
            start = jnp.where(low, *starts_p)
            total = end[BLOCK - 1 : BLOCK]
            mixed[rows, lanes] = (
                inner
                + jnp.exp2(end) * outer[:, : 2 * HEAD]
                + jnp.exp2(total - start) * outer[:, 2 * HEAD :]
                + shortcut[:, lanes] * x_low[rows, lanes].astype(f32)
            ).astype(bf16)
        return carry

    each_chunk(chunks, mix, 0)


def add_products(target, grads, weights):
    @pl.when(pl.program_id(0) == 0)
    def _():
        target[...] = jnp.zeros(target.shape, f32)

    products = grads * weights[...].astype(f32)
    target[...] += products[:, :BLOCK] + products[:, BLOCK:]


def gate_kernel(
    inner_width,
    length, normed, normed_t, tokens, cotangent, cotangent_t,
    gating_own, gating_other, out_own, out_other, amplitude,
    mixed_own, mixed_other, x_own, x_other,
    mixed_grad_own, mixed_grad_other, gate_grad_own, gate_grad_other,
    gating_grad_own, gating_grad_other, out_grad_own, out_grad_other,
    amplitude_grad_own, amplitude_grad_other, shortcut_grad_own, shortcut_grad_other,
    layer_out, row_sums,
    squares, total, gates, scale_s, cross_s, gated_s, dgated_s, mixed_grad_s, gate_grad_s,
):
    chunks = normed.shape[0] // BLOCK
    step = pl.program_id(0)
    groups = pl.num_programs(0) // 2
    group = lax.rem(step, groups)
    own = group < groups // 2

    def pick(first, second):
        return jnp.where(own, first, second)

    @pl.when(step == 0)
    def _():
        squares[...] = jnp.zeros(squares.shape, f32)
        total[...] = jnp.zeros(total.shape, f32)
        row_sums[...] = jnp.zeros(row_sums.shape, f32)

    @pl.when(step < groups)
    def _():
        gates[group] = dot(normed[...], pick(gating_own[...], gating_other[...]))

        def body(c, carry):
            rows = chunk(c)
            gate = gates[group, rows]
            gated = pick(mixed_own[rows], mixed_other[rows]).astype(f32) * (gate * sigmoid(gate))
            square = gated * gated
            squares[rows] += square[:, : GROUP // 2] + square[:, GROUP // 2 :]
            gated_s[rows] = (gated * amplitude[...]).astype(bf16)
            return carry

        each_chunk(chunks, body, 0)
        total[...] += dot_nt(gated_s[...], pick(out_own[...], out_other[...]))

    @pl.when(step == groups - 1)
    def _():
        def finish(c, carry):
            rows = chunk(c)
            mean = jnp.sum(squares[rows], axis=1, keepdims=True) / inner_width
            scale = lax.rsqrt(mean + epsilon)
            inside = (c * BLOCK + iota((BLOCK, 1), 0)) < length[0]
            projected = total[rows]
            sum_out = tokens[rows].astype(f32) + scale * projected
            layer_out[rows] = jnp.where(inside, sum_out, 0.0).astype(bf16)
            inner = jnp.sum(cotangent[rows].astype(f32) * projected, axis=1, keepdims=True)
            cross = scale * scale * scale * inner / inner_width
            scale_s[rows] = jnp.broadcast_to(scale, (BLOCK, BLOCK))
            cross_s[rows] = jnp.broadcast_to(cross, (BLOCK, BLOCK))
            return carry

        each_chunk(chunks, finish, 0)

    @pl.when(step >= groups)
    def _():
        dgated_s[...] = dot(cotangent[...], pick(out_own[...], out_other[...]))

        def body(c, carry):
            amplitude_sum, shortcut_sum = carry
            rows = chunk(c)
            dgated = dgated_s[rows]
            gate = gates[group, rows]
            sig = sigmoid(gate)
            act = gate * sig
            slope = sig * (1.0 + gate * (1.0 - sig))
            y = pick(mixed_own[rows], mixed_other[rows]).astype(f32)
            x = pick(x_own[rows], x_other[rows]).astype(f32)
            gz = y * act
            scale = jnp.concatenate((scale_s[rows], scale_s[rows]), axis=1)
            cross = jnp.concatenate((cross_s[rows], cross_s[rows]), axis=1)
            unit = gz * scale
            gated_s[rows] = (unit * amplitude[...]).astype(bf16)
            dgz = scale * (amplitude[...] * dgated) - gz * cross
            gate_grad_s[rows] = (dgz * y * slope).astype(bf16)
            dmix = dgz * act
            mixed_grad_s[rows] = dmix.astype(bf16)
            amplitude_sum = amplitude_sum + jnp.sum(dgated * unit, axis=0, keepdims=True)
            shortcut_sum = shortcut_sum + jnp.sum(dmix * x, axis=0, keepdims=True)
            return amplitude_sum, shortcut_sum

        zero = jnp.zeros((1, GROUP), f32)
        amplitude_sum, shortcut_sum = each_chunk(chunks, body, (zero, zero))
        grads = dot(normed_t[...], gate_grad_s[...])
        products = grads * pick(gating_own[...], gating_other[...]).astype(f32)
        row_sums[...] += products[:, :BLOCK] + products[:, BLOCK:]
        gating = grads.astype(bf16)
        out = dot(cotangent_t[...], gated_s[...]).astype(bf16)

        @pl.when(own)
        def _():
            mixed_grad_own[...] = mixed_grad_s[...]
            gate_grad_own[...] = gate_grad_s[...]
            gating_grad_own[...] = gating
            out_grad_own[...] = out
            amplitude_grad_own[...] = amplitude_sum
            shortcut_grad_own[...] = shortcut_sum

        @pl.when(jnp.logical_not(own))
        def _():
            mixed_grad_other[...] = mixed_grad_s[...]
            gate_grad_other[...] = gate_grad_s[...]
            gating_grad_other[...] = gating
            out_grad_other[...] = out
            amplitude_grad_other[...] = amplitude_sum
            shortcut_grad_other[...] = shortcut_sum


def mix_back_kernel(half, first, last, *refs):
    refs = list(refs)
    (
        length, normed_t, content, filters, shortcut, b_rows, c_rows, select_t, gram_t,
        ends_t, starts_t, mixed_grad, x_low, values, early, late, ends_w, starts_w, steps_w,
    ) = refs[:19]
    refs = refs[19:]
    if not first:
        gram_in, b_in, c_in = refs[:3]
        refs = refs[3:]
    (
        values_grad, content_grad, filters_grad, decay_grad, direct_grad, gram_grad, b_grad, c_grad,
        row_sums,
        padded, pre_grad, gain_e, gain_l, totals,
        early_grad, late_grad, sums, local_rows, through,
    ) = refs
    step_id = pl.program_id(0)
    rows_all = x_low.shape[0]
    chunks = rows_all // BLOCK
    pairs = GROUP // (2 * HEAD)

    @pl.when(step_id == 0)
    def _():
        if first:
            gram_grad[...] = jnp.zeros(gram_grad.shape, f32)
            b_grad[...] = jnp.zeros(b_grad.shape, f32)
            c_grad[...] = jnp.zeros(c_grad.shape, f32)
        else:
            gram_grad[...] = gram_in[...]
            b_grad[...] = b_in[...]
            c_grad[...] = c_in[...]

    padded[0:8] = jnp.zeros((8, GROUP), f32)
    padded[8:] = values[...].astype(f32)
    pre_grad[rows_all : rows_all + 8] = jnp.zeros((8, GROUP), f32)

    def gains(c, carry):
        rows = chunk(c)
        low = lane_low()
        for p in range(pairs):
            lanes = slice(2 * HEAD * p, 2 * HEAD * (p + 1))
            wides = [slice(BLOCK * (2 * p + k), BLOCK * (2 * p + k + 1)) for k in range(2)]
            ends_p = [ends_w[rows, w] for w in wides]
            starts_p = [starts_w[rows, w] for w in wides]
            end = jnp.where(low, *ends_p)
            start = jnp.where(low, *starts_p)
            total = end[BLOCK - 1 : BLOCK]
            totals[c, :, lanes] = jnp.broadcast_to(total, (8, 2 * HEAD))
            dy = mixed_grad[rows, lanes].astype(f32)
            both = jnp.concatenate((jnp.exp2(end) * dy, jnp.exp2(total - start) * dy), axis=1)
            gain = dot(select_t[c, STATE:], both.astype(bf16))
            gain_e[c, :, lanes] = gain[:, : 2 * HEAD]
            gain_l[c, :, lanes] = gain[:, 2 * HEAD :]
        return carry

    each_chunk(chunks, gains, 0)

    state = jnp.zeros((STATE, GROUP), f32)
    for c in reversed(range(chunks)):
        early_grad[c] = state.astype(bf16)
        kept = jnp.exp2(totals[c, :1]) * state
        through[c] = jnp.broadcast_to(
            jnp.sum(kept * early[c].astype(f32), axis=0, keepdims=True), (8, GROUP)
        )
        state = kept + gain_e[c]
    state = jnp.zeros((STATE, GROUP), f32)
    for c in range(chunks):
        late_grad[c] = state.astype(bf16)
        kept = jnp.exp2(totals[c, :1]) * state
        through[c] += jnp.broadcast_to(
            jnp.sum(kept * late[c].astype(f32), axis=0, keepdims=True), (8, GROUP)
        )
        state = kept + gain_l[c]

    down = iota((BLOCK, BLOCK), 0)
    across = iota((BLOCK, BLOCK), 1)

    def mix(c, carry):
        rows = chunk(c)
        low = lane_low()
        coupled = gram_t[c]
        gram_sum = gram_grad[c]
        b_sum = b_grad[rows]
        c_sum = c_grad[rows]
        row_id = iota((8, BLOCK), 0)
        lane_id = iota((8, BLOCK), 1)
        flow = jnp.zeros((8, BLOCK), f32)
        apart = jnp.zeros((16, BLOCK), f32)
        columns_sum = jnp.zeros((BLOCK, BLOCK), f32)
        below_rows = []
        above_rows = []
        for p in range(pairs):
            lanes = slice(2 * HEAD * p, 2 * HEAD * (p + 1))
            wides = [slice(BLOCK * (2 * p + k), BLOCK * (2 * p + k + 1)) for k in range(2)]
            ends_p = [ends_w[rows, w] for w in wides]
            starts_p = [starts_w[rows, w] for w in wides]
            end = jnp.where(low, *ends_p)
            start = jnp.where(low, *starts_p)
            total = end[BLOCK - 1 : BLOCK]
            step = steps_w[rows, lanes]
            x = x_low[rows, lanes].astype(f32)
            dy = mixed_grad[rows, lanes].astype(f32)
            xs = x * step
            dy_rows = pair_rows(dy, low)
            powers = []
            coupling = []
            for k in range(2):
                end_row = ends_t[0, 2 * p + k : 2 * p + k + 1, rows]
                start_row = starts_t[0, 2 * p + k : 2 * p + k + 1, rows]
                power = jnp.exp2(jnp.minimum(end_row - ends_p[k], starts_p[k] - start_row))
                powers.append(power)
                coupling.append(coupled * power)
            inner = dot(jnp.concatenate(coupling, axis=1).astype(bf16), dy_rows)
            pair_products = dot_nt(xs.astype(bf16), dy_rows)
            for k in range(2):
                product = pair_products[:, BLOCK * k : BLOCK * (k + 1)]
                gram_sum = gram_sum + product * powers[k]
                spread_log = product * coupling[k]
                below = jnp.where(down < across, spread_log, 0.0)
                above = spread_log - below
                below_rows.append(jnp.sum(below, axis=0, keepdims=True))
                above_rows.append(jnp.sum(above, axis=0, keepdims=True))
                below_cols = jnp.sum(below, axis=1, keepdims=True)
                above_cols = jnp.sum(above, axis=1, keepdims=True)
                lane = 2 * p + k
                columns_sum = jnp.where(across == lane, below_cols, columns_sum)
                columns_sum = jnp.where(across == lane + 8, above_cols, columns_sum)
            states = jnp.concatenate((early[c, :, lanes], late[c, :, lanes]), axis=1)
            states_grad = jnp.concatenate((early_grad[c, :, lanes], late_grad[c, :, lanes]), axis=1)
            raw_y = dot(c_rows[rows], states)
            raw_x = dot(b_rows[rows], states_grad)
            dy_both = jnp.concatenate((jnp.exp2(end) * dy, jnp.exp2(total - start) * dy), axis=1)
            weight_both = jnp.concatenate((jnp.exp2(total - end), jnp.exp2(start)), axis=1)
            xs_both = jnp.concatenate((xs, xs), axis=1) * weight_both
            outer_both = weight_both * raw_x
            c_sum = c_sum + dot_nt(dy_both.astype(bf16), states)
            b_sum = b_sum + dot_nt(xs_both.astype(bf16), states_grad)
            grad_xs = inner + outer_both[:, : 2 * HEAD] + outer_both[:, 2 * HEAD :]
            from_y = dy_both * raw_y
            from_x = xs_both * raw_x
            local = from_y[:, 2 * HEAD :] - from_x[:, 2 * HEAD :]
            moving = from_y[:, : 2 * HEAD] - from_x[:, : 2 * HEAD] - local
            passed = from_x[:, : 2 * HEAD] + from_y[:, 2 * HEAD :]
            through[c, :, lanes] += jnp.broadcast_to(
                jnp.sum(passed, axis=0, keepdims=True), (8, 2 * HEAD)
            )
            pick = (row_id == 2 * p + lane_id // HEAD).astype(f32)
            none = jnp.zeros((8, BLOCK), f32)
            pick_same = jnp.concatenate((pick, pick), axis=1).astype(bf16)
            pick_apart = jnp.concatenate(
                (
                    jnp.concatenate((pick, none), axis=1),
                    jnp.concatenate((none, pick), axis=1),
                ),
                axis=0,
            ).astype(bf16)
            high = moving.astype(bf16)
            rest = (moving - high.astype(f32)).astype(bf16)
            flow = flow + dot_nt(pick_same, jnp.concatenate((high, rest), axis=1))
            apart = apart + dot_nt(
                pick_apart, jnp.concatenate((local, x * grad_xs), axis=1).astype(bf16)
            )
            pre_grad[rows, lanes] = step * grad_xs + shortcut[:, lanes] * dy
        gram_grad[c] = gram_sum
        b_grad[rows] = b_sum
        c_grad[rows] = c_sum
        tile = slice(c * 8, c * 8 + 8)
        flat = columns_sum.T
        pad = jnp.zeros((4, BLOCK), f32)
        below_all = jnp.concatenate(below_rows + [pad], axis=0)
        above_all = jnp.concatenate(above_rows + [pad], axis=0)
        below_flat = flat[0:8]
        above_flat = flat[8:16]
        sums[tile] = flow + (below_all - below_flat) - (above_all - above_flat)
        local_rows[tile] = apart[:8] + (above_all - above_flat)
        direct_grad[0, tile] = apart[8:]
        return carry

    each_chunk(chunks, mix, 0)

    head_cols = (iota((GROUP, BLOCK), 0) // HEAD == iota((GROUP, BLOCK), 1)).astype(f32)
    tall = 8 * chunks
    through_tall = dot_full(through[...].reshape(tall, GROUP), head_cols)
    own = iota((tall, BLOCK), 1) == iota((tall, BLOCK), 0) % 8
    through_rows = jnp.sum(jnp.where(own, through_tall, 0.0), axis=1, keepdims=True)
    decay_grad[0] = (
        dot_full(sums[...], (down >= across).astype(f32)) + local_rows[...] + through_rows
    )

    def conv_back(c, carry):
        rows = chunk(c)
        pre = conv_taps(padded, c, filters)
        sig = sigmoid(pre)
        inside = (c * BLOCK + iota((BLOCK, GROUP), 0)) < length[0]
        grad = jnp.where(inside, pre_grad[rows] * (sig * (1.0 + pre * (1.0 - sig))), 0.0)
        pre_grad[rows] = grad
        return tuple(
            carry[k]
            + jnp.sum(grad * padded[chunk(c, 5 + k)], axis=0, keepdims=True)
            for k in range(4)
        )

    zero = jnp.zeros((1, GROUP), f32)
    filter_sums = each_chunk(chunks, conv_back, (zero,) * 4)
    filters_grad[...] = jnp.concatenate(filter_sums, axis=0)

    def conv_shift(c, carry):
        rows = chunk(c)
        total = pre_grad[rows] * filters[3:4]
        for ahead in range(1, 4):
            total = total + pre_grad[chunk(c, ahead)] * filters[3 - ahead : 4 - ahead]
        values_grad[rows] = total.astype(bf16)
        return carry

    each_chunk(chunks, conv_shift, 0)
    grads = dot(normed_t[...], values_grad[...])
    content_grad[...] = grads.astype(bf16)
    add_products(row_sums, grads, content)

    if last:

        @pl.when(step_id == pl.num_programs(0) - 1)
        def _():
            def finish(c, carry):
                rows = chunk(c)
                grad = jnp.where(down != across, gram_grad[c], 0.0)
                b_grad[rows] += dot(grad.astype(bf16), c_rows[rows])
                c_grad[rows] += dot(grad.T.astype(bf16), b_rows[rows])
                return carry

            each_chunk(chunks, finish, 0)


def whole(shape):
    return pl.BlockSpec(shape, lambda *_: (0,) * len(shape), pipeline_mode=pl.Buffered(1))


def columns(rows, width=GROUP, after=0):
    return pl.BlockSpec((rows, width), lambda g, *_: (0, g + after))


def planes(shape):
    return pl.BlockSpec(shape, lambda g, *_: (0,) * (len(shape) - 1) + (g,))


def turned(after, rows):
    return pl.BlockSpec((1, 8, rows), lambda g, *_: (g + after, 0, 0))


def lead(shape):
    return pl.BlockSpec((1,) + shape, lambda g, *_: (g,) + (0,) * len(shape))


scalar = pl.BlockSpec(memory_space=pltpu.SMEM)


def shaped(shape, dtype):
    return jax.ShapeDtypeStruct(shape, dtype)


def params(limit=60):
    return pltpu.CompilerParams(vmem_limit_bytes=limit << 20)


def cost(micros):
    return pl.CostEstimate(flops=0, bytes_accessed=int(micros * 3.0e6), transcendentals=0)


def prepare(rank, normed, first_own, first_other, kernels, biases, rates, heads):
    rows, width = normed.shape
    chunks = rows // BLOCK
    groups = 2 * heads // SLOTS
    extra = whole((width, BLOCK))
    shapes = (
        shaped((rows, BLOCK), f32),
        shaped((rows, STATE), bf16),
        shaped((rows, STATE), bf16),
        shaped((chunks, BLOCK, BLOCK), bf16),
        shaped((chunks, BLOCK, BLOCK), f32),
        shaped((chunks, BLOCK, BLOCK), f32),
        shaped((rows, BLOCK), f32),
        shaped((rows, BLOCK), f32),
        shaped((rows, BLOCK), f32),
        shaped((groups, 8, rows), f32),
        shaped((groups, 8, rows), f32),
        shaped((groups, 8, rows), f32),
        shaped((groups, 8, rows), f32),
    )
    return pl.pallas_call(
        functools.partial(prep_kernel, heads),
        grid=(1,),
        in_specs=[
            scalar, whole(normed.shape), extra, extra,
            whole(kernels.shape), whole(biases.shape), whole(rates.shape),
        ],
        out_specs=tuple(whole(o.shape) for o in shapes),
        out_shape=shapes,
        scratch_shapes=[pltpu.VMEM((rows + 8, BLOCK), f32), pltpu.VMEM((rows, BLOCK), f32)],
        compiler_params=params(LIM_prep),
        cost_estimate=cost(4),
        name="prep",
    )(rank, normed, first_own, first_other, kernels, biases, rates)


def front_kernel(tokens, rescale, normed, normed_t, inverse_out):
    width = tokens.shape[1]

    def body(c, carry):
        rows = chunk(c)
        tok = tokens[rows].astype(f32)
        inverse = lax.rsqrt(jnp.sum(tok * tok, axis=1, keepdims=True) / width + epsilon)
        scaled = tok * inverse * rescale[...]
        normed[rows] = scaled.astype(bf16)
        inverse_out[rows] = jnp.broadcast_to(inverse, (BLOCK, BLOCK))
        for k in range(width // BLOCK):
            normed_t[chunk(k), rows] = scaled[:, chunk(k)].T.astype(bf16)
        return carry

    each_chunk(tokens.shape[0] // BLOCK, body, 0)


def front(tokens, rescale):
    rows, width = tokens.shape
    vmem = pl.BlockSpec(memory_space=pltpu.VMEM)
    return pl.pallas_call(
        front_kernel,
        in_specs=[vmem, vmem],
        out_specs=(vmem, vmem, vmem),
        out_shape=(
            shaped((rows, width), bf16), shaped((width, rows), bf16), shaped((rows, BLOCK), f32)
        ),
        compiler_params=params(LIM_front),
        cost_estimate=cost(5),
        name="front",
    )(tokens, rescale.reshape(1, width))


def mask_kernel(length, cotangent, masked, masked_t):
    width = cotangent.shape[1]

    def body(c, carry):
        rows = chunk(c)
        inside = (c * BLOCK + iota((BLOCK, width), 0)) < length[0]
        kept = jnp.where(inside, cotangent[rows].astype(f32), 0.0)
        masked[rows] = kept.astype(bf16)
        for k in range(width // BLOCK):
            masked_t[chunk(k), rows] = kept[:, chunk(k)].T.astype(bf16)
        return carry

    each_chunk(cotangent.shape[0] // BLOCK, body, 0)


def mask_rows(length, cotangent):
    rows, width = cotangent.shape
    vmem = pl.BlockSpec(memory_space=pltpu.VMEM)
    return pl.pallas_call(
        mask_kernel,
        in_specs=[scalar, vmem],
        out_specs=(vmem, vmem),
        out_shape=(shaped((rows, width), bf16), shaped((width, rows), bf16)),
        compiler_params=params(LIM_mask_rows),
        cost_estimate=cost(5),
        name="mask_rows",
    )(length, cotangent)


def finish_kernel(
    rank, normed_t, weights_own, weights_other, select_in, b_grad, c_grad, kernels, rates,
    decay_own, decay_other, direct_own, direct_other, slope_t, steps_t, sums_0, sums_1, sums_2,
    grad_own, grad_other, extra_own, extra_other, kernels_grad, biases_grad, decays_grad, row_sums,
    padded, grad_s,
):
    rows = select_in.shape[0]
    chunks = rows // BLOCK
    half = decay_own.shape[0]
    padded[0:8] = jnp.zeros((8, BLOCK), f32)
    padded[8:] = select_in[...]
    grad_s[rows : rows + 8] = jnp.zeros((8, BLOCK), f32)

    def back(c, carry):
        here = chunk(c)
        pre = conv_taps(padded, c, kernels)
        sig = sigmoid(pre)
        grad = jnp.concatenate((b_grad[here], c_grad[here]), axis=1)
        grad = grad * (sig * (1.0 + pre * (1.0 - sig)))
        grad_s[here] = grad
        return tuple(
            carry[k] + jnp.sum(grad * padded[chunk(c, 5 + k)], axis=0, keepdims=True)
            for k in range(4)
        )

    zero = jnp.zeros((1, BLOCK), f32)
    kernels_grad[...] = jnp.concatenate(each_chunk(chunks, back, (zero,) * 4), axis=0)
    lane = iota((BLOCK, BLOCK), 1)
    used = SLOTS * half

    def turn(c, carry):
        here = chunk(c)
        total = grad_s[here] * kernels[3:4]
        for ahead in range(1, 4):
            total = total + grad_s[chunk(c, ahead)] * kernels[3 - ahead : 4 - ahead]
        tile = slice(SLOTS * c, SLOTS * (c + 1))
        tiles = []
        sums = []
        valid = iota((SLOTS, BLOCK), 0) < GROUP // HEAD
        for g in range(2 * half):
            decay = decay_own if g < half else decay_other
            direct = direct_own if g < half else direct_other
            fall = jnp.where(valid, decay[g % half, tile], 0.0)
            slope = jnp.where(valid, slope_t[g, :, here], 0.0)
            step = (direct[g % half, tile] - rates[g] * fall) * slope
            tiles.append(step)
            sums.append((step, rates[g] * steps_t[g, :, here] * fall))
        blank = jnp.zeros((BLOCK - 2 * used, BLOCK), f32)
        steps = jnp.concatenate(tiles + [blank], axis=0).T
        turned = pltpu.roll(total, STATE, 1)
        first = jnp.where(rank[0] == 0, total, turned)
        second = jnp.where(rank[0] == 0, turned, total)
        keep = lane < STATE + used
        grad_own[here] = jnp.where(
            lane < STATE, first, jnp.where(keep, pltpu.roll(steps, STATE, 1), 0.0)
        ).astype(bf16)
        grad_other[here] = jnp.where(
            lane < STATE, second, jnp.where(keep, pltpu.roll(steps, STATE - used, 1), 0.0)
        ).astype(bf16)
        return [(a + x, b - y) for (a, b), (x, y) in zip(carry, sums)]

    empty = jnp.zeros((SLOTS, BLOCK), f32)
    sums = each_chunk(chunks, turn, [(empty, empty)] * (2 * half))
    for g in range(2 * half):
        biases_grad[g] = sums[g][0]
        decays_grad[g] = sums[g][1]
    own = dot(normed_t[...], grad_own[...])
    other = dot(normed_t[...], grad_other[...])
    extra_own[...] = own
    extra_other[...] = other.astype(bf16)
    row_sums[...] = (
        own * weights_own[...].astype(f32)
        + other * weights_other[...].astype(f32)
        + (sums_0[...] + sums_1[...] + sums_2[...])
    )


def finish(rank, normed_t, narrows, prep, b_grad, c_grad, kernels, rate_tiles, deep, row_sums):
    width, rows = normed_t.shape
    groups = prep[11].shape[0]
    shapes = (
        shaped((rows, BLOCK), bf16),
        shaped((rows, BLOCK), bf16),
        shaped((width, BLOCK), f32),
        shaped((width, BLOCK), bf16),
        shaped(kernels.shape, f32),
        shaped((groups, SLOTS, BLOCK), f32),
        shaped((groups, SLOTS, BLOCK), f32),
        shaped((width, BLOCK), f32),
    )
    rest = (
        prep[0], b_grad, c_grad, kernels, rate_tiles, deep[0][3], deep[1][3], deep[0][4], deep[1][4],
        prep[12], prep[11], *row_sums,
    )
    return pl.pallas_call(
        finish_kernel,
        grid=(1,),
        in_specs=[scalar, whole(normed_t.shape)]
        + [whole(w.shape) for w in narrows]
        + [whole(r.shape) for r in rest],
        out_specs=tuple(whole(o.shape) for o in shapes),
        out_shape=shapes,
        scratch_shapes=[pltpu.VMEM((rows + 8, BLOCK), f32), pltpu.VMEM((rows + 8, BLOCK), f32)],
        compiler_params=params(LIM_finish),
        cost_estimate=cost(6),
        name="finish",
    )(rank, normed_t, *narrows, *rest)


def back_kernel(
    values_own, values_other, gate_own, gate_other, content_own, content_other, gating_own,
    gating_other, extra_own, extra_other, weights_own, weights_other, tokens, inverse_in, rescale,
    cotangent, grad_out, total,
):
    step = pl.program_id(0)

    def products():
        return (
            dot_nt(values_own[...], content_own[...])
            + dot_nt(values_other[...], content_other[...])
            + dot_nt(gate_own[...], gating_own[...])
            + dot_nt(gate_other[...], gating_other[...])
        )

    @pl.when(step == 0)
    def _():
        total[...] = (
            products()
            + dot_nt(extra_own[...], weights_own[...])
            + dot_nt(extra_other[...], weights_other[...])
        )

    @pl.when(step > 0)
    def _():
        total[...] += products()

    @pl.when(step == pl.num_programs(0) - 1)
    def _():
        width = tokens.shape[1]

        def body(c, carry):
            rows = chunk(c)
            inverse = inverse_in[rows, :1]
            unit = tokens[rows].astype(f32) * inverse
            weighted = total[rows] * rescale[...]
            mean = jnp.sum(weighted * unit, axis=1, keepdims=True) / width
            grad = cotangent[rows].astype(f32) + inverse * (weighted - unit * mean)
            grad_out[rows] = grad.astype(bf16)
            return carry

        each_chunk(tokens.shape[0] // BLOCK, body, 0)


def backward_rows(deep, back, firsts, narrows, seconds, extras, tokens, inverse_wide, rescale, cotangent):
    rows, width = tokens.shape
    inner = deep[0][0].shape[1]
    fixed = (tokens, inverse_wide, rescale.reshape(1, width), cotangent)
    return pl.pallas_call(
        back_kernel,
        grid=(inner // GROUP,),
        in_specs=[columns(rows)] * 4
        + [columns(width)] * 4
        + [whole((rows, BLOCK))] * 2
        + [whole(w.shape) for w in narrows]
        + [whole(f.shape) for f in fixed],
        out_specs=whole((rows, width)),
        out_shape=shaped((rows, width), bf16),
        scratch_shapes=[pltpu.VMEM((rows, width), f32)],
        compiler_params=params(LIM_back),
        cost_estimate=cost(14),
        name="back",
    )(
        deep[0][0], deep[1][0], back[0][1], back[1][1], *firsts, *seconds, *extras, *narrows, *fixed
    )


def mix_forward(half, length, normed, content, filters, shortcut, prep, inner):
    (_, _, c_rows, select_t, gram, _, ends, starts, steps, ends_t, starts_t, _, _) = prep
    rows, width = normed.shape
    chunks = rows // BLOCK
    grid = inner // GROUP
    wide = GROUP // HEAD * BLOCK
    return pl.pallas_call(
        functools.partial(mix_kernel, half),
        grid=(grid,),
        in_specs=[
            scalar, whole(normed.shape), columns(width), columns(4), columns(1),
            whole(c_rows.shape), whole(select_t.shape), whole(gram.shape),
            whole(ends.shape), whole(starts.shape), whole(steps.shape),
            turned(half * grid, rows), turned(half * grid, rows),
        ],
        out_specs=(
            columns(rows), columns(rows), columns(rows),
            planes((chunks, STATE, GROUP)), planes((chunks, STATE, GROUP)),
            columns(rows, wide), columns(rows, wide), columns(rows),
        ),
        out_shape=(
            shaped((rows, inner), bf16),
            shaped((rows, inner), bf16),
            shaped((rows, inner), bf16),
            shaped((chunks, STATE, inner), bf16),
            shaped((chunks, STATE, inner), bf16),
            shaped((rows, grid * wide), f32),
            shaped((rows, grid * wide), f32),
            shaped((rows, inner), f32),
        ),
        scratch_shapes=[
            pltpu.VMEM((rows + 8, GROUP), f32),
            pltpu.VMEM((rows, GROUP), f32),
            pltpu.VMEM((chunks, STATE, GROUP), f32),
            pltpu.VMEM((chunks, STATE, GROUP), f32),
            pltpu.VMEM((chunks, 8, GROUP), f32),
        ],
        compiler_params=params(LIM_mix),
        cost_estimate=cost(14),
        name="mix",
    )(length, normed, content, filters, shortcut, c_rows, select_t, gram, ends, starts, steps, ends_t, starts_t)


def gate_both(length, normed, normed_t, tokens, cotangent, cotangent_t, seconds, amplitude, kept, inner_width):
    rows, width = normed.shape
    inner = kept[0][0].shape[1]
    half = inner // GROUP
    groups = 2 * half

    def read(h):
        def at(g):
            k = g % groups
            return jnp.minimum(k, half - 1) if h == 0 else jnp.maximum(k - half, 0)

        return at

    def write(h):
        return lambda g: jnp.clip(g - groups - h * half, 0, half - 1)

    def blocks(height, at, after=0):
        return pl.BlockSpec((height, GROUP), lambda g: (0, at(g) + after))

    fixed = (normed, normed_t, tokens, cotangent, cotangent_t)
    ins = [length, *fixed, *seconds, *seconds, amplitude]
    ins += [kept[0][0], kept[1][0], kept[0][1], kept[1][1]]
    specs = [scalar] + [whole(f.shape) for f in fixed]
    specs += [blocks(width, read(h)) for h in range(2)]
    specs += [blocks(width, read(h), half) for h in range(2)]
    specs += [pl.BlockSpec((1, GROUP), lambda g: (0, g % groups))]
    specs += [blocks(rows, read(h)) for h in range(2)] * 2
    heights = (rows, rows, width, width, 1, 1)
    kinds = (bf16, bf16, bf16, bf16, f32, f32)
    outs = [shaped((n, inner), k) for n, k in zip(heights, kinds) for _ in range(2)]
    out_specs = [blocks(n, write(h)) for n in heights for h in range(2)]
    outs += [shaped((rows, width), bf16), shaped((width, BLOCK), f32)]
    out_specs += [whole((rows, width)), whole((width, BLOCK))]
    got = pl.pallas_call(
        functools.partial(gate_kernel, inner_width),
        grid=(2 * groups,),
        in_specs=specs,
        out_specs=tuple(out_specs),
        out_shape=tuple(outs),
        scratch_shapes=[
            pltpu.VMEM((rows, BLOCK), f32),
            pltpu.VMEM((rows, width), f32),
            pltpu.VMEM((groups, rows, GROUP), f32),
            pltpu.VMEM((rows, BLOCK), f32),
            pltpu.VMEM((rows, BLOCK), f32),
            pltpu.VMEM((rows, GROUP), bf16),
            pltpu.VMEM((rows, GROUP), f32),
            pltpu.VMEM((rows, GROUP), bf16),
            pltpu.VMEM((rows, GROUP), bf16),
        ],
        compiler_params=params(LIM_gate),
        cost_estimate=cost(35),
        name="gate",
    )(*ins)
    return [got[h:12:2] for h in range(2)], got[12], got[13]


def mix_backward(half, length, normed_t, weights, filters, shortcut, prep, mixed_grad, kept, carried, last):
    (_, b_rows, c_rows, select_t, _, gram_t, _, _, _, ends_t, starts_t, _, _) = prep
    _, x_low, values, early, late, *wides = kept
    width, rows = normed_t.shape
    inner = x_low.shape[1]
    chunks = rows // BLOCK
    grid = inner // GROUP
    first = carried is None
    wide = GROUP // HEAD * BLOCK
    shared = (b_rows, c_rows, select_t, gram_t, ends_t, starts_t)
    ins = [length, normed_t, weights, filters, shortcut, *shared]
    ins += [mixed_grad, x_low, values, early, late, *wides]
    specs = [scalar, whole(normed_t.shape), columns(width), columns(4), columns(1)]
    specs += [whole(s.shape) for s in shared[:-2]] + [turned(half * grid, rows)] * 2
    specs += [columns(rows)] * 3 + [planes((chunks, STATE, GROUP))] * 2
    specs += [columns(rows, wide), columns(rows, wide), columns(rows)]
    if not first:
        ins += list(carried)
        specs += [whole(c.shape) for c in carried]
    tall = 8 * chunks
    return pl.pallas_call(
        functools.partial(mix_back_kernel, half, first, last),
        grid=(grid,),
        in_specs=specs,
        out_specs=(
            columns(rows), columns(width), columns(4), lead((tall, BLOCK)), lead((tall, BLOCK)),
            whole((chunks, BLOCK, BLOCK)), whole((rows, STATE)), whole((rows, STATE)),
            whole((width, BLOCK)),
        ),
        out_shape=(
            shaped((rows, inner), bf16),
            shaped((width, inner), bf16),
            shaped((4, inner), f32),
            shaped((grid, tall, BLOCK), f32),
            shaped((grid, tall, BLOCK), f32),
            shaped((chunks, BLOCK, BLOCK), f32),
            shaped((rows, STATE), f32),
            shaped((rows, STATE), f32),
            shaped((width, BLOCK), f32),
        ),
        scratch_shapes=[
            pltpu.VMEM((rows + 8, GROUP), f32),
            pltpu.VMEM((rows + 8, GROUP), f32),
            pltpu.VMEM((chunks, STATE, GROUP), f32),
            pltpu.VMEM((chunks, STATE, GROUP), f32),
            pltpu.VMEM((chunks, 8, GROUP), f32),
            pltpu.VMEM((chunks, STATE, GROUP), bf16),
            pltpu.VMEM((chunks, STATE, GROUP), bf16),
            pltpu.VMEM((tall, BLOCK), f32),
            pltpu.VMEM((tall, BLOCK), f32),
            pltpu.VMEM((chunks, 8, GROUP), f32),
        ],
        compiler_params=params(LIM_mix_back),
        cost_estimate=cost(28),
        name="mix_back",
    )(*ins)


def shift_down(v, by):
    return jnp.pad(v, ((by, 0), (0, 0)))[: v.shape[0]]


def shift_up(v, by):
    return jnp.pad(v, ((0, by), (0, 0)))[by:]


def select_back(select_in, grad, kernels):
    taps = kernels.shape[0]
    shifted = [shift_down(select_in, taps - 1 - k) for k in range(taps)]
    pre = sum(shifted[k] * kernels[k] for k in range(taps))
    sig = sigmoid(pre)
    grad_pre = grad * (sig * (1.0 + pre * (1.0 - sig)))
    kernels_grad = jnp.stack([jnp.sum(grad_pre * shifted[k], axis=0) for k in range(taps)])
    select_grad = sum(shift_up(grad_pre, taps - 1 - k) * kernels[k] for k in range(taps))
    return select_grad, kernels_grad


def heads_to_rows(tall):
    grid, rows, tokens = tall.shape
    shaped_up = tall.reshape(grid, rows // 8, 8, tokens)[:, :, :4]
    return shaped_up.transpose(0, 2, 1, 3).reshape(grid * 4, (rows // 8) * tokens)


def place_kernel(count, places, *refs):
    parts, wide, narrow = refs[:PLANE], refs[PLANE], refs[PLANE + 1]
    cut = wide.shape[2]
    for k in range(PLANE):
        for s in range(count):
            slot = places[k * count + s]
            wide[slot] = parts[k][s, :, :cut]
            narrow[slot] = parts[k][s, :, cut:]


PLANE = 4
DP = ("column", "plane")


def pairs_by(size, by):
    return [(i, i ^ by) for i in range(size)]


def gather_column(local):
    count = lax.axis_size("column")
    others = [lax.ppermute(local, "column", pairs_by(count, s)) for s in range(1, count)]
    return jnp.stack([local] + others)


def gather_plane(column):
    return [column] + [
        lax.ppermute(column, "plane", pairs_by(PLANE, k)) for k in range(1, PLANE)
    ]


def place(parts):
    count, block, width = parts[0].shape
    high, low = lax.axis_index("column"), lax.axis_index("plane")
    places = jnp.stack([(high ^ s) * PLANE + (low ^ k) for k in range(PLANE) for s in range(count)])
    vmem = pl.BlockSpec(memory_space=pltpu.VMEM)
    placed = pl.pallas_call(
        functools.partial(place_kernel, count),
        in_specs=[scalar] + [vmem] * PLANE,
        out_specs=(vmem, vmem),
        out_shape=[shaped((PLANE * count, block, w), bf16) for w in (width - BLOCK, BLOCK)],
        compiler_params=params(LIM_place),
        cost_estimate=cost(2),
        name="place",
    )(places.astype(jnp.int32), *parts)
    return [p.reshape(PLANE * count * block, p.shape[2]) for p in placed]


def block_of(blocks, index, axis):
    return lax.dynamic_index_in_dim(blocks, index, axis, keepdims=False)


def plane_send(v, by):
    return lax.ppermute(v, "plane", pairs_by(PLANE, by))


def start_sum(total):
    count = lax.axis_size("column")
    low = lax.axis_index("plane")
    rows, width = total.shape
    blocks = total.reshape(count, PLANE, rows // (count * PLANE), width)
    half = width // 2
    parts = (blocks[..., :half], blocks[..., half:])
    sent = []
    for part, near, far in ((parts[0], 1, 2), (parts[1], 2, 1)):
        away = jnp.stack((block_of(part, low ^ near, 1), block_of(part, low ^ 3, 1)))
        keep = jnp.stack((block_of(part, low, 1), block_of(part, low ^ far, 1)))
        sent.append((keep, plane_send(away, near)))
    return sent


def middle_sum(sent):
    moved = []
    for (keep, got), by in zip(sent, (2, 1)):
        both = (keep.astype(f32) + got.astype(f32)).astype(bf16)
        moved.append((both[0], plane_send(both[1], by)))
    return moved


def last_sum(moved):
    count = lax.axis_size("column")
    high = lax.axis_index("column")
    column = jnp.concatenate(
        [(keep.astype(f32) + got.astype(f32)).astype(bf16) for keep, got in moved], axis=-1
    )
    terms = [block_of(column, high, 0)] + [
        lax.ppermute(block_of(column, high ^ s, 0), "column", pairs_by(count, s))
        for s in range(1, count)
    ]
    return column, terms


def finish_sum(terms):
    return tree_sum([t.astype(f32) for t in terms])


def tree_sum(terms):
    while len(terms) > 1:
        terms = [terms[k] + terms[k + 1] for k in range(0, len(terms), 2)]
    return terms[0]


def exchange(total):
    return lax.all_to_all(total, DP, 0, 0, tiled=True)


def sum_blocks(received, blocks):
    cut = received.reshape(blocks, received.shape[0] // blocks, received.shape[1])
    return jnp.sum(cut.astype(f32), axis=0)


def swap(v):
    return lax.ppermute(v, "tensor", [(0, 1), (1, 0)])


def pad_columns(v, width):
    return jnp.pad(v, ((0, 0), (0, width - v.shape[1])))


def tie(value, *others):
    return lax.optimization_barrier((value, *others))[0]


def on_device(
    layer_in,
    upstream,
    lengths,
    rescale,
    gating,
    content,
    selector,
    timestep,
    filters,
    kernels,
    biases,
    decays,
    shortcut,
    amplitude,
    outgoing,
):
    parts = lax.axis_size("tensor")
    rank = lax.axis_index("tensor")
    micro = lengths.shape[0]
    half_rows = layer_in.shape[0] // micro
    rows = half_rows * parts
    width = layer_in.shape[1]
    inner = gating.shape[1]
    heads = timestep.shape[1]
    state_cols = selector.shape[1]
    inner_width = inner * parts

    state_half = state_cols // parts
    own_select = lax.dynamic_slice_in_dim(selector, rank * state_half, state_half, 1)
    spaced = heads // (GROUP // HEAD) * SLOTS
    step_local = jnp.pad(
        timestep.reshape(-1, spaced // SLOTS, GROUP // HEAD),
        ((0, 0), (0, 0), (0, SLOTS - GROUP // HEAD)),
    ).reshape(-1, spaced)
    first_local = jnp.concatenate(
        (content, pad_columns(jnp.concatenate((own_select, step_local), axis=1), BLOCK)), axis=1
    )
    second_local = jnp.concatenate((gating, outgoing.T), axis=1)
    first_column = gather_column(first_local)
    second_own = lax.all_gather(second_local, DP, axis=0, tiled=True)

    def across(array):
        blocks = array.reshape(micro, half_rows, width)
        return lax.all_to_all(blocks, "tensor", 0, 0, tiled=True).reshape(rows, width)

    def outputs_of(array):
        mine = lax.dynamic_slice_in_dim(array, rank * half_rows, half_rows, 0)
        theirs = lax.dynamic_slice_in_dim(array, (1 - rank) * half_rows, half_rows, 0)
        return mine, swap(theirs)

    def join(mine, got):
        return jnp.where(
            rank == 0, jnp.concatenate((mine, got)), jnp.concatenate((got, mine))
        )

    tokens = across(layer_in)
    cotangent = across(upstream)
    length = lax.dynamic_slice_in_dim(lengths, rank, 1, 0)
    rank_1 = rank.reshape(1)

    flat = jnp.concatenate((filters.reshape(-1), amplitude, biases, decays, shortcut))
    flat_other = swap(flat)
    taps = filters.shape[0]

    def unpack(vector):
        edges = [0, taps * inner, (taps + 1) * inner]
        edges += [edges[-1] + heads * k for k in range(1, 4)]
        cut = [vector[a:b] for a, b in zip(edges[:-1], edges[1:])]
        return (cut[0].reshape(taps, inner), cut[1].reshape(1, inner), *cut[2:])

    filters_2, amplitude_2, biases_2, decays_2, shortcut_2 = zip(unpack(flat), unpack(flat_other))

    per = GROUP // HEAD

    def head_lanes(pair):
        cut = jnp.concatenate(pair).reshape(-1, per)
        return pad_columns(jnp.pad(cut, ((0, 0), (0, SLOTS - per))).reshape(1, -1), BLOCK)

    rates = jnp.exp(jnp.concatenate(decays_2))
    rate_lanes = head_lanes((rates,))
    shortcut_lanes = [jnp.repeat(s, HEAD).reshape(1, inner) for s in shortcut_2]
    first_column, tokens = lax.optimization_barrier((first_column, tokens))
    normed, normed_t, inverse_wide = front(tokens, rescale)
    dbranch, dbranch_t = mask_rows(length, cotangent)
    first_parts = gather_plane(first_column)
    first_parts[0] = tie(first_parts[0], dbranch, normed)
    first_own, narrow_own = place(first_parts)
    narrow_other = swap(narrow_own)
    first_other = swap(first_own)
    firsts = (first_own, first_other)
    narrows = (narrow_own, narrow_other)
    prep = prepare(
        rank_1, normed, *narrows, kernels, head_lanes(biases_2), rate_lanes, spaced
    )
    kept = [None, None]
    kept[0] = mix_forward(
        0, length, normed, first_own, filters_2[0], shortcut_lanes[0], prep, inner
    )
    second_own = tie(second_own, kept[0][0])
    second_other = swap(second_own)
    seconds = (second_own, second_other)
    kept[1] = mix_forward(
        1, length, normed, tie(first_other, second_own), filters_2[1], shortcut_lanes[1], prep, inner
    )
    back, layer_seq, gate_sums = gate_both(
        length, normed, normed_t, tokens, dbranch, dbranch_t, seconds,
        jnp.concatenate(amplitude_2, axis=1), kept, inner_width,
    )
    layer_pair = outputs_of(layer_seq)
    second_grads = jnp.concatenate(
        [(back[0][k].astype(f32) + swap(back[1][k]).astype(f32)).astype(bf16) for k in (2, 3)],
        axis=1,
    )
    second_grads, later_grad = lax.optimization_barrier((second_grads, back[1][0]))
    second_sent = start_sum(second_grads)

    deep = [None, None]
    deep[1] = mix_backward(
        1, length, normed_t, firsts[1], filters_2[1], shortcut_lanes[1], prep, later_grad, kept[1], None, False
    )
    content_swapped = swap(deep[1][1])
    early_grad, *landed = lax.optimization_barrier((back[0][0], *[got for _, got in second_sent]))
    second_sent = [(keep, got) for (keep, _), got in zip(second_sent, landed)]
    second_sent[0] = (second_sent[0][0], tie(second_sent[0][1], deep[1][1]))
    second_moved = middle_sum(second_sent)
    deep[0] = mix_backward(
        0, length, normed_t, firsts[0], filters_2[0], shortcut_lanes[0], prep, early_grad, kept[0],
        deep[1][5:8], True,
    )
    content_own, *landed = lax.optimization_barrier((deep[0][1], *[got for _, got in second_moved]))
    second_moved = [(keep, got) for (keep, _), got in zip(second_moved, landed)]
    _, second_terms = last_sum(second_moved)

    content_grads = (content_own.astype(f32) + content_swapped.astype(f32)).astype(bf16)
    rate_tiles = jnp.broadcast_to(
        jnp.pad(rates.reshape(-1, per), ((0, 0), (0, SLOTS - per)))[:, :, None],
        (2 * heads // per, SLOTS, BLOCK),
    )
    row_sums = (deep[0][8], deep[1][8], gate_sums)
    (
        grad_own, grad_other, extra_own, extra_other, kernels_part, biases_tile, decays_tile, rows_sum
    ) = finish(
        rank_1, normed_t, narrows, prep, deep[0][6], deep[0][7], kernels, rate_tiles, deep, row_sums
    )

    content_grads, rows_sum = lax.optimization_barrier((content_grads, rows_sum))
    first_sent = start_sum(content_grads)

    def compact(tiles):
        return jnp.sum(tiles[:, :per], axis=2).reshape(2 * heads)

    biases_part, decays_part = compact(biases_tile), compact(decays_tile)
    extra_sum = (extra_own + swap(extra_other).astype(f32)).astype(bf16)
    rescale_part = jnp.sum(rows_sum, axis=1) / rescale
    def per_head(row):
        return jnp.sum(row.reshape(heads, HEAD), axis=1)

    small_own, small_other = (
        jnp.concatenate(
            (
                deep[h][2].reshape(-1),
                back[h][4].reshape(-1),
                biases_part[h * heads : (h + 1) * heads],
                decays_part[h * heads : (h + 1) * heads],
                per_head(back[h][5]),
                rescale_part,
                kernels_part.reshape(-1),
            )
        )
        for h in range(2)
    )
    small = small_own + swap(small_other)
    used = small.shape[0]
    lines = -(-used // (16 * BLOCK)) * 16
    small = jnp.pad(small, (0, lines * BLOCK - used)).reshape(1, lines, BLOCK)
    small_high = small.astype(bf16)
    small_low = (small - small_high.astype(f32)).astype(bf16)
    blocks = lax.axis_size(DP)
    own_rows = width // blocks
    both = jnp.concatenate((small_high, small_low), axis=1)
    sent = jnp.concatenate(
        (
            extra_sum.reshape(blocks, own_rows, BLOCK),
            jnp.broadcast_to(both, (blocks, 2 * lines, BLOCK)),
        ),
        axis=1,
    )
    sent, *landed = lax.optimization_barrier((sent, *[got for _, got in first_sent]))
    first_sent = [(keep, got) for (keep, _), got in zip(first_sent, landed)]
    first_moved = middle_sum(first_sent)
    grad_own, *held = lax.optimization_barrier((grad_own, *[keep for keep, _ in first_moved]))
    first_moved = [(keep, got) for keep, (_, got) in zip(held, first_moved)]
    grad_seq = backward_rows(
        deep, back, firsts, narrows, seconds, (grad_own, grad_other), tokens, inverse_wide, rescale,
        dbranch,
    )
    grad_seq, *landed = lax.optimization_barrier((grad_seq, *[got for _, got in first_moved]))
    first_moved = [(keep, got) for (keep, _), got in zip(first_moved, landed)]
    column, first_terms = last_sum(first_moved)
    *layer_pair, column = lax.optimization_barrier((*layer_pair, column))
    input_grad = join(*outputs_of(grad_seq))
    layer_out = join(*layer_pair)

    got = lax.all_to_all(sent, DP, 0, 0, tiled=True)
    gathered = jnp.sum(got.astype(f32), axis=0)
    extra_total = gathered[:own_rows]
    summed = (gathered[own_rows : own_rows + lines] + gathered[own_rows + lines :]).reshape(-1)
    cut = (taps + 1) * inner + 3 * heads
    filters_grad, amplitude_grad, biases_grad, decays_grad, shortcut_grad = unpack(summed[:cut])
    second_total = finish_sum(second_terms)
    first_total = finish_sum(first_terms)
    state_own = extra_total[:, :state_half]
    state_other = swap(state_own)
    selector_grad = jnp.where(
        rank == 0,
        jnp.concatenate((state_own, state_other), axis=1),
        jnp.concatenate((state_other, state_own), axis=1),
    )
    return (
        layer_out,
        input_grad,
        summed[cut : cut + width],
        second_total[:, :inner],
        first_total,
        selector_grad,
        extra_total[:, state_half : state_half + spaced]
        .reshape(-1, spaced // SLOTS, SLOTS)[:, :, :per]
        .reshape(-1, heads),
        filters_grad,
        summed[cut + width : used].reshape(taps, state_cols),
        biases_grad,
        decays_grad,
        shortcut_grad,
        amplitude_grad.reshape(inner),
        second_total[:, inner:].T,
    )


def solution(mesh):
    devices = mesh.devices
    split = Mesh(
        devices.reshape(devices.shape[0] // PLANE, PLANE, devices.shape[1]), (*DP, "tensor")
    )
    return jax.shard_map(
        on_device,
        mesh=split,
        in_specs=(
            P((*DP, "tensor"), None),
            P((*DP, "tensor"), None),
            P(DP),
            P(),
            P(DP, "tensor"),
            P(DP, "tensor"),
            P(DP, None),
            P(DP, "tensor"),
            P(None, "tensor"),
            P(),
            P("tensor"),
            P("tensor"),
            P("tensor"),
            P("tensor"),
            P("tensor", DP),
        ),
        out_specs=(
            P((*DP, "tensor"), None),
            P((*DP, "tensor"), None),
            P(),
            P(DP, "tensor"),
            P(DP, "tensor"),
            P(DP, None),
            P(DP, "tensor"),
            P(None, "tensor"),
            P(),
            P("tensor"),
            P("tensor"),
            P("tensor"),
            P("tensor"),
            P("tensor", DP),
        ),
        check_vma=False,
    )
```
